128 devices in a mesh: wave: 8 (over x, core), band: 16 (over y, z).
Axes of the slice: x: 4, y: 4, z: 4, core: 2. Of those that a mesh axis runs over, the one named last changes fastest.
Arguments:
- control: float32 [256, 224, 192], P('band', 'wave'), may hold values from -6 to 6
- spectral_scale: float32 [256, 224, 192], P('band', 'wave'), may hold values from 0.3 to 3
- vertical_root: float32 [96, 96], replicated, may hold values from -0.625 to 0.625
- legendre: float32 [224, 448, 256], P('wave'), may hold values from -0.375 to 0.375
- zonal_number: int32 [224], replicated, may hold values from 0 to 223, each once
- courant: float32 [448, 96, 1024], P('band', None, 'wave'), may hold values from 0.05 to 0.9
- lidar_coef: float32 [12], replicated, may hold values from 0.2 to 1
- aod_coef: float32 [96], replicated, may hold values from 0.02 to 0.2
- obs_count: int32 [128, 128], P(('wave', 'band')), may hold values from 0 to 128, as said below
- obs_column: int32 [16384, 128], P(('wave', 'band')), may hold values from 0 to 3583
- obs_level: int32 [16384, 128], P(('wave', 'band')), may hold values from 0 to 7
- lidar_obs: float32 [16384, 128], P(('wave', 'band')), may hold values from -6 to 6
- aod_obs: float32 [16384, 128], P(('wave', 'band')), may hold values from -6 to 6
- obs_weight: float32 [16384, 128], P(('wave', 'band')), may hold values from 0.5 to 2
Outputs:
- gradient: float32 [256, 224, 192], P('band', 'wave')
- state_increment: float32 [448, 96, 1024], P('band', None, 'wave')
The draws below stay inside these ranges and needn't reach their ends.
Inputs may be any that keep to these rules, and one draw needn't show every extreme that they name: `obs_count`: live slots from a device to an owner; in every draw one owner receives 128 from every device. `zonal_number`: each number of 0 to 223 once.
All inputs are finite; a program needn't handle non-finite values.
Results may differ from the reference program's by a relative error of at most 0.0003.
Values sent between devices are 32-bit elements; how exact they have to be, the bound alone decides.
No kernel may reach another device: no remote copies, remote signals or barrier semaphores. Data moves between devices by JAX's collectives and lax.ppermute only.
A program may use at most 128 MiB of HBM per device.

```python
import math
import jax
import jax.numpy as jnp
from jax import lax

NT = 256
MW = 224
NLAT = 448
NLON = 1024
LEV = 8
BINS = 12
STEPS = 4
SLOT = 128
LB = 96
N_WAVE = 8
N_BAND = 16
DEVICES = 128


def draw_obs_count(key, part):
    count_key, owner_key = jax.random.split(jax.random.fold_in(key, 11))
    counts = jax.random.randint(count_key, (DEVICES, DEVICES), 0, SLOT + 1)
    owner = jax.random.randint(owner_key, (), 0, DEVICES)
    filled = jnp.arange(DEVICES)[None, :] == owner
    return jnp.where(filled, SLOT, counts).astype(jnp.int32)


def with_ends(array, stream_key, low, largest):
    spot = [jax.random.randint(jax.random.fold_in(stream_key, axis), (), 0, length) for axis, length in enumerate(array.shape)]
    longest = array.shape.index(max(array.shape))
    next_to = spot[:longest] + [(spot[longest] + 1) % array.shape[longest]] + spot[longest + 1:]
    return array.at[tuple(spot)].set(low).at[tuple(next_to)].set(largest)


def level_of(stream_key, extent, cuts, smallest, top_value):
    factor_of = 1.0
    for axis_at, blocks in cuts:
        heights = jax.random.uniform(jax.random.fold_in(jax.random.fold_in(stream_key, 6), axis_at), (blocks,), jnp.float32, smallest / len(cuts), top_value / len(cuts))
        factor_of = factor_of * jnp.repeat(jnp.exp(heights), extent[axis_at] // blocks).reshape((-1,) + (1,) * (len(extent) - 1 - axis_at))
    return factor_of


def scatter_about(rng, dims, deviation, reach, pieces=(), kind=jnp.bfloat16):
    entries = deviation * jax.random.normal(rng, dims, jnp.float32)
    if pieces:
        entries = entries * level_of(rng, dims, pieces, -0.22, 0.18)
    return jnp.clip(entries, -reach, reach).astype(kind)


def setup_inputs(seed: int = 0) -> dict:
    keys = jax.random.split(jax.random.key(seed), 15)
    return {
        "control": scatter_about(keys[0], (NT, MW, 2 * LB), 1.0, 6.0, ((0, 16), (1, 8)), jnp.float32),
        "spectral_scale": jnp.clip(jnp.exp(math.log(3.0) - 2.3025851 * jax.random.uniform(keys[1], (NT, MW, 2 * LB), jnp.float32) ** level_of(keys[1], (NT, MW, 2 * LB), ((0, 16), (1, 8)), -0.2, 0.2)), 0.3, 3.0),
        "vertical_root": scatter_about(keys[2], (LB, LB), LB ** -0.5, 0.625, (), jnp.float32),
        "legendre": scatter_about(keys[3], (MW, NLAT, NT), NT ** -0.5, 0.375, ((0, 8),), jnp.float32),
        "zonal_number": jax.random.permutation(keys[4], MW).astype(jnp.int32),
        "courant": jnp.clip(0.05 + 0.84999998 * jax.random.uniform(keys[5], (NLAT, LB, NLON), jnp.float32) ** level_of(keys[5], (NLAT, LB, NLON), ((0, 16), (2, 8)), -0.2, 0.2), 0.05, 0.9),
        "lidar_coef": jnp.clip(jnp.exp(jax.random.uniform(keys[6], (BINS,), jnp.float32, math.log(0.2), math.log(1.0))), 0.2, 1.0),
        "aod_coef": jnp.clip(jnp.exp(jax.random.uniform(keys[7], (LB,), jnp.float32, math.log(0.02), math.log(0.2))), 0.02, 0.2),
        "obs_count": draw_obs_count(jax.random.fold_in(keys[14], 71), 0),
        "obs_column": with_ends(jax.random.randint(keys[9], (DEVICES * DEVICES, SLOT), 0, NLAT * NLON // DEVICES), jax.random.fold_in(keys[9], 1), 0, (NLAT * NLON // DEVICES) - 1).astype(jnp.int32),
        "obs_level": with_ends(jax.random.randint(keys[10], (DEVICES * DEVICES, SLOT), 0, LEV), jax.random.fold_in(keys[10], 1), 0, LEV - 1).astype(jnp.int32),
        "lidar_obs": scatter_about(keys[11], (DEVICES * DEVICES, SLOT), 1.0, 6.0, ((0, 128),), jnp.float32),
        "aod_obs": scatter_about(keys[12], (DEVICES * DEVICES, SLOT), 1.0, 6.0, ((0, 128),), jnp.float32),
        "obs_weight": jnp.clip(jnp.exp(math.log(2.0) - 1.3862944 * jax.random.uniform(keys[13], (DEVICES * DEVICES, SLOT), jnp.float32) ** level_of(keys[13], (DEVICES * DEVICES, SLOT), ((0, 128),), -0.2, 0.2)), 0.5, 2.0),
    }


highest = lax.Precision.HIGHEST


def trig_tables(numbers, lon_first, lon_count, lon_total, factor):
    longitudes = lon_first + jnp.arange(lon_count, dtype=jnp.int32)
    phases = (numbers[:, None] * longitudes[None, :]) % lon_total
    angles = phases.astype(jnp.float32) * (2.0 * math.pi / lon_total)
    return jnp.cos(angles) * factor, jnp.sin(angles) * factor


def settle(tracer, courant):
    outflow = courant * tracer
    inflow = jnp.concatenate([jnp.zeros_like(outflow[:, :BINS]), outflow[:, :-BINS]], axis=1)
    return tracer - outflow + inflow


def settle_adjoint(adjoint, courant):
    below = jnp.concatenate([adjoint[:, BINS:], jnp.zeros_like(adjoint[:, :BINS])], axis=1)
    return adjoint + courant * (below - adjoint)


def departures(profile, levels, active, lidar_vals, aod_vals, weights, lidar_coef, aod_coef):
    chosen = (jnp.arange(LEV, dtype=jnp.int32)[None, :] == levels[:, None]).astype(profile.dtype)
    layered = profile.reshape(-1, LEV, BINS)
    at_level = jnp.sum(chosen[:, :, None] * layered, axis=1)
    lidar_model = jnp.sum(at_level * lidar_coef[None, :], axis=1)
    aod_model = jnp.sum(profile * aod_coef[None, :], axis=1)
    lidar_resid = active * weights * (lidar_model - lidar_vals)
    aod_resid = active * weights * (aod_model - aod_vals)
    spread = lidar_resid[:, None, None] * chosen[:, :, None] * lidar_coef[None, None, :]
    return spread.reshape(-1, LEV * BINS) + aod_resid[:, None] * aod_coef[None, :]


def reference(control, spectral_scale, vertical_root, legendre, zonal_number, courant, lidar_coef, aod_coef, obs_count, obs_column, obs_level, lidar_obs, aod_obs, obs_weight):
    channels = LEV * BINS
    factor = MW ** -0.5
    paired = control.reshape(NT, MW, channels, 2)
    mixed = jnp.einsum('nmcp,cd->nmdp', paired, vertical_root, precision=highest).reshape(NT, MW, 2 * channels)
    scaled = spectral_scale * mixed
    spectral = jnp.einsum('mln,nmc->mlc', legendre, scaled, precision=highest)
    cosine, sine_table = trig_tables(zonal_number, 0, NLON, NLON, factor)
    parts = spectral.reshape(MW, NLAT, channels, 2)
    tracer = jnp.einsum('mo,mtc->tco', cosine, parts[..., 0], precision=highest) - jnp.einsum('mo,mtc->tco', sine_table, parts[..., 1], precision=highest)
    for repeat in range(STEPS):
        tracer = settle(tracer, courant)

    lat_block = NLAT // N_BAND
    lon_block = NLON // N_WAVE
    owners = jnp.arange(DEVICES, dtype=jnp.int32)[:, None]
    slot_index = jnp.arange(SLOT, dtype=jnp.int32)[None, :]

    def one_source(adjoint, source):
        first_row = source * DEVICES
        columns = lax.dynamic_slice_in_dim(obs_column, first_row, DEVICES, 0)
        levels = lax.dynamic_slice_in_dim(obs_level, first_row, DEVICES, 0).reshape(-1)
        lidar_vals = lax.dynamic_slice_in_dim(lidar_obs, first_row, DEVICES, 0).reshape(-1)
        aod_vals = lax.dynamic_slice_in_dim(aod_obs, first_row, DEVICES, 0).reshape(-1)
        weights = lax.dynamic_slice_in_dim(obs_weight, first_row, DEVICES, 0).reshape(-1)
        counts = lax.dynamic_index_in_dim(obs_count, source, 0, keepdims=False)
        active = (slot_index < counts[:, None]).astype(jnp.float32).reshape(-1)
        lat_index = ((owners % N_BAND) * lat_block + columns // lon_block).reshape(-1)
        lon_index = ((owners // N_BAND) * lon_block + columns % lon_block).reshape(-1)
        profile = tracer[lat_index, :, lon_index]
        contrib = departures(profile, levels, active, lidar_vals, aod_vals, weights, lidar_coef, aod_coef)
        return adjoint.at[lat_index, :, lon_index].add(contrib), None

    adjoint, unused = lax.scan(one_source, jnp.zeros_like(tracer), jnp.arange(DEVICES, dtype=jnp.int32))
    for repeat in range(STEPS):
        adjoint = settle_adjoint(adjoint, courant)
    real_adj = jnp.einsum('mo,tco->mtc', cosine, adjoint, precision=highest)
    imag_adj = -jnp.einsum('mo,tco->mtc', sine_table, adjoint, precision=highest)
    spectral_adj = jnp.stack([real_adj, imag_adj], axis=-1).reshape(MW, NLAT, 2 * channels)
    scaled_adj = jnp.einsum('mtn,mtc->nmc', legendre, spectral_adj, precision=highest)
    mixed_adj = (spectral_scale * scaled_adj).reshape(NT, MW, channels, 2)
    control_adj = jnp.einsum('nmdp,cd->nmcp', mixed_adj, vertical_root, precision=highest).reshape(NT, MW, 2 * channels)
    return control + control_adj, tracer
```

```python
import math

import jax
import jax.numpy as jnp
from jax import lax
from jax.experimental import pallas as pl
from jax.experimental.pallas import tpu as pltpu
from jax.sharding import PartitionSpec as P

MW = 224
LEV = 8
BINS = 12
CH = 96
STEPS = 4
WAVES = 8
BANDS = 16
DEVICES = 128
SLOT = 128
GROUPS = 7
NLON = 1024
NLAT = 448
NT = 256
FACTOR = MW ** (-0.5)
f32 = jnp.float32
bf16 = jnp.bfloat16
highest = lax.Precision.HIGHEST
LIMIT = 48 << 20


def params(**kw):
    return pltpu.CompilerParams(vmem_limit_bytes=LIMIT, **kw)


def split(x):
    hi = x.astype(bf16)
    return hi, (x - hi.astype(f32)).astype(bf16)


def mm(a, b):
    return lax.dot_general(a, b, (((1,), (0,)), ((), ())), preferred_element_type=f32)


def mm_nt(a, b):
    return lax.dot_general(a, b, (((1,), (1,)), ((), ())), preferred_element_type=f32)


def iota(shape, dim):
    return lax.broadcasted_iota(jnp.int32, shape, dim)


def turn(parts, axis, width):
    n = len(parts)
    size = parts[0].shape[axis]
    at = iota(parts[0].shape, axis)
    step = n // 2
    while step:
        keep = (at // (step * width)) % 2 == 0
        new = list(parts)
        for i in range(n):
            if (i // step) % 2 == 0:
                a, b = parts[i], parts[i + step]
                new[i] = jnp.where(keep, a, pltpu.roll(b, step * width, axis))
                new[i + step] = jnp.where(keep, pltpu.roll(a, size - step * width, axis), b)
        parts = new
        step //= 2
    return parts


def doubled_root(root):
    rows = (iota((2 * CH, CH), 0) // 2 == iota((2 * CH, CH), 1)).astype(f32)
    cols = (iota((CH, 2 * CH), 1) // 2 == iota((CH, 2 * CH), 0)).astype(f32)
    wide = jnp.dot(rows, root, precision=highest, preferred_element_type=f32)
    wide = jnp.dot(wide, cols, precision=highest, preferred_element_type=f32)
    same = iota((2 * CH, 2 * CH), 0) % 2 == iota((2 * CH, 2 * CH), 1) % 2
    return jnp.where(same, wide, 0.0)


def mix_kernel(control_ref, scale_ref, root_ref, out_ref):
    root = doubled_root(root_ref[...])
    rh, rl = split(root)
    tiles = []
    for m4 in range(4):
        x = jnp.concatenate([control_ref[4 * g + m4] for g in range(GROUPS)], axis=0)
        s = jnp.concatenate([scale_ref[4 * g + m4] for g in range(GROUPS)], axis=0)
        xh, xl = split(x)
        y = (mm(xh, rh) + mm(xl, rh) + mm(xh, rl)) * s
        y = jnp.concatenate([y, jnp.zeros((16, 2 * CH), f32)], axis=0)
        tiles.append(y.T.reshape(24, 8, 128))
    for j, z in enumerate(turn(tiles, 1, 2)):
        out_ref[:, j] = z


def legendre_kernel(modes_ref, table_ref, out_ref, x_ref, order_ref):
    g = pl.program_id(0)

    @pl.when(g == 0)
    def _():
        for half in range(2):
            for c in range(6):
                got = [modes_ref[8 * half + s, 8 * c : 8 * c + 8] for s in range(8)]
                for k, z in enumerate(turn(got, 1, 16)):
                    x_ref[k, 8 * c : 8 * c + 8, 128 * half : 128 * half + 128] = z
        order_ref[...] = lat_order()

    x = x_ref[g]
    slot = (iota((48, NT), 0) % 8) // 2
    acc = None
    for m4 in range(4):
        xh, xl = split(jnp.where(slot == m4, x, 0.0))
        th, tl = split(table_ref[m4])
        both = mm_nt(jnp.concatenate([xh, xl], axis=0), th)
        part = both[:48] + both[48:] + mm_nt(xh, tl)
        acc = part if acc is None else acc + part
    ah, al = split(acc)
    both = mm(jnp.concatenate([ah, al], axis=0), order_ref[...])
    out = both[:48] + both[48:]
    for q in range(4):
        for hc in range(2):
            out_ref[2 * q + hc] = out[24 * hc : 24 * hc + 24, 128 * q : 128 * q + 128]


def lat_order():
    at = iota((NLAT, 512), 1)
    lat = ((at // 8) % 16) * 28 + (at // 128) * 7 + at % 8
    return jnp.where((iota((NLAT, 512), 0) == lat) & (at % 8 < 7), 1.0, 0.0).astype(bf16)


def wave_table_kernel(number_ref, high_ref, low_ref):
    rows = 16
    half = NLON // 2
    row = iota((rows, MW), 0)
    slot = iota((rows, MW), 1)
    part = iota((rows, half), 0) % 2
    lon = iota((rows, half), 1)
    numbers = number_ref[...].astype(f32)
    coefs = [(-1.0) ** k / math.factorial(2 * k + 1) for k in range(6)]

    @pl.loop(0, 2 * MW // rows)
    def _(i):
        first = pl.multiple_of(i * rows, rows)
        mine = (row + first) // 2 == slot
        n = jnp.sum(jnp.where(mine, numbers, 0.0), axis=1, keepdims=True).astype(jnp.int32)
        phase = (n * lon + 256 * part) & (NLON - 1)
        turn_at = (jnp.abs(phase - half) - half // 2).astype(f32)
        y = turn_at * (2.0 * math.pi / NLON)
        y2 = y * y
        value = coefs[5]
        for k in range(4, -1, -1):
            value = value * y2 + coefs[k]
        value = value * y * FACTOR
        vh, vl = split(value)
        high_ref[pl.ds(first, rows), :half] = vh
        low_ref[pl.ds(first, rows), :half] = vl
        sign = (1 - 2 * (n & 1)).astype(f32)
        vh, vl = split(value * sign)
        high_ref[pl.ds(first, rows), half:] = vh
        low_ref[pl.ds(first, rows), half:] = vl


def synthesis_kernel(spec_ref, high_ref, low_ref, out_ref, lhs_ref):
    @pl.when(pl.program_id(0) == 0)
    def _():
        for c in range(3):
            s = spec_ref[:, :, c].reshape(2 * MW, 128).T
            sh, sl = split(s)
            lhs_ref[128 * c : 128 * c + 128] = sh
            lhs_ref[384 + 128 * c : 512 + 128 * c] = sl

    both = mm(lhs_ref[...], high_ref[...])
    out = both[:384] + both[384:] + mm(lhs_ref[:384], low_ref[...])
    for c in range(3):
        for w in range(2):
            tile = out[128 * c : 128 * c + 128, 128 * w : 128 * w + 128]
            out_ref[w, :, c] = tile.reshape(BANDS, 8, 128)


def analysis_kernel(grid_ref, high_ref, low_ref, out_ref, acc_ref):
    i = pl.program_id(0)
    for c in range(3):
        rows = jnp.concatenate(
            [grid_ref[w, :, c].reshape(128, 128) for w in range(2)], axis=1
        )
        gh, gl = split(rows)
        high = high_ref[...]
        part = mm_nt(high, gh) + mm_nt(high, gl) + mm_nt(low_ref[...], gh)

        @pl.when(i == 0)
        def _():
            acc_ref[c] = part

        @pl.when((i > 0) & (i < 3))
        def _():
            acc_ref[c] += part

        @pl.when(i == 3)
        def _():
            out_ref[:, :, c] = (acc_ref[c] + part).reshape(WAVES, GROUPS, 8, 128)


def legendre_adjoint_kernel(spec_ref, table_ref, out_ref, x_ref, order_ref):
    g = pl.program_id(0)

    @pl.when(g == 0)
    def _():
        order_ref[...] = lat_order()
        x_ref[GROUPS] = jnp.zeros((48, NT), f32)

    parts = []
    for hc in range(2):
        cols = [spec_ref[2 * q + hc].reshape(24, 128) for q in range(4)]
        parts.append(jnp.concatenate(cols, axis=1))
    s = jnp.concatenate(parts, axis=0)
    sh, sl = split(s)
    both = mm_nt(jnp.concatenate([sh, sl], axis=0), order_ref[...])
    x = both[:48] + both[48:]
    slot = (iota((48, NLAT), 0) % 8) // 2
    acc = None
    for m4 in range(4):
        xh, xl = split(jnp.where(slot == m4, x, 0.0))
        th, tl = split(table_ref[m4])
        both = mm(jnp.concatenate([xh, xl], axis=0), th)
        part = both[:48] + both[48:] + mm(xh, tl)
        acc = part if acc is None else acc + part
    x_ref[g] = acc

    @pl.when(g == GROUPS - 1)
    def _():
        for half in range(2):
            for c in range(6):
                got = [
                    x_ref[k, 8 * c : 8 * c + 8, 128 * half : 128 * half + 128]
                    for k in range(8)
                ]
                for s, z in enumerate(turn(got, 1, 16)):
                    out_ref[8 * half + s, 8 * c : 8 * c + 8] = z


def unmix_kernel(modes_ref, control_ref, scale_ref, root_ref, out_ref):
    root = doubled_root(root_ref[...])
    rh, rl = split(root)
    tiles = turn([modes_ref[:, j] for j in range(4)], 1, 2)
    for m4 in range(4):
        y = tiles[m4].reshape(2 * CH, 128).T[: 16 * GROUPS]
        s = jnp.concatenate([scale_ref[4 * g + m4] for g in range(GROUPS)], axis=0)
        yh, yl = split(y * s)
        z = mm_nt(yh, rh) + mm_nt(yl, rh) + mm_nt(yh, rl)
        for g in range(GROUPS):
            m = 4 * g + m4
            out_ref[m] = control_ref[m] + z[16 * g : 16 * g + 16]


def pack_kernel(count_ref, column_ref, level_ref, lidar_ref, aod_ref, weight_ref, out_ref):
    counts = jnp.broadcast_to(count_ref[...].astype(f32), (DEVICES, DEVICES)).T
    live = iota((DEVICES, SLOT), 1).astype(f32) < counts
    weight = jnp.where(live, weight_ref[...], 0.0)
    out_ref[:, 0, :] = column_ref[...].astype(f32)
    out_ref[:, 1, :] = level_ref[...].astype(f32)
    out_ref[:, 2, :] = weight
    out_ref[:, 3, :] = weight * lidar_ref[...]
    out_ref[:, 4, :] = weight * aod_ref[...]
    for k in range(5, 8):
        out_ref[:, k, :] = jnp.zeros((DEVICES, SLOT), f32)


def sums_kernel(obs_ref, out_ref, acc_ref):
    i = pl.program_id(0)
    count = obs_ref.shape[0]

    def line(k):
        return jnp.concatenate([obs_ref[s, k : k + 1, :] for s in range(count)], axis=1)

    wide = count * SLOT
    column = line(0).astype(jnp.int32)
    level = line(1).astype(jnp.int32)
    lat = column // 128
    lon = column % 128
    q = (lat >= 7).astype(jnp.int32) + (lat >= 14).astype(jnp.int32) + (lat >= 21).astype(jnp.int32)
    row = q * 64 + level * 8 + (lat - 7 * q)
    rows = jnp.where(iota((256, wide), 0) == row, 1.0, 0.0).astype(bf16)
    cols = jnp.where(iota((128, wide), 0) == lon, 1.0, 0.0).astype(bf16)
    values = []
    for k in range(2, 5):
        for v in split(line(k)):
            values.append(cols * v)
    part = mm_nt(rows, jnp.concatenate(values, axis=0))

    @pl.when(i == 0)
    def _():
        acc_ref[...] = part

    @pl.when(i > 0)
    def _():
        acc_ref[...] += part

    @pl.when(i == pl.num_programs(0) - 1)
    def _():
        for k in range(3):
            out_ref[k] = (
                acc_ref[:, 256 * k : 256 * k + 128] + acc_ref[:, 256 * k + 128 : 256 * k + 256]
            )


def grid_kernel(
    grid_ref, courant_ref, sums_ref, lidar_ref, aod_ref, state_ref, adjoint_ref, flow_ref, hold_ref
):
    for h in range(12):
        rows = [courant_ref[min(t, 6), 8 * h : 8 * h + 8] for t in range(8)]
        for j, z in enumerate(turn(rows, 0, 1)):
            flow_ref[8 * h + j] = z

    chains = [(b2, hc, c) for b2 in range(2) for hc in range(2) for c in range(3)]
    lidar_sum = [None] * LEV
    aod_sum = None
    for b2, hc, c in chains:
        bin_at = b2 * 6 + hc * 3 + c
        x = [grid_ref[0, hc, 2 * l + b2, c] for l in range(LEV)]
        flow = [flow_ref[BINS * l + bin_at] for l in range(LEV)]
        for step in range(STEPS):
            out = [flow[l] * x[l] for l in range(LEV)]
            x = [x[l] - out[l] if l == 0 else x[l] - out[l] + out[l - 1] for l in range(LEV)]
        coef = lidar_ref[bin_at]
        for l in range(LEV):
            hold_ref[BINS * l + bin_at] = x[l]
            lidar_sum[l] = x[l] * coef if lidar_sum[l] is None else lidar_sum[l] + x[l] * coef
            term = x[l] * aod_ref[BINS * l + bin_at]
            aod_sum = term if aod_sum is None else aod_sum + term

    for h in range(12):
        rows = turn([hold_ref[8 * h + j] for j in range(8)], 0, 1)
        for t in range(7):
            state_ref[t, 8 * h : 8 * h + 8] = rows[t]

    weight = [sums_ref[0, 8 * l : 8 * l + 8] for l in range(LEV)]
    lidar = [weight[l] * lidar_sum[l] - sums_ref[1, 8 * l : 8 * l + 8] for l in range(LEV)]
    aod = sum(weight[1:], weight[0]) * aod_sum
    for l in range(LEV):
        aod = aod - sums_ref[2, 8 * l : 8 * l + 8]
    for b2, hc, c in chains:
        bin_at = b2 * 6 + hc * 3 + c
        coef = lidar_ref[bin_at]
        flow = [flow_ref[BINS * l + bin_at] for l in range(LEV)]
        a = [lidar[l] * coef + aod * aod_ref[BINS * l + bin_at] for l in range(LEV)]
        for step in range(STEPS):
            a = [
                a[l] + flow[l] * ((a[l + 1] - a[l]) if l + 1 < LEV else -a[l]) for l in range(LEV)
            ]
        for l in range(LEV):
            adjoint_ref[0, hc, 2 * l + b2, c] = a[l]


def shape(*lengths, kind=f32):
    return jax.ShapeDtypeStruct(lengths, kind)


def whole(*lengths):
    return pl.BlockSpec(lengths, lambda *_: (0,) * len(lengths))


def cost(flops, size):
    return pl.CostEstimate(flops=flops, bytes_accessed=size, transcendentals=0)


def exchange(tiles, axis):
    return lax.all_to_all(tiles, axis, split_axis=0, concat_axis=0, tiled=True)


def observation_sums(counts, columns, levels, lidar_obs, aod_obs, weights):
    packed = pl.pallas_call(
        pack_kernel,
        out_shape=shape(DEVICES, 8, SLOT),
        compiler_params=params(),
        name="pack",
    )(counts, columns, levels, lidar_obs, aod_obs, weights)
    arrived = exchange(packed, ("wave", "band"))
    return pl.pallas_call(
        sums_kernel,
        grid=(16,),
        in_specs=[pl.BlockSpec((8, 8, SLOT), lambda i: (i, 0, 0))],
        out_specs=whole(3, 256, 128),
        out_shape=shape(3, 256, 128),
        scratch_shapes=[pltpu.VMEM((256, 768), f32)],
        compiler_params=params(dimension_semantics=("arbitrary",)),
        cost_estimate=cost(2 * 16384 * 256 * 768, 1 << 20),
        name="sums",
    )(arrived)


def body(
    control,
    spectral_scale,
    vertical_root,
    legendre,
    zonal_number,
    courant,
    lidar_coef,
    aod_coef,
    obs_count,
    obs_column,
    obs_level,
    lidar_obs,
    aod_obs,
    obs_weight,
):
    control = jnp.swapaxes(control, 0, 1)
    scale = jnp.swapaxes(spectral_scale, 0, 1)
    modes = pl.pallas_call(
        mix_kernel,
        out_shape=shape(24, 4, 8, 128),
        compiler_params=params(),
        cost_estimate=cost(6 * 448 * 192 * 192, 1 << 20),
        name="mix",
    )(control, scale, vertical_root)
    modes = exchange(modes.reshape(BANDS, 48, 128), "band")

    sums = observation_sums(obs_count, obs_column, obs_level, lidar_obs, aod_obs, obs_weight)
    high, low = pl.pallas_call(
        wave_table_kernel,
        out_shape=(shape(2 * MW, NLON, kind=bf16), shape(2 * MW, NLON, kind=bf16)),
        compiler_params=params(),
        cost_estimate=cost(20 * 448 * 1024, 2 << 20),
        name="wave_table",
    )(zonal_number.reshape(1, MW))

    legendre_cost = cost(6 * 28 * 448 * 256 * 48, 14 << 20)
    table_spec = pl.BlockSpec((4, NLAT, NT), lambda g: (g, 0, 0))
    in_order = params(dimension_semantics=("arbitrary",))
    legendre_scratch = [pltpu.VMEM((8, 48, NT), f32), pltpu.VMEM((NLAT, 512), bf16)]
    spec = pl.pallas_call(
        legendre_kernel,
        grid=(GROUPS,),
        in_specs=[whole(BANDS, 48, 128), table_spec],
        out_specs=pl.BlockSpec((WAVES, 24, 128), lambda g: (0, g, 0)),
        out_shape=shape(WAVES, 24 * GROUPS, 128),
        scratch_shapes=legendre_scratch,
        compiler_params=in_order,
        cost_estimate=legendre_cost,
        name="legendre",
    )(modes, legendre)
    spec = exchange(spec, "wave").reshape(WAVES, GROUPS, 3, 8, 128)

    wave_spec = pl.BlockSpec((2 * MW, 256), lambda i: (0, i))
    tile_spec = pl.BlockSpec((2, BANDS, 3, 8, 128), lambda i: (i, 0, 0, 0, 0))
    wave_cost = cost(6 * 384 * 448 * 1024, 4 << 20)
    grid = pl.pallas_call(
        synthesis_kernel,
        grid=(4,),
        in_specs=[whole(WAVES, GROUPS, 3, 8, 128), wave_spec, wave_spec],
        out_specs=tile_spec,
        out_shape=shape(WAVES, BANDS, 3, 8, 128),
        scratch_shapes=[pltpu.VMEM((768, 2 * MW), bf16)],
        compiler_params=in_order,
        cost_estimate=wave_cost,
        name="synthesis",
    )(spec, high, low)
    grid = exchange(grid.reshape(DEVICES, 24, 128), ("wave", "band"))

    block = pl.BlockSpec((1, 2, BANDS, 3, 8, 128), lambda q: (q, 0, 0, 0, 0, 0))
    field = pl.BlockSpec((7, CH, 128), lambda q: (q, 0, 0))
    scalars = pl.BlockSpec(memory_space=pltpu.SMEM)
    state, adjoint = pl.pallas_call(
        grid_kernel,
        grid=(4,),
        in_specs=[block, field, pl.BlockSpec((3, 64, 128), lambda q: (0, q, 0)), scalars, scalars],
        out_specs=(field, block),
        out_shape=(shape(28, CH, 128), shape(4, 2, BANDS, 3, 8, 128)),
        scratch_shapes=[pltpu.VMEM((CH, 8, 128), f32), pltpu.VMEM((CH, 8, 128), f32)],
        compiler_params=in_order,
        cost_estimate=cost(40 * 28 * 96 * 128, 6 << 20),
        name="grid_steps",
    )(grid.reshape(4, 2, BANDS, 3, 8, 128), courant, sums, lidar_coef, aod_coef)
    adjoint = exchange(adjoint.reshape(DEVICES, 24, 128), ("wave", "band"))

    spec = pl.pallas_call(
        analysis_kernel,
        grid=(4,),
        in_specs=[tile_spec, wave_spec, wave_spec],
        out_specs=whole(WAVES, GROUPS, 3, 8, 128),
        out_shape=shape(WAVES, GROUPS, 3, 8, 128),
        scratch_shapes=[pltpu.VMEM((3, 2 * MW, 128), f32)],
        compiler_params=in_order,
        cost_estimate=wave_cost,
        name="analysis",
    )(adjoint.reshape(WAVES, BANDS, 3, 8, 128), high, low)
    spec = exchange(spec.reshape(WAVES, 24 * GROUPS, 128), "wave")

    modes = pl.pallas_call(
        legendre_adjoint_kernel,
        grid=(GROUPS,),
        in_specs=[pl.BlockSpec((WAVES, 24, 128), lambda g: (0, g, 0)), table_spec],
        out_specs=whole(BANDS, 48, 128),
        out_shape=shape(BANDS, 48, 128),
        scratch_shapes=legendre_scratch,
        compiler_params=in_order,
        cost_estimate=legendre_cost,
        name="legendre_adjoint",
    )(spec, legendre)
    modes = exchange(modes, "band").reshape(24, 4, 8, 128)

    gradient = pl.pallas_call(
        unmix_kernel,
        out_shape=shape(28, 16, 192),
        compiler_params=params(),
        cost_estimate=cost(6 * 448 * 192 * 192, 1 << 20),
        name="unmix",
    )(modes, control, scale, vertical_root)
    return jnp.swapaxes(gradient, 0, 1), state


def solution(mesh):
    both = ("wave", "band")
    placed = (
        P("band", "wave", None),
        P("band", "wave", None),
        P(),
        P("wave", None, None),
        P(),
        P("band", None, "wave"),
        P(),
        P(),
        P(both, None),
        P(both, None),
        P(both, None),
        P(both, None),
        P(both, None),
        P(both, None),
    )
    return jax.shard_map(
        body,
        mesh=mesh,
        in_specs=placed,
        out_specs=(P("band", "wave", None), P("band", None, "wave")),
        check_vma=False,
    )
```

```python
import math

import jax
import jax.numpy as jnp
from jax import lax
from jax.experimental import pallas as pl
from jax.experimental.pallas import tpu as pltpu
from jax.sharding import PartitionSpec as P

MW = 224
LEV = 8
BINS = 12
CH = 96
STEPS = 4
WAVES = 8
BANDS = 16
DEVICES = 128
SLOT = 128
GROUPS = 7
NLON = 1024
NLAT = 448
NT = 256
FACTOR = MW ** (-0.5)
f32 = jnp.float32
bf16 = jnp.bfloat16
highest = lax.Precision.HIGHEST
LIMIT = 24 << 20


def params(**kw):
    return pltpu.CompilerParams(vmem_limit_bytes=LIMIT, **kw)


def split(x):
    hi = x.astype(bf16)
    return hi, (x - hi.astype(f32)).astype(bf16)


def mm(a, b):
    return lax.dot_general(a, b, (((1,), (0,)), ((), ())), preferred_element_type=f32)


def mm_nt(a, b):
    return lax.dot_general(a, b, (((1,), (1,)), ((), ())), preferred_element_type=f32)


def iota(shape, dim):
    return lax.broadcasted_iota(jnp.int32, shape, dim)


def turn(parts, axis, width):
    n = len(parts)
    size = parts[0].shape[axis]
    at = iota(parts[0].shape, axis)
    step = n // 2
    while step:
        keep = (at // (step * width)) % 2 == 0
        new = list(parts)
        for i in range(n):
            if (i // step) % 2 == 0:
                a, b = parts[i], parts[i + step]
                new[i] = jnp.where(keep, a, pltpu.roll(b, step * width, axis))
                new[i + step] = jnp.where(keep, pltpu.roll(a, size - step * width, axis), b)
        parts = new
        step //= 2
    return parts


def doubled_root(root):
    rows = (iota((2 * CH, CH), 0) // 2 == iota((2 * CH, CH), 1)).astype(f32)
    cols = (iota((CH, 2 * CH), 1) // 2 == iota((CH, 2 * CH), 0)).astype(f32)
    wide = jnp.dot(rows, root, precision=highest, preferred_element_type=f32)
    wide = jnp.dot(wide, cols, precision=highest, preferred_element_type=f32)
    same = iota((2 * CH, 2 * CH), 0) % 2 == iota((2 * CH, 2 * CH), 1) % 2
    return jnp.where(same, wide, 0.0)


def mix_kernel(
    control_hbm,
    scale_hbm,
    root_hbm,
    column_hbm,
    level_hbm,
    lidar_hbm,
    aod_hbm,
    weight_hbm,
    count_hbm,
    out_ref,
    control_ref,
    scale_ref,
    root_ref,
    index_ref,
    value_ref,
    count_ref,
    obs_ref,
    sem,
):
    copies = [
        pltpu.make_async_copy(source, target, sem.at[k])
        for k, (source, target) in enumerate(
            (
                (root_hbm, root_ref),
                (control_hbm, control_ref),
                (scale_hbm, scale_ref),
                (column_hbm, index_ref.at[0]),
                (level_hbm, index_ref.at[1]),
                (lidar_hbm, value_ref.at[0]),
                (aod_hbm, value_ref.at[1]),
                (weight_hbm, value_ref.at[2]),
                (count_hbm, count_ref),
            )
        )
    ]
    for copy in copies:
        copy.start()
    for copy in copies[:3]:
        copy.wait()
    root = doubled_root(root_ref[...])
    rh, rl = split(root)
    tiles = []
    for m4 in range(4):
        x = jnp.concatenate([control_ref[4 * g + m4] for g in range(GROUPS)], axis=0)
        s = jnp.concatenate([scale_ref[4 * g + m4] for g in range(GROUPS)], axis=0)
        xh, xl = split(x)
        y = (mm(xh, rh) + mm(xl, rh) + mm(xh, rl)) * s
        y = jnp.concatenate([y, jnp.zeros((16, 2 * CH), f32)], axis=0)
        tiles.append(y.T.reshape(24, 8, 128))
    for j, z in enumerate(turn(tiles, 1, 2)):
        for h in range(24):
            c = 4 * h + j
            out_ref[c // 6, 8 * (c % 6) : 8 * (c % 6) + 8] = z[h]

    for copy in copies[3:]:
        copy.wait()
    counts = jnp.broadcast_to(count_ref[...].astype(f32), (DEVICES, DEVICES)).T
    live = iota((DEVICES, SLOT), 1).astype(f32) < counts
    weight = jnp.where(live, value_ref[2], 0.0)
    obs_ref[0] = index_ref[0].astype(f32)
    obs_ref[1] = index_ref[1].astype(f32)
    obs_ref[2] = weight
    obs_ref[3] = weight * value_ref[0]
    obs_ref[4] = weight * value_ref[1]
    for band in range(BANDS):
        for k in range(5):
            rows = obs_ref[k, pl.ds(band, WAVES, stride=BANDS), :]
            out_ref[band, 48 + 8 * k : 56 + 8 * k] = rows


def table_copies(table_hbm, table_ref, sem):
    copies = [
        pltpu.make_async_copy(table_hbm.at[m], table_ref.at[m], sem.at[m])
        for m in range(4 * GROUPS)
    ]
    for copy in copies:
        copy.start()
    return copies


def legendre_kernel(modes_ref, table_hbm, out_ref, acc_ref, table_ref, sem):
    copies = table_copies(table_hbm, table_ref, sem)
    x = [[None] * 12 for g in range(8)]
    for half in range(2):
        for c in range(6):
            got = [modes_ref[8 * half + s, 8 * c : 8 * c + 8] for s in range(8)]
            for g, z in enumerate(turn(got, 1, 16)):
                x[g][6 * half + c] = z
    for k in range(5):
        for half in range(2):
            got = [modes_ref[8 * half + s, 48 + 8 * k : 56 + 8 * k] for s in range(8)]
            at = 168 + 16 * k + 8 * half
            for w, z in enumerate(turn(got, 0, 1)):
                out_ref[w, at : at + 8] = z

    slot = (iota((48, NT), 0) % 8) // 2
    for g in range(GROUPS):
        halves = [jnp.concatenate(x[g][6 * h : 6 * h + 6], axis=0) for h in range(2)]
        mine = jnp.concatenate(halves, axis=1)
        acc = None
        for m4 in range(4):
            xh, xl = split(jnp.where(slot == m4, mine, 0.0))
            copies[4 * g + m4].wait()
            th, tl = split(table_ref[4 * g + m4])
            both = mm_nt(jnp.concatenate([xh, xl], axis=0), th)
            part = both[:48] + both[48:] + mm_nt(xh, tl)
            acc = part if acc is None else acc + part
        for hc in range(2):
            at = 168 * hc + 24 * g
            acc_ref[at : at + 24] = acc[24 * hc : 24 * hc + 24]
    ah, al = split(acc_ref[...])
    order = lat_order()
    out = mm(ah, order) + mm(al, order)
    for q in range(4):
        for hc in range(2):
            out_ref[2 * q + hc, :168] = out[168 * hc : 168 * hc + 168, 128 * q : 128 * q + 128]


def lat_order():
    at = iota((NLAT, 512), 1)
    lat = ((at // 8) % 16) * 28 + (at // 128) * 7 + at % 8
    return jnp.where((iota((NLAT, 512), 0) == lat) & (at % 8 < 7), 1.0, 0.0).astype(bf16)


def wave_table_kernel(number_ref, high_ref, low_ref):
    rows = 16
    half = NLON // 2
    row = iota((rows, MW), 0)
    slot = iota((rows, MW), 1)
    part = iota((rows, half), 0) % 2
    lon = iota((rows, half), 1)
    numbers = number_ref[...].astype(f32)
    coefs = [(-1.0) ** k / math.factorial(2 * k + 1) for k in range(6)]

    @pl.loop(0, 2 * MW // rows)
    def _(i):
        first = pl.multiple_of(i * rows, rows)
        mine = (row + first) // 2 == slot
        n = jnp.sum(jnp.where(mine, numbers, 0.0), axis=1, keepdims=True).astype(jnp.int32)
        phase = (n * lon + 256 * part) & (NLON - 1)
        turn_at = (jnp.abs(phase - half) - half // 2).astype(f32)
        y = turn_at * (2.0 * math.pi / NLON)
        y2 = y * y
        value = coefs[5]
        for k in range(4, -1, -1):
            value = value * y2 + coefs[k]
        value = value * y * FACTOR
        vh, vl = split(value)
        high_ref[pl.ds(first, rows), :half] = vh
        low_ref[pl.ds(first, rows), :half] = vl
        sign = (1 - 2 * (n & 1)).astype(f32)
        vh, vl = split(value * sign)
        high_ref[pl.ds(first, rows), half:] = vh
        low_ref[pl.ds(first, rows), half:] = vl


def synthesis_kernel(spec_ref, high_ref, low_ref, out_ref, lhs_ref):
    @pl.when(pl.program_id(0) == 0)
    def _():
        rows = spec_ref[:, :168].reshape(WAVES, GROUPS, 3, 8, 128)
        for c in range(3):
            s = rows[:, :, c].reshape(2 * MW, 128).T
            sh, sl = split(s)
            lhs_ref[128 * c : 128 * c + 128] = sh
            lhs_ref[384 + 128 * c : 512 + 128 * c] = sl

    both = mm(lhs_ref[...], high_ref[...])
    out = both[:384] + both[384:] + mm(lhs_ref[:384], low_ref[...])
    for c in range(3):
        for w in range(2):
            tile = out[128 * c : 128 * c + 128, 128 * w : 128 * w + 128]
            out_ref[w, :, c] = tile.reshape(BANDS, 8, 128)


def analysis_kernel(grid_ref, high_ref, low_ref, out_ref, acc_ref):
    i = pl.program_id(0)
    tiles = []
    for c in range(3):
        parts = [grid_ref[w, :, c].reshape(128, 128) for w in range(2)]
        tiles.append(jnp.concatenate(parts, axis=1))
    gh, gl = split(jnp.concatenate(tiles, axis=0))
    both = mm_nt(high_ref[...], jnp.concatenate([gh, gl], axis=0))
    part = both[:, :384] + both[:, 384:] + mm_nt(low_ref[...], gh)

    @pl.when(i == 0)
    def _():
        acc_ref[...] = part

    @pl.when((i > 0) & (i < 3))
    def _():
        acc_ref[...] += part

    @pl.when(i == 3)
    def _():
        total = acc_ref[...] + part
        for c in range(3):
            rows = total[:, 128 * c : 128 * c + 128]
            out_ref[:, :, c] = rows.reshape(WAVES, GROUPS, 8, 128)


def legendre_adjoint_kernel(spec_ref, table_hbm, out_ref, acc_ref, table_ref, sem):
    copies = table_copies(table_hbm, table_ref, sem)
    order = lat_order()
    for hc in range(2):
        s = jnp.concatenate([spec_ref[2 * q + hc] for q in range(4)], axis=1)
        sh, sl = split(s)
        acc_ref[168 * hc : 168 * hc + 168] = mm_nt(sh, order) + mm_nt(sl, order)
    slot = (iota((48, NLAT), 0) % 8) // 2
    x = []
    for g in range(GROUPS):
        rows = [acc_ref[168 * hc + 24 * g : 168 * hc + 24 * g + 24] for hc in range(2)]
        mine = jnp.concatenate(rows, axis=0)
        acc = None
        for m4 in range(4):
            xh, xl = split(jnp.where(slot == m4, mine, 0.0))
            copies[4 * g + m4].wait()
            th, tl = split(table_ref[4 * g + m4])
            both = mm(jnp.concatenate([xh, xl], axis=0), th)
            part = both[:48] + both[48:] + mm(xh, tl)
            acc = part if acc is None else acc + part
        x.append(acc)
    x.append(jnp.zeros((48, NT), f32))
    for half in range(2):
        for c in range(6):
            got = [v[8 * c : 8 * c + 8, 128 * half : 128 * half + 128] for v in x]
            for s, z in enumerate(turn(got, 1, 16)):
                out_ref[8 * half + s, 8 * c : 8 * c + 8] = z


def unmix_kernel(modes_ref, control_ref, scale_ref, root_ref, out_ref):
    root = doubled_root(root_ref[...])
    rh, rl = split(root)
    tiles = turn([modes_ref[:, j] for j in range(4)], 1, 2)
    for m4 in range(4):
        y = tiles[m4].reshape(2 * CH, 128).T[: 16 * GROUPS]
        s = jnp.concatenate([scale_ref[4 * g + m4] for g in range(GROUPS)], axis=0)
        yh, yl = split(y * s)
        z = mm_nt(yh, rh) + mm_nt(yl, rh) + mm_nt(yh, rl)
        for g in range(GROUPS):
            m = 4 * g + m4
            out_ref[m] = control_ref[m] + z[16 * g : 16 * g + 16]


def sums_kernel(obs_ref, out_ref, acc_ref):
    i = pl.program_id(0)
    part = None
    for half in range(2):

        def line(k):
            at = 168 + 16 * k + 8 * half
            rows = obs_ref[0, at : at + 8]
            return jnp.concatenate([rows[s : s + 1] for s in range(8)], axis=1)

        column = line(0).astype(jnp.int32)
        level = line(1).astype(jnp.int32)
        lat = column // 128
        lon = column % 128
        q = sum((lat >= 7 * k).astype(jnp.int32) for k in range(1, 4))
        row = q * 64 + level * 8 + (lat - 7 * q)
        rows = jnp.where(iota((256, 1024), 0) == row, 1.0, 0.0).astype(bf16)
        cols = jnp.where(iota((128, 1024), 0) == lon, 1.0, 0.0).astype(bf16)
        values = []
        for k in range(2, 5):
            for v in split(line(k)):
                values.append(cols * v)
        new = mm_nt(rows, jnp.concatenate(values, axis=0))
        part = new if part is None else part + new

    @pl.when(i == 0)
    def _():
        acc_ref[...] = part

    @pl.when(i > 0)
    def _():
        acc_ref[...] += part

    @pl.when(i == WAVES - 1)
    def _():
        for k in range(3):
            first = acc_ref[:, 256 * k : 256 * k + 128]
            out_ref[k] = first + acc_ref[:, 256 * k + 128 : 256 * k + 256]


def grid_kernel(
    grid_ref, courant_ref, sums_ref, lidar_ref, aod_ref, state_ref, adjoint_ref, flow_ref, hold_ref
):
    for h in range(12):
        rows = [courant_ref[min(t, 6), 8 * h : 8 * h + 8] for t in range(8)]
        for j, z in enumerate(turn(rows, 0, 1)):
            flow_ref[8 * h + j] = z

    chains = [(b2, hc, c) for b2 in range(2) for hc in range(2) for c in range(3)]
    lidar_sum = [None] * LEV
    aod_sum = None
    for b2, hc, c in chains:
        bin_at = b2 * 6 + hc * 3 + c
        x = [grid_ref[0, hc, 2 * l + b2, c] for l in range(LEV)]
        flow = [flow_ref[BINS * l + bin_at] for l in range(LEV)]
        for step in range(STEPS):
            out = [flow[l] * x[l] for l in range(LEV)]
            x = [x[l] - out[l] if l == 0 else x[l] - out[l] + out[l - 1] for l in range(LEV)]
        coef = lidar_ref[bin_at]
        for l in range(LEV):
            hold_ref[BINS * l + bin_at] = x[l]
            lidar_sum[l] = x[l] * coef if lidar_sum[l] is None else lidar_sum[l] + x[l] * coef
            term = x[l] * aod_ref[BINS * l + bin_at]
            aod_sum = term if aod_sum is None else aod_sum + term

    for h in range(12):
        rows = turn([hold_ref[8 * h + j] for j in range(8)], 0, 1)
        for t in range(7):
            state_ref[t, 8 * h : 8 * h + 8] = rows[t]

    weight = [sums_ref[0, 8 * l : 8 * l + 8] for l in range(LEV)]
    lidar = [weight[l] * lidar_sum[l] - sums_ref[1, 8 * l : 8 * l + 8] for l in range(LEV)]
    aod = sum(weight[1:], weight[0]) * aod_sum
    for l in range(LEV):
        aod = aod - sums_ref[2, 8 * l : 8 * l + 8]
    for b2, hc, c in chains:
        bin_at = b2 * 6 + hc * 3 + c
        coef = lidar_ref[bin_at]
        flow = [flow_ref[BINS * l + bin_at] for l in range(LEV)]
        a = [lidar[l] * coef + aod * aod_ref[BINS * l + bin_at] for l in range(LEV)]
        for step in range(STEPS):
            a = [
                a[l] + flow[l] * ((a[l + 1] - a[l]) if l + 1 < LEV else -a[l]) for l in range(LEV)
            ]
        for l in range(LEV):
            adjoint_ref[0, hc, 2 * l + b2, c] = a[l]


def shape(*lengths, kind=f32):
    return jax.ShapeDtypeStruct(lengths, kind)


def whole(*lengths):
    return pl.BlockSpec(lengths, lambda *_: (0,) * len(lengths))


def in_hbm(x):
    return pltpu.with_memory_space_constraint(x, pltpu.HBM)


def cost(flops, size):
    return pl.CostEstimate(flops=flops, bytes_accessed=size, transcendentals=0)


def exchange(tiles, axis):
    return lax.all_to_all(tiles, axis, split_axis=0, concat_axis=0, tiled=True)


def body(
    control,
    spectral_scale,
    vertical_root,
    legendre,
    zonal_number,
    courant,
    lidar_coef,
    aod_coef,
    obs_count,
    obs_column,
    obs_level,
    lidar_obs,
    aod_obs,
    obs_weight,
):
    control = jnp.swapaxes(control, 0, 1)
    scale = jnp.swapaxes(spectral_scale, 0, 1)
    hbm = pl.BlockSpec(memory_space=pltpu.HBM)
    modes = pl.pallas_call(
        mix_kernel,
        in_specs=[hbm] * 9,
        out_specs=whole(BANDS, 88, 128),
        out_shape=shape(BANDS, 88, 128),
        scratch_shapes=[
            pltpu.VMEM((28, 16, 192), f32),
            pltpu.VMEM((28, 16, 192), f32),
            pltpu.VMEM((CH, CH), f32),
            pltpu.VMEM((2, DEVICES, SLOT), jnp.int32),
            pltpu.VMEM((3, DEVICES, SLOT), f32),
            pltpu.VMEM((1, DEVICES), jnp.int32),
            pltpu.VMEM((5, DEVICES, SLOT), f32),
            pltpu.SemaphoreType.DMA((9,)),
        ],
        compiler_params=params(),
        cost_estimate=cost(6 * 448 * 192 * 192, 1 << 20),
        name="mix",
    )(
        *(
            in_hbm(x)
            for x in (
                control,
                scale,
                vertical_root,
                obs_column,
                obs_level,
                lidar_obs,
                aod_obs,
                obs_weight,
                obs_count,
            )
        )
    )
    modes = exchange(modes, "band")

    high, low = pl.pallas_call(
        wave_table_kernel,
        out_shape=(shape(2 * MW, NLON, kind=bf16), shape(2 * MW, NLON, kind=bf16)),
        compiler_params=params(),
        cost_estimate=cost(20 * 448 * 1024, 2 << 20),
        name="wave_table",
    )(zonal_number.reshape(1, MW))

    legendre_cost = cost(6 * 28 * 448 * 256 * 48, 14 << 20)
    in_order = params(dimension_semantics=("arbitrary",))
    legendre_scratch = [
        pltpu.VMEM((336, NLAT), f32),
        pltpu.VMEM((28, NLAT, NT), f32),
        pltpu.SemaphoreType.DMA((28,)),
    ]
    spec = pl.pallas_call(
        legendre_kernel,
        in_specs=[whole(BANDS, 88, 128), hbm],
        out_specs=whole(WAVES, 248, 128),
        out_shape=shape(WAVES, 248, 128),
        scratch_shapes=legendre_scratch,
        compiler_params=params(),
        cost_estimate=legendre_cost,
        name="legendre",
    )(modes, in_hbm(legendre))
    spec = exchange(spec, "wave")
    sums = pl.pallas_call(
        sums_kernel,
        grid=(WAVES,),
        in_specs=[pl.BlockSpec((1, 248, 128), lambda i: (i, 0, 0))],
        out_specs=whole(3, 256, 128),
        out_shape=shape(3, 256, 128),
        scratch_shapes=[pltpu.VMEM((256, 768), f32)],
        compiler_params=in_order,
        cost_estimate=cost(2 * 16384 * 256 * 768, 1 << 20),
        name="sums",
    )(spec)

    wave_spec = pl.BlockSpec((2 * MW, 256), lambda i: (0, i))
    tile_spec = pl.BlockSpec((2, BANDS, 3, 8, 128), lambda i: (i, 0, 0, 0, 0))
    wave_cost = cost(6 * 384 * 448 * 1024, 4 << 20)
    grid = pl.pallas_call(
        synthesis_kernel,
        grid=(4,),
        in_specs=[whole(WAVES, 248, 128), wave_spec, wave_spec],
        out_specs=tile_spec,
        out_shape=shape(WAVES, BANDS, 3, 8, 128),
        scratch_shapes=[pltpu.VMEM((768, 2 * MW), bf16)],
        compiler_params=in_order,
        cost_estimate=wave_cost,
        name="synthesis",
    )(spec, high, low)
    grid = exchange(grid.reshape(DEVICES, 24, 128), ("wave", "band"))

    block = pl.BlockSpec((1, 2, BANDS, 3, 8, 128), lambda q: (q, 0, 0, 0, 0, 0))
    field = pl.BlockSpec((7, CH, 128), lambda q: (q, 0, 0))
    scalars = pl.BlockSpec(memory_space=pltpu.SMEM)
    state, adjoint = pl.pallas_call(
        grid_kernel,
        grid=(4,),
        in_specs=[block, field, pl.BlockSpec((3, 64, 128), lambda q: (0, q, 0)), scalars, scalars],
        out_specs=(field, block),
        out_shape=(shape(28, CH, 128), shape(4, 2, BANDS, 3, 8, 128)),
        scratch_shapes=[pltpu.VMEM((CH, 8, 128), f32), pltpu.VMEM((CH, 8, 128), f32)],
        compiler_params=in_order,
        cost_estimate=cost(40 * 28 * 96 * 128, 6 << 20),
        name="grid_steps",
    )(grid.reshape(4, 2, BANDS, 3, 8, 128), in_hbm(courant), in_hbm(sums), lidar_coef, aod_coef)
    adjoint = exchange(adjoint.reshape(DEVICES, 24, 128), ("wave", "band"))

    spec = pl.pallas_call(
        analysis_kernel,
        grid=(4,),
        in_specs=[tile_spec, wave_spec, wave_spec],
        out_specs=whole(WAVES, GROUPS, 3, 8, 128),
        out_shape=shape(WAVES, GROUPS, 3, 8, 128),
        scratch_shapes=[pltpu.VMEM((2 * MW, 384), f32)],
        compiler_params=in_order,
        cost_estimate=wave_cost,
        name="analysis",
    )(adjoint.reshape(WAVES, BANDS, 3, 8, 128), high, low)
    spec = exchange(spec.reshape(WAVES, 24 * GROUPS, 128), "wave")

    modes = pl.pallas_call(
        legendre_adjoint_kernel,
        in_specs=[whole(WAVES, 168, 128), hbm],
        out_specs=whole(BANDS, 48, 128),
        out_shape=shape(BANDS, 48, 128),
        scratch_shapes=legendre_scratch,
        compiler_params=params(),
        cost_estimate=legendre_cost,
        name="legendre_adjoint",
    )(spec, in_hbm(legendre))
    modes = exchange(modes, "band").reshape(24, 4, 8, 128)

    gradient = pl.pallas_call(
        unmix_kernel,
        out_shape=shape(28, 16, 192),
        compiler_params=params(),
        cost_estimate=cost(6 * 448 * 192 * 192, 1 << 20),
        name="unmix",
    )(modes, control, scale, vertical_root)
    return jnp.swapaxes(gradient, 0, 1), state


def solution(mesh):
    both = ("wave", "band")
    placed = (
        P("band", "wave", None),
        P("band", "wave", None),
        P(),
        P("wave", None, None),
        P(),
        P("band", None, "wave"),
        P(),
        P(),
        P(both, None),
        P(both, None),
        P(both, None),
        P(both, None),
        P(both, None),
        P(both, None),
    )
    return jax.shard_map(
        body,
        mesh=mesh,
        in_specs=placed,
        out_specs=(P("band", "wave", None), P("band", None, "wave")),
        check_vma=False,
    )
```

```python
import math

import jax
import jax.numpy as jnp
from jax import lax
from jax.experimental import pallas as pl
from jax.experimental.pallas import tpu as pltpu
from jax.sharding import PartitionSpec as P

MW = 224
LEV = 8
BINS = 12
CH = 96
STEPS = 4
WAVES = 8
BANDS = 16
DEVICES = 128
SLOT = 128
GROUPS = 7
NLON = 1024
NLAT = 448
NT = 256
TILE = 21
FACTOR = MW ** (-0.5)
f32 = jnp.float32
bf16 = jnp.bfloat16
highest = lax.Precision.HIGHEST
LIMIT = 24 << 20


def params(**kw):
    return pltpu.CompilerParams(vmem_limit_bytes=LIMIT, **kw)


def split(x):
    hi = x.astype(bf16)
    return hi, (x - hi.astype(f32)).astype(bf16)


def mm(a, b):
    return lax.dot_general(a, b, (((1,), (0,)), ((), ())), preferred_element_type=f32)


def mm_nt(a, b):
    return lax.dot_general(a, b, (((1,), (1,)), ((), ())), preferred_element_type=f32)


def iota(shape, dim):
    return lax.broadcasted_iota(jnp.int32, shape, dim)


def turn(parts, axis, width):
    n = len(parts)
    size = parts[0].shape[axis]
    at = iota(parts[0].shape, axis)
    step = n // 2
    while step:
        keep = (at // (step * width)) % 2 == 0
        new = list(parts)
        for i in range(n):
            if (i // step) % 2 == 0:
                a, b = parts[i], parts[i + step]
                new[i] = jnp.where(keep, a, pltpu.roll(b, step * width, axis))
                new[i + step] = jnp.where(keep, pltpu.roll(a, size - step * width, axis), b)
        parts = new
        step //= 2
    return parts


def doubled_root(root):
    rows = (iota((2 * CH, CH), 0) // 2 == iota((2 * CH, CH), 1)).astype(f32)
    cols = (iota((CH, 2 * CH), 1) // 2 == iota((CH, 2 * CH), 0)).astype(f32)
    wide = jnp.dot(rows, root, precision=highest, preferred_element_type=f32)
    wide = jnp.dot(wide, cols, precision=highest, preferred_element_type=f32)
    same = iota((2 * CH, 2 * CH), 0) % 2 == iota((2 * CH, 2 * CH), 1) % 2
    return jnp.where(same, wide, 0.0)


def mix_kernel(
    control_hbm,
    scale_hbm,
    root_hbm,
    column_hbm,
    level_hbm,
    lidar_hbm,
    aod_hbm,
    weight_hbm,
    count_hbm,
    out_ref,
    control_ref,
    scale_ref,
    root_ref,
    index_ref,
    value_ref,
    count_ref,
    obs_ref,
    sem,
):
    copies = [
        pltpu.make_async_copy(source, target, sem.at[k])
        for k, (source, target) in enumerate(
            (
                (root_hbm, root_ref),
                (control_hbm, control_ref),
                (scale_hbm, scale_ref),
                (column_hbm, index_ref.at[0]),
                (level_hbm, index_ref.at[1]),
                (lidar_hbm, value_ref.at[0]),
                (aod_hbm, value_ref.at[1]),
                (weight_hbm, value_ref.at[2]),
                (count_hbm, count_ref),
            )
        )
    ]
    for copy in copies:
        copy.start()
    for copy in copies[:3]:
        copy.wait()
    root = doubled_root(root_ref[...])
    rh, rl = split(root)
    tiles = []
    for m4 in range(4):
        x = jnp.concatenate([control_ref[4 * g + m4] for g in range(GROUPS)], axis=0)
        s = jnp.concatenate([scale_ref[4 * g + m4] for g in range(GROUPS)], axis=0)
        xh, xl = split(x)
        y = (mm(xh, rh) + mm(xl, rh) + mm(xh, rl)) * s
        y = jnp.concatenate([y, jnp.zeros((16, 2 * CH), f32)], axis=0)
        tiles.append(y.T.reshape(24, 8, 128))
    for j, z in enumerate(turn(tiles, 1, 2)):
        for h in range(24):
            c = 4 * h + j
            out_ref[c // 6, 8 * (c % 6) : 8 * (c % 6) + 8] = z[h]

    for copy in copies[3:]:
        copy.wait()
    counts = jnp.broadcast_to(count_ref[...].astype(f32), (DEVICES, DEVICES)).T
    live = iota((DEVICES, SLOT), 1).astype(f32) < counts
    weight = jnp.where(live, value_ref[2], 0.0)
    obs_ref[0] = index_ref[0].astype(f32)
    obs_ref[1] = index_ref[1].astype(f32)
    obs_ref[2] = weight
    obs_ref[3] = weight * value_ref[0]
    obs_ref[4] = weight * value_ref[1]
    for band in range(BANDS):
        for k in range(5):
            rows = obs_ref[k, pl.ds(band, WAVES, stride=BANDS), :]
            out_ref[band, 48 + 8 * k : 56 + 8 * k] = rows


def table_copies(table_hbm, table_ref, sem):
    copies = []
    for g in range(GROUPS):
        at = pl.ds(4 * g, 4)
        copies.append(pltpu.make_async_copy(table_hbm.at[at], table_ref.at[at], sem.at[g]))
    for copy in copies:
        copy.start()
    return copies


def legendre_kernel(modes_ref, table_hbm, out_ref, x_ref, acc_ref, table_ref, sem):
    copies = table_copies(table_hbm, table_ref, sem)
    for half in range(2):
        for c in range(6):
            got = [modes_ref[8 * half + s, 8 * c : 8 * c + 8] for s in range(8)]
            for g, z in enumerate(turn(got, 1, 16)):
                if g < GROUPS:
                    x_ref[g, 8 * c : 8 * c + 8, 128 * half : 128 * half + 128] = z
    for k in range(5):
        for half in range(2):
            got = [modes_ref[8 * half + s, 48 + 8 * k : 56 + 8 * k] for s in range(8)]
            at = 168 + 16 * k + 8 * half
            for w, z in enumerate(turn(got, 0, 1)):
                out_ref[w, at : at + 8] = z

    slot = (iota((48, NT), 0) % 8) // 2
    order = lat_order()
    for g in range(GROUPS):
        copies[g].wait()
        x = x_ref[g]
        acc = None
        for m4 in range(4):
            xh, xl = split(jnp.where(slot == m4, x, 0.0))
            both = jnp.concatenate(split(table_ref[4 * g + m4]), axis=0)
            both = mm_nt(jnp.concatenate([xh, xl], axis=0), both)
            part = both[:48, :NLAT] + (both[48:, :NLAT] + both[:48, NLAT:])
            acc = part if acc is None else acc + part
        acc_ref[g] = acc
        for first, last in ((0, 5), (5, 7)):
            if g + 1 == last:
                rows = 48 * (last - first)
                part = acc_ref[first:last].reshape(rows, NLAT)
                both = mm(jnp.concatenate(split(part), axis=0), order)
                out = both[:rows] + both[rows:]
                for k in range(first, last):
                    for q in range(4):
                        for hc in range(2):
                            at = 48 * (k - first) + 24 * hc
                            tile = out[at : at + 24, 128 * q : 128 * q + 128]
                            out_ref[2 * q + hc, 24 * k : 24 * k + 24] = tile


def lat_order():
    at = iota((NLAT, 512), 1)
    lat = ((at // 8) % 16) * 28 + (at // 128) * 7 + at % 8
    return jnp.where((iota((NLAT, 512), 0) == lat) & (at % 8 < 7), 1.0, 0.0).astype(bf16)


def wave_table_kernel(number_ref, high_ref, low_ref):
    rows = 16
    half = NLON // 2
    row = iota((rows, MW), 0)
    slot = iota((rows, MW), 1)
    part = iota((rows, half), 0) % 2
    lon = iota((rows, half), 1)
    numbers = number_ref[...].astype(f32)
    coefs = [(-1.0) ** k / math.factorial(2 * k + 1) for k in range(6)]

    @pl.loop(0, 2 * MW // rows)
    def _(i):
        first = pl.multiple_of(i * rows, rows)
        mine = (row + first) // 2 == slot
        n = jnp.sum(jnp.where(mine, numbers, 0.0), axis=1, keepdims=True).astype(jnp.int32)
        phase = (n * lon + 256 * part) & (NLON - 1)
        turn_at = (jnp.abs(phase - half) - half // 2).astype(f32)
        y = turn_at * (2.0 * math.pi / NLON)
        y2 = y * y
        value = coefs[5]
        for k in range(4, -1, -1):
            value = value * y2 + coefs[k]
        value = value * y * FACTOR
        vh, vl = split(value)
        high_ref[pl.ds(first, rows), :half] = vh
        low_ref[pl.ds(first, rows), :half] = vl
        sign = (1 - 2 * (n & 1)).astype(f32)
        vh, vl = split(value * sign)
        high_ref[pl.ds(first, rows), half:] = vh
        low_ref[pl.ds(first, rows), half:] = vl


def synthesis_kernel(spec_ref, high_ref, low_ref, out_ref, lhs_ref):
    @pl.when(pl.program_id(0) == 0)
    def _():
        rows = spec_ref[:, :168].reshape(WAVES, GROUPS, 3, 8, 128)
        for c in range(3):
            s = rows[:, :, c].reshape(2 * MW, 128).T
            sh, sl = split(s)
            lhs_ref[128 * c : 128 * c + 128] = sh
            lhs_ref[384 + 128 * c : 512 + 128 * c] = sl

    both = mm(lhs_ref[...], high_ref[...])
    out = both[:384] + both[384:] + mm(lhs_ref[:384], low_ref[...])
    for w in range(2):
        for band in range(BANDS):
            for c in range(3):
                row = 128 * c + 8 * band
                at = TILE * (BANDS * w + band) + 7 * c
                out_ref[at : at + 7] = out[row : row + 7, 128 * w : 128 * w + 128]


def analysis_kernel(grid_ref, high_ref, low_ref, out_ref, acc_ref):
    i = pl.program_id(0)
    blank = jnp.zeros((1, 128), f32)
    tiles = []
    for c in range(3):
        parts = []
        for w in range(2):
            rows = []
            for band in range(BANDS):
                at = TILE * (BANDS * w + band) + 7 * c
                rows += [grid_ref[at : at + 7], blank]
            parts.append(jnp.concatenate(rows, axis=0))
        tiles.append(jnp.concatenate(parts, axis=1))
    gh, gl = split(jnp.concatenate(tiles, axis=0))
    both = mm_nt(high_ref[...], jnp.concatenate([gh, gl], axis=0))
    part = both[:, :384] + both[:, 384:] + mm_nt(low_ref[...], gh)

    @pl.when(i == 0)
    def _():
        acc_ref[...] = part

    @pl.when((i > 0) & (i < 3))
    def _():
        acc_ref[...] += part

    @pl.when(i == 3)
    def _():
        total = acc_ref[...] + part
        for c in range(3):
            rows = total[:, 128 * c : 128 * c + 128]
            out_ref[:, :, c] = rows.reshape(WAVES, GROUPS, 8, 128)


def legendre_adjoint_kernel(spec_ref, table_hbm, out_ref, acc_ref, table_ref, sem):
    copies = table_copies(table_hbm, table_ref, sem)
    order = lat_order()
    for hc in range(2):
        s = jnp.concatenate([spec_ref[2 * q + hc] for q in range(4)], axis=1)
        sh, sl = split(s)
        acc_ref[168 * hc : 168 * hc + 168] = mm_nt(sh, order) + mm_nt(sl, order)
    slot = (iota((48, NLAT), 0) % 8) // 2
    x = []
    for g in range(GROUPS):
        copies[g].wait()
        rows = [acc_ref[168 * hc + 24 * g : 168 * hc + 24 * g + 24] for hc in range(2)]
        mine = jnp.concatenate(rows, axis=0)
        acc = None
        for m4 in range(4):
            xh, xl = split(jnp.where(slot == m4, mine, 0.0))
            th, tl = split(table_ref[4 * g + m4])
            both = mm(jnp.concatenate([xh, xl], axis=0), th)
            part = both[:48] + both[48:] + mm(xh, tl)
            acc = part if acc is None else acc + part
        x.append(acc)
    x.append(jnp.zeros((48, NT), f32))
    for half in range(2):
        for c in range(6):
            got = [v[8 * c : 8 * c + 8, 128 * half : 128 * half + 128] for v in x]
            for s, z in enumerate(turn(got, 1, 16)):
                out_ref[8 * half + s, 8 * c : 8 * c + 8] = z


def unmix_kernel(modes_ref, control_ref, scale_ref, root_ref, out_ref):
    root = doubled_root(root_ref[...])
    rh, rl = split(root)
    tiles = turn([modes_ref[:, j] for j in range(4)], 1, 2)
    for m4 in range(4):
        y = tiles[m4].reshape(2 * CH, 128).T[: 16 * GROUPS]
        s = jnp.concatenate([scale_ref[4 * g + m4] for g in range(GROUPS)], axis=0)
        yh, yl = split(y * s)
        z = mm_nt(yh, rh) + mm_nt(yl, rh) + mm_nt(yh, rl)
        for g in range(GROUPS):
            m = 4 * g + m4
            out_ref[m] = control_ref[m] + z[16 * g : 16 * g + 16]


def sums_kernel(obs_ref, out_ref, acc_ref):
    i = pl.program_id(0)
    part = None
    for half in range(2):

        def line(k):
            at = 168 + 16 * k + 8 * half
            rows = obs_ref[0, at : at + 8]
            return jnp.concatenate([rows[s : s + 1] for s in range(8)], axis=1)

        column = line(0).astype(jnp.int32)
        level = line(1).astype(jnp.int32)
        lat = column // 128
        lon = column % 128
        q = sum((lat >= 7 * k).astype(jnp.int32) for k in range(1, 4))
        row = q * 64 + level * 8 + (lat - 7 * q)
        rows = jnp.where(iota((256, 1024), 0) == row, 1.0, 0.0).astype(bf16)
        cols = jnp.where(iota((128, 1024), 0) == lon, 1.0, 0.0).astype(bf16)
        values = []
        for k in range(2, 5):
            for v in split(line(k)):
                values.append(cols * v)
        new = mm_nt(rows, jnp.concatenate(values, axis=0))
        part = new if part is None else part + new

    @pl.when(i == 0)
    def _():
        acc_ref[...] = part

    @pl.when(i > 0)
    def _():
        acc_ref[...] += part

    @pl.when(i == WAVES - 1)
    def _():
        for k in range(3):
            first = acc_ref[:, 256 * k : 256 * k + 128]
            out_ref[k] = first + acc_ref[:, 256 * k + 128 : 256 * k + 256]


def grid_kernel(
    grid_ref, courant_ref, sums_ref, lidar_ref, aod_ref, state_ref, adjoint_ref, flow_ref, hold_ref
):
    for h in range(12):
        rows = [courant_ref[min(t, 6), 8 * h : 8 * h + 8] for t in range(8)]
        for j, z in enumerate(turn(rows, 0, 1)):
            flow_ref[8 * h + j] = z

    def tile_rows(l, b2, hc, c):
        return pl.ds(TILE * (BANDS * hc + 2 * l + b2) + 7 * c, 7)

    blank = jnp.zeros((1, 128), f32)
    chains = [(b2, hc, c) for b2 in range(2) for hc in range(2) for c in range(3)]
    lidar_sum = [None] * LEV
    aod_sum = None
    for b2, hc, c in chains:
        bin_at = b2 * 6 + hc * 3 + c
        x = [
            jnp.concatenate([grid_ref[tile_rows(l, b2, hc, c)], blank], axis=0)
            for l in range(LEV)
        ]
        flow = [flow_ref[BINS * l + bin_at] for l in range(LEV)]
        for step in range(STEPS):
            out = [flow[l] * x[l] for l in range(LEV)]
            x = [x[l] - out[l] if l == 0 else x[l] - out[l] + out[l - 1] for l in range(LEV)]
        coef = lidar_ref[bin_at]
        for l in range(LEV):
            hold_ref[BINS * l + bin_at] = x[l]
            lidar_sum[l] = x[l] * coef if lidar_sum[l] is None else lidar_sum[l] + x[l] * coef
            term = x[l] * aod_ref[BINS * l + bin_at]
            aod_sum = term if aod_sum is None else aod_sum + term

    for h in range(12):
        rows = turn([hold_ref[8 * h + j] for j in range(8)], 0, 1)
        for t in range(7):
            state_ref[t, 8 * h : 8 * h + 8] = rows[t]

    weight = [sums_ref[0, 8 * l : 8 * l + 8] for l in range(LEV)]
    lidar = [weight[l] * lidar_sum[l] - sums_ref[1, 8 * l : 8 * l + 8] for l in range(LEV)]
    aod = sum(weight[1:], weight[0]) * aod_sum
    for l in range(LEV):
        aod = aod - sums_ref[2, 8 * l : 8 * l + 8]
    for b2, hc, c in chains:
        bin_at = b2 * 6 + hc * 3 + c
        coef = lidar_ref[bin_at]
        flow = [flow_ref[BINS * l + bin_at] for l in range(LEV)]
        a = [lidar[l] * coef + aod * aod_ref[BINS * l + bin_at] for l in range(LEV)]
        for step in range(STEPS):
            a = [
                a[l] + flow[l] * ((a[l + 1] - a[l]) if l + 1 < LEV else -a[l]) for l in range(LEV)
            ]
        for l in range(LEV):
            adjoint_ref[tile_rows(l, b2, hc, c)] = a[l][:7]


def shape(*lengths, kind=f32):
    return jax.ShapeDtypeStruct(lengths, kind)


def whole(*lengths):
    return pl.BlockSpec(lengths, lambda *_: (0,) * len(lengths))


def in_hbm(x):
    return pltpu.with_memory_space_constraint(x, pltpu.HBM)


def cost(flops, size):
    return pl.CostEstimate(flops=flops, bytes_accessed=size, transcendentals=0)


def exchange(tiles, axis):
    return lax.all_to_all(tiles, axis, split_axis=0, concat_axis=0, tiled=True)


def exchange_tiles(tiles):
    rows = tiles.reshape(DEVICES, 1, TILE * 128)
    return exchange(rows, ("wave", "band")).reshape(DEVICES * TILE, 128)


def body(
    control,
    spectral_scale,
    vertical_root,
    legendre,
    zonal_number,
    courant,
    lidar_coef,
    aod_coef,
    obs_count,
    obs_column,
    obs_level,
    lidar_obs,
    aod_obs,
    obs_weight,
):
    control = jnp.swapaxes(control, 0, 1)
    scale = jnp.swapaxes(spectral_scale, 0, 1)
    hbm = pl.BlockSpec(memory_space=pltpu.HBM)
    modes = pl.pallas_call(
        mix_kernel,
        in_specs=[hbm] * 9,
        out_specs=whole(BANDS, 88, 128),
        out_shape=shape(BANDS, 88, 128),
        scratch_shapes=[
            pltpu.VMEM((28, 16, 192), f32),
            pltpu.VMEM((28, 16, 192), f32),
            pltpu.VMEM((CH, CH), f32),
            pltpu.VMEM((2, DEVICES, SLOT), jnp.int32),
            pltpu.VMEM((3, DEVICES, SLOT), f32),
            pltpu.VMEM((1, DEVICES), jnp.int32),
            pltpu.VMEM((5, DEVICES, SLOT), f32),
            pltpu.SemaphoreType.DMA((9,)),
        ],
        compiler_params=params(),
        cost_estimate=cost(6 * 448 * 192 * 192, 1 << 20),
        name="mix",
    )(
        *(
            in_hbm(x)
            for x in (
                control,
                scale,
                vertical_root,
                obs_column,
                obs_level,
                lidar_obs,
                aod_obs,
                obs_weight,
                obs_count,
            )
        )
    )
    modes = exchange(modes, "band")

    high, low = pl.pallas_call(
        wave_table_kernel,
        out_shape=(shape(2 * MW, NLON, kind=bf16), shape(2 * MW, NLON, kind=bf16)),
        compiler_params=params(),
        cost_estimate=cost(20 * 448 * 1024, 2 << 20),
        name="wave_table",
    )(zonal_number.reshape(1, MW))

    legendre_cost = cost(6 * 28 * 448 * 256 * 48, 14 << 20)
    in_order = params(dimension_semantics=("arbitrary",))
    table_scratch = [pltpu.VMEM((28, NLAT, NT), f32), pltpu.SemaphoreType.DMA((GROUPS,))]
    spec = pl.pallas_call(
        legendre_kernel,
        in_specs=[whole(BANDS, 88, 128), hbm],
        out_specs=whole(WAVES, 248, 128),
        out_shape=shape(WAVES, 248, 128),
        scratch_shapes=[
            pltpu.VMEM((GROUPS, 48, NT), f32),
            pltpu.VMEM((GROUPS, 48, NLAT), f32),
            *table_scratch,
        ],
        compiler_params=params(),
        cost_estimate=legendre_cost,
        name="legendre",
    )(modes, in_hbm(legendre))
    spec = exchange(spec, "wave")
    sums = pl.pallas_call(
        sums_kernel,
        grid=(WAVES,),
        in_specs=[pl.BlockSpec((1, 248, 128), lambda i: (i, 0, 0))],
        out_specs=whole(3, 256, 128),
        out_shape=shape(3, 256, 128),
        scratch_shapes=[pltpu.VMEM((256, 768), f32)],
        compiler_params=in_order,
        cost_estimate=cost(2 * 16384 * 256 * 768, 1 << 20),
        name="sums",
    )(spec)

    wave_spec = pl.BlockSpec((2 * MW, 256), lambda i: (0, i))
    tile_spec = pl.BlockSpec((2 * BANDS * TILE, 128), lambda i: (i, 0))
    tiles = shape(DEVICES * TILE, 128)
    wave_cost = cost(6 * 384 * 448 * 1024, 4 << 20)
    grid = pl.pallas_call(
        synthesis_kernel,
        grid=(4,),
        in_specs=[whole(WAVES, 248, 128), wave_spec, wave_spec],
        out_specs=tile_spec,
        out_shape=tiles,
        scratch_shapes=[pltpu.VMEM((768, 2 * MW), bf16)],
        compiler_params=in_order,
        cost_estimate=wave_cost,
        name="synthesis",
    )(spec, high, low)
    grid = exchange_tiles(grid)

    field = pl.BlockSpec((7, CH, 128), lambda q: (q, 0, 0))
    scalars = pl.BlockSpec(memory_space=pltpu.SMEM)
    state, adjoint = pl.pallas_call(
        grid_kernel,
        grid=(4,),
        in_specs=[tile_spec, field, pl.BlockSpec((3, 64, 128), lambda q: (0, q, 0)), scalars, scalars],
        out_specs=(field, tile_spec),
        out_shape=(shape(28, CH, 128), tiles),
        scratch_shapes=[pltpu.VMEM((CH, 8, 128), f32), pltpu.VMEM((CH, 8, 128), f32)],
        compiler_params=in_order,
        cost_estimate=cost(40 * 28 * 96 * 128, 6 << 20),
        name="grid_steps",
    )(grid, in_hbm(courant), in_hbm(sums), lidar_coef, aod_coef)
    adjoint = exchange_tiles(adjoint)

    spec = pl.pallas_call(
        analysis_kernel,
        grid=(4,),
        in_specs=[tile_spec, wave_spec, wave_spec],
        out_specs=whole(WAVES, GROUPS, 3, 8, 128),
        out_shape=shape(WAVES, GROUPS, 3, 8, 128),
        scratch_shapes=[pltpu.VMEM((2 * MW, 384), f32)],
        compiler_params=in_order,
        cost_estimate=wave_cost,
        name="analysis",
    )(adjoint, high, low)
    spec = exchange(spec.reshape(WAVES, 24 * GROUPS, 128), "wave")

    modes = pl.pallas_call(
        legendre_adjoint_kernel,
        in_specs=[whole(WAVES, 168, 128), hbm],
        out_specs=whole(BANDS, 48, 128),
        out_shape=shape(BANDS, 48, 128),
        scratch_shapes=[pltpu.VMEM((336, NLAT), f32), *table_scratch],
        compiler_params=params(),
        cost_estimate=legendre_cost,
        name="legendre_adjoint",
    )(spec, in_hbm(legendre))
    modes = exchange(modes, "band").reshape(24, 4, 8, 128)

    gradient = pl.pallas_call(
        unmix_kernel,
        out_shape=shape(28, 16, 192),
        compiler_params=params(),
        cost_estimate=cost(6 * 448 * 192 * 192, 1 << 20),
        name="unmix",
    )(modes, control, scale, vertical_root)
    return jnp.swapaxes(gradient, 0, 1), state


def solution(mesh):
    both = ("wave", "band")
    placed = (
        P("band", "wave", None),
        P("band", "wave", None),
        P(),
        P("wave", None, None),
        P(),
        P("band", None, "wave"),
        P(),
        P(),
        P(both, None),
        P(both, None),
        P(both, None),
        P(both, None),
        P(both, None),
        P(both, None),
    )
    return jax.shard_map(
        body,
        mesh=mesh,
        in_specs=placed,
        out_specs=(P("band", "wave", None), P("band", None, "wave")),
        check_vma=False,
    )
```

```python
import math

import jax
import jax.numpy as jnp
from jax import lax
from jax.experimental import pallas as pl
from jax.experimental.pallas import tpu as pltpu
from jax.sharding import PartitionSpec as P

MW = 224
LEV = 8
BINS = 12
CH = 96
STEPS = 4
WAVES = 8
BANDS = 16
DEVICES = 128
SLOT = 128
GROUPS = 7
NLON = 1024
NLAT = 448
NT = 256
TILE = 21
HEAD = 4
FACTOR = MW ** (-0.5)
f32 = jnp.float32
bf16 = jnp.bfloat16
highest = lax.Precision.HIGHEST
LIMIT = 24 << 20


def params(**kw):
    return pltpu.CompilerParams(vmem_limit_bytes=LIMIT, **kw)


def split(x):
    hi = x.astype(bf16)
    return hi, (x - hi.astype(f32)).astype(bf16)


def mm(a, b):
    return lax.dot_general(a, b, (((1,), (0,)), ((), ())), preferred_element_type=f32)


def mm_nt(a, b):
    return lax.dot_general(a, b, (((1,), (1,)), ((), ())), preferred_element_type=f32)


def iota(shape, dim):
    return lax.broadcasted_iota(jnp.int32, shape, dim)


def turn(parts, axis, width):
    n = len(parts)
    size = parts[0].shape[axis]
    at = iota(parts[0].shape, axis)
    step = n // 2
    while step:
        keep = (at // (step * width)) % 2 == 0
        new = list(parts)
        for i in range(n):
            if (i // step) % 2 == 0:
                a, b = parts[i], parts[i + step]
                new[i] = jnp.where(keep, a, pltpu.roll(b, step * width, axis))
                new[i + step] = jnp.where(keep, pltpu.roll(a, size - step * width, axis), b)
        parts = new
        step //= 2
    return parts


def doubled_root(root):
    rows = (iota((2 * CH, CH), 0) // 2 == iota((2 * CH, CH), 1)).astype(f32)
    cols = (iota((CH, 2 * CH), 1) // 2 == iota((CH, 2 * CH), 0)).astype(f32)
    wide = jnp.dot(rows, root, precision=highest, preferred_element_type=f32)
    wide = jnp.dot(wide, cols, precision=highest, preferred_element_type=f32)
    same = iota((2 * CH, 2 * CH), 0) % 2 == iota((2 * CH, 2 * CH), 1) % 2
    return jnp.where(same, wide, 0.0)


def mix_kernel(
    control_hbm,
    scale_hbm,
    root_hbm,
    column_hbm,
    level_hbm,
    lidar_hbm,
    aod_hbm,
    weight_hbm,
    count_hbm,
    out_ref,
    control_ref,
    scale_ref,
    root_ref,
    index_ref,
    value_ref,
    count_ref,
    obs_ref,
    sem,
):
    copies = [
        pltpu.make_async_copy(source, target, sem.at[k])
        for k, (source, target) in enumerate(
            (
                (root_hbm, root_ref),
                (control_hbm, control_ref),
                (scale_hbm, scale_ref),
                (column_hbm, index_ref.at[0]),
                (level_hbm, index_ref.at[1]),
                (lidar_hbm, value_ref.at[0]),
                (aod_hbm, value_ref.at[1]),
                (weight_hbm, value_ref.at[2]),
                (count_hbm, count_ref),
            )
        )
    ]
    for copy in copies[3:] + copies[:3]:
        copy.start()
    for copy in copies[3:]:
        copy.wait()
    counts = jnp.broadcast_to(count_ref[...].astype(f32), (DEVICES, DEVICES)).T
    live = iota((DEVICES, SLOT), 1).astype(f32) < counts
    weight = jnp.where(live, value_ref[2], 0.0)
    obs_ref[0] = index_ref[0].astype(f32)
    obs_ref[1] = index_ref[1].astype(f32)
    obs_ref[2] = weight
    obs_ref[3] = weight * value_ref[0]
    obs_ref[4] = weight * value_ref[1]
    for band in range(BANDS):
        for k in range(5):
            rows = obs_ref[k, pl.ds(band, WAVES, stride=BANDS), :]
            out_ref[band, 48 + 8 * k : 56 + 8 * k] = rows

    for copy in copies[:3]:
        copy.wait()
    root = doubled_root(root_ref[...])
    rh, rl = split(root)
    tiles = []
    for m4 in range(4):
        x = jnp.concatenate([control_ref[4 * g + m4] for g in range(GROUPS)], axis=0)
        s = jnp.concatenate([scale_ref[4 * g + m4] for g in range(GROUPS)], axis=0)
        xh, xl = split(x)
        y = (mm(xh, rh) + mm(xl, rh) + mm(xh, rl)) * s
        y = jnp.concatenate([y, jnp.zeros((16, 2 * CH), f32)], axis=0)
        tiles.append(y.T.reshape(24, 8, 128))
    for j, z in enumerate(turn(tiles, 1, 2)):
        for h in range(24):
            c = 4 * h + j
            out_ref[c // 6, 8 * (c % 6) : 8 * (c % 6) + 8] = z[h]


def head_kernel(table_hbm, out_ref, sem):
    copy = pltpu.make_async_copy(table_hbm.at[pl.ds(0, HEAD)], out_ref, sem)
    copy.start()
    copy.wait()


def table_copies(table_hbm, table_ref, sem):
    copies = {}
    first = HEAD
    while first < 4 * GROUPS:
        count = 4 - first % 4
        source = table_hbm.at[pl.ds(first, count)]
        target = table_ref.at[pl.ds(first - HEAD, count)]
        copies[first] = pltpu.make_async_copy(source, target, sem.at[len(copies)])
        first += count
    for copy in copies.values():
        copy.start()
    return copies


def table_slot(m, copies, head_ref, table_ref):
    if m < HEAD:
        return head_ref[m]
    if m in copies:
        copies[m].wait()
    return table_ref[m - HEAD]


def legendre_kernel(modes_ref, head_ref, table_hbm, out_ref, x_ref, acc_ref, table_ref, sem):
    copies = table_copies(table_hbm, table_ref, sem)
    for half in range(2):
        for c in range(6):
            got = [modes_ref[8 * half + s, 8 * c : 8 * c + 8] for s in range(8)]
            for g, z in enumerate(turn(got, 1, 16)):
                if g < GROUPS:
                    x_ref[g, 8 * c : 8 * c + 8, 128 * half : 128 * half + 128] = z
    for k in range(5):
        for half in range(2):
            got = [modes_ref[8 * half + s, 48 + 8 * k : 56 + 8 * k] for s in range(8)]
            at = 168 + 16 * k + 8 * half
            for w, z in enumerate(turn(got, 0, 1)):
                out_ref[w, at : at + 8] = z

    slot = (iota((48, NT), 0) % 8) // 2
    order = lat_order()
    for g in range(GROUPS):
        x = x_ref[g]
        acc = None
        for m4 in range(4):
            xh, xl = split(jnp.where(slot == m4, x, 0.0))
            both = jnp.concatenate(split(table_slot(4 * g + m4, copies, head_ref, table_ref)), axis=0)
            both = mm_nt(jnp.concatenate([xh, xl], axis=0), both)
            part = both[:48, :NLAT] + (both[48:, :NLAT] + both[:48, NLAT:])
            acc = part if acc is None else acc + part
        acc_ref[g] = acc
        for first, last in ((0, 5), (5, 7)):
            if g + 1 == last:
                rows = 48 * (last - first)
                part = acc_ref[first:last].reshape(rows, NLAT)
                both = mm(jnp.concatenate(split(part), axis=0), order)
                out = both[:rows] + both[rows:]
                for k in range(first, last):
                    for q in range(4):
                        for hc in range(2):
                            at = 48 * (k - first) + 24 * hc
                            tile = out[at : at + 24, 128 * q : 128 * q + 128]
                            out_ref[2 * q + hc, 24 * k : 24 * k + 24] = tile


def lat_order():
    at = iota((NLAT, 512), 1)
    lat = ((at // 8) % 16) * 28 + (at // 128) * 7 + at % 8
    return jnp.where((iota((NLAT, 512), 0) == lat) & (at % 8 < 7), 1.0, 0.0).astype(bf16)


def wave_table_kernel(number_ref, high_ref, low_ref):
    rows = 16
    half = NLON // 2
    row = iota((rows, MW), 0)
    slot = iota((rows, MW), 1)
    part = iota((rows, half), 0) % 2
    lon = iota((rows, half), 1)
    numbers = number_ref[...].astype(f32)
    coefs = [(-1.0) ** k / math.factorial(2 * k + 1) for k in range(6)]

    @pl.loop(0, 2 * MW // rows)
    def _(i):
        first = pl.multiple_of(i * rows, rows)
        mine = (row + first) // 2 == slot
        n = jnp.sum(jnp.where(mine, numbers, 0.0), axis=1, keepdims=True).astype(jnp.int32)
        phase = (n * lon + 256 * part) & (NLON - 1)
        turn_at = (jnp.abs(phase - half) - half // 2).astype(f32)
        y = turn_at * (2.0 * math.pi / NLON)
        y2 = y * y
        value = coefs[5]
        for k in range(4, -1, -1):
            value = value * y2 + coefs[k]
        value = value * y * FACTOR
        vh, vl = split(value)
        high_ref[pl.ds(first, rows), :half] = vh
        low_ref[pl.ds(first, rows), :half] = vl
        sign = (1 - 2 * (n & 1)).astype(f32)
        vh, vl = split(value * sign)
        high_ref[pl.ds(first, rows), half:] = vh
        low_ref[pl.ds(first, rows), half:] = vl


def synthesis_kernel(spec_ref, high_ref, low_ref, out_ref, lhs_ref):
    rows = spec_ref[:, :168].reshape(WAVES, GROUPS, 3, 8, 128)
    for c in range(3):
        high, low = split(rows[:, :, c].reshape(2 * MW, 128).T)
        lhs_ref[128 * c : 128 * c + 128] = high
        lhs_ref[384 + 128 * c : 512 + 128 * c] = low
    for i in range(4):
        lon = pl.ds(256 * i, 256)
        both = mm(lhs_ref[...], high_ref[:, lon])
        out = both[:384] + both[384:] + mm(lhs_ref[:384], low_ref[:, lon])
        for w in range(2):
            for band in range(BANDS):
                for c in range(3):
                    row = 128 * c + 8 * band
                    at = TILE * (BANDS * (2 * i + w) + band) + 7 * c
                    out_ref[at : at + 7] = out[row : row + 7, 128 * w : 128 * w + 128]


def analysis_kernel(grid_ref, high_ref, low_ref, out_ref):
    blank = jnp.zeros((1, 128), f32)
    total = None
    for i in range(4):
        tiles = []
        for c in range(3):
            parts = []
            for w in range(2):
                rows = []
                for band in range(BANDS):
                    at = TILE * (BANDS * (2 * i + w) + band) + 7 * c
                    rows += [grid_ref[at : at + 7], blank]
                parts.append(jnp.concatenate(rows, axis=0))
            tiles.append(jnp.concatenate(parts, axis=1))
        gh, gl = split(jnp.concatenate(tiles, axis=0))
        lon = pl.ds(256 * i, 256)
        both = mm_nt(high_ref[:, lon], jnp.concatenate([gh, gl], axis=0))
        part = both[:, :384] + both[:, 384:] + mm_nt(low_ref[:, lon], gh)
        total = part if total is None else total + part
    for c in range(3):
        rows = total[:, 128 * c : 128 * c + 128]
        out_ref[:, :, c] = rows.reshape(WAVES, GROUPS, 8, 128)


def legendre_adjoint_kernel(spec_ref, head_ref, table_hbm, out_ref, acc_ref, table_ref, sem):
    copies = table_copies(table_hbm, table_ref, sem)
    order = lat_order()
    for hc in range(2):
        s = jnp.concatenate([spec_ref[2 * q + hc] for q in range(4)], axis=1)
        sh, sl = split(s)
        acc_ref[168 * hc : 168 * hc + 168] = mm_nt(sh, order) + mm_nt(sl, order)
    slot = (iota((48, NLAT), 0) % 8) // 2
    x = []
    for g in range(GROUPS):
        rows = [acc_ref[168 * hc + 24 * g : 168 * hc + 24 * g + 24] for hc in range(2)]
        mine = jnp.concatenate(rows, axis=0)
        acc = None
        for m4 in range(4):
            xh, xl = split(jnp.where(slot == m4, mine, 0.0))
            th, tl = split(table_slot(4 * g + m4, copies, head_ref, table_ref))
            both = mm(jnp.concatenate([xh, xl], axis=0), th)
            part = both[:48] + both[48:] + mm(xh, tl)
            acc = part if acc is None else acc + part
        x.append(acc)
    x.append(jnp.zeros((48, NT), f32))
    for half in range(2):
        for c in range(6):
            got = [v[8 * c : 8 * c + 8, 128 * half : 128 * half + 128] for v in x]
            for s, z in enumerate(turn(got, 1, 16)):
                out_ref[8 * half + s, 8 * c : 8 * c + 8] = z


def unmix_kernel(modes_ref, control_ref, scale_ref, root_ref, out_ref):
    root = doubled_root(root_ref[...])
    rh, rl = split(root)
    tiles = turn([modes_ref[:, j] for j in range(4)], 1, 2)
    for m4 in range(4):
        y = tiles[m4].reshape(2 * CH, 128).T[: 16 * GROUPS]
        s = jnp.concatenate([scale_ref[4 * g + m4] for g in range(GROUPS)], axis=0)
        yh, yl = split(y * s)
        z = mm_nt(yh, rh) + mm_nt(yl, rh) + mm_nt(yh, rl)
        for g in range(GROUPS):
            m = 4 * g + m4
            out_ref[m] = control_ref[m] + z[16 * g : 16 * g + 16]


def sums_kernel(obs_ref, out_ref, acc_ref):
    i = pl.program_id(0)
    part = None
    for half in range(2):

        def line(k):
            at = 168 + 16 * k + 8 * half
            rows = obs_ref[0, at : at + 8]
            return jnp.concatenate([rows[s : s + 1] for s in range(8)], axis=1)

        column = line(0).astype(jnp.int32)
        level = line(1).astype(jnp.int32)
        lat = column // 128
        lon = column % 128
        q = sum((lat >= 7 * k).astype(jnp.int32) for k in range(1, 4))
        row = q * 64 + level * 8 + (lat - 7 * q)
        rows = jnp.where(iota((256, 1024), 0) == row, 1.0, 0.0).astype(bf16)
        cols = jnp.where(iota((128, 1024), 0) == lon, 1.0, 0.0).astype(bf16)
        values = []
        for k in range(2, 5):
            for v in split(line(k)):
                values.append(cols * v)
        new = mm_nt(rows, jnp.concatenate(values, axis=0))
        part = new if part is None else part + new

    @pl.when(i == 0)
    def _():
        acc_ref[...] = part

    @pl.when(i > 0)
    def _():
        acc_ref[...] += part

    @pl.when(i == WAVES - 1)
    def _():
        for k in range(3):
            first = acc_ref[:, 256 * k : 256 * k + 128]
            out_ref[k] = first + acc_ref[:, 256 * k + 128 : 256 * k + 256]


def flow_kernel(courant_ref, out_ref):
    for h in range(12):
        rows = [courant_ref[min(t, 6), 8 * h : 8 * h + 8] for t in range(8)]
        for j, z in enumerate(turn(rows, 0, 1)):
            out_ref[8 * h + j] = z


def state_kernel(hold_ref, out_ref):
    for h in range(12):
        rows = turn([hold_ref[8 * h + j] for j in range(8)], 0, 1)
        for t in range(7):
            out_ref[t, 8 * h : 8 * h + 8] = rows[t]


def grid_kernel(grid_ref, flow_ref, sums_ref, lidar_ref, aod_ref, hold_ref, adjoint_ref):
    def tile_rows(l, b2, hc, c):
        return pl.ds(TILE * (BANDS * hc + 2 * l + b2) + 7 * c, 7)

    blank = jnp.zeros((1, 128), f32)
    chains = [(b2, hc, c) for b2 in range(2) for hc in range(2) for c in range(3)]
    lidar_sum = [None] * LEV
    aod_sum = None
    for b2, hc, c in chains:
        bin_at = b2 * 6 + hc * 3 + c
        x = [
            jnp.concatenate([grid_ref[tile_rows(l, b2, hc, c)], blank], axis=0)
            for l in range(LEV)
        ]
        flow = [flow_ref[BINS * l + bin_at] for l in range(LEV)]
        for step in range(STEPS):
            out = [flow[l] * x[l] for l in range(LEV)]
            x = [x[l] - out[l] if l == 0 else x[l] - out[l] + out[l - 1] for l in range(LEV)]
        coef = lidar_ref[bin_at]
        for l in range(LEV):
            hold_ref[BINS * l + bin_at] = x[l]
            lidar_sum[l] = x[l] * coef if lidar_sum[l] is None else lidar_sum[l] + x[l] * coef
            term = x[l] * aod_ref[BINS * l + bin_at]
            aod_sum = term if aod_sum is None else aod_sum + term

    weight = [sums_ref[0, 8 * l : 8 * l + 8] for l in range(LEV)]
    lidar = [weight[l] * lidar_sum[l] - sums_ref[1, 8 * l : 8 * l + 8] for l in range(LEV)]
    aod = sum(weight[1:], weight[0]) * aod_sum
    for l in range(LEV):
        aod = aod - sums_ref[2, 8 * l : 8 * l + 8]
    for b2, hc, c in chains:
        bin_at = b2 * 6 + hc * 3 + c
        coef = lidar_ref[bin_at]
        flow = [flow_ref[BINS * l + bin_at] for l in range(LEV)]
        a = [lidar[l] * coef + aod * aod_ref[BINS * l + bin_at] for l in range(LEV)]
        for step in range(STEPS):
            a = [
                a[l] + flow[l] * ((a[l + 1] - a[l]) if l + 1 < LEV else -a[l]) for l in range(LEV)
            ]
        for l in range(LEV):
            adjoint_ref[tile_rows(l, b2, hc, c)] = a[l][:7]


def shape(*lengths, kind=f32):
    return jax.ShapeDtypeStruct(lengths, kind)


def whole(*lengths):
    return pl.BlockSpec(lengths, lambda *_: (0,) * len(lengths))


def in_hbm(x):
    return pltpu.with_memory_space_constraint(x, pltpu.HBM)


def cost(flops, size):
    return pl.CostEstimate(flops=flops, bytes_accessed=size, transcendentals=0)


def exchange(tiles, axis):
    return lax.all_to_all(tiles, axis, split_axis=0, concat_axis=0, tiled=True)


def exchange_tiles(tiles):
    rows = tiles.reshape(DEVICES, 1, TILE * 128)
    return exchange(rows, ("wave", "band")).reshape(DEVICES * TILE, 128)


def body(
    control,
    spectral_scale,
    vertical_root,
    legendre,
    zonal_number,
    courant,
    lidar_coef,
    aod_coef,
    obs_count,
    obs_column,
    obs_level,
    lidar_obs,
    aod_obs,
    obs_weight,
):
    control = jnp.swapaxes(control, 0, 1)
    scale = jnp.swapaxes(spectral_scale, 0, 1)
    hbm = pl.BlockSpec(memory_space=pltpu.HBM)
    modes = pl.pallas_call(
        mix_kernel,
        in_specs=[hbm] * 9,
        out_specs=whole(BANDS, 88, 128),
        out_shape=shape(BANDS, 88, 128),
        scratch_shapes=[
            pltpu.VMEM((28, 16, 192), f32),
            pltpu.VMEM((28, 16, 192), f32),
            pltpu.VMEM((CH, CH), f32),
            pltpu.VMEM((2, DEVICES, SLOT), jnp.int32),
            pltpu.VMEM((3, DEVICES, SLOT), f32),
            pltpu.VMEM((1, DEVICES), jnp.int32),
            pltpu.VMEM((5, DEVICES, SLOT), f32),
            pltpu.SemaphoreType.DMA((9,)),
        ],
        compiler_params=params(),
        cost_estimate=cost(6 * 448 * 192 * 192, 1 << 20),
        name="mix",
    )(
        *(
            in_hbm(x)
            for x in (
                control,
                scale,
                vertical_root,
                obs_column,
                obs_level,
                lidar_obs,
                aod_obs,
                obs_weight,
                obs_count,
            )
        )
    )
    modes = exchange(modes, "band")

    high, low = pl.pallas_call(
        wave_table_kernel,
        out_shape=(shape(2 * MW, NLON, kind=bf16), shape(2 * MW, NLON, kind=bf16)),
        compiler_params=params(),
        cost_estimate=cost(20 * 448 * 1024, 2 << 20),
        name="wave_table",
    )(zonal_number.reshape(1, MW))


    def head(table):
        return pl.pallas_call(
            head_kernel,
            in_specs=[hbm],
            out_specs=whole(HEAD, NLAT, NT),
            out_shape=shape(HEAD, NLAT, NT),
            scratch_shapes=[pltpu.SemaphoreType.DMA(())],
            compiler_params=params(),
            cost_estimate=cost(0, 8 * HEAD * NLAT * NT),
            name="head",
        )(in_hbm(table))

    legendre_cost = cost(6 * 28 * 448 * 256 * 48, 14 << 20)
    in_order = params(dimension_semantics=("arbitrary",))
    table_scratch = [pltpu.VMEM((28 - HEAD, NLAT, NT), f32), pltpu.SemaphoreType.DMA((GROUPS,))]
    spec = pl.pallas_call(
        legendre_kernel,
        in_specs=[whole(BANDS, 88, 128), whole(HEAD, NLAT, NT), hbm],
        out_specs=whole(WAVES, 248, 128),
        out_shape=shape(WAVES, 248, 128),
        scratch_shapes=[
            pltpu.VMEM((GROUPS, 48, NT), f32),
            pltpu.VMEM((GROUPS, 48, NLAT), f32),
            *table_scratch,
        ],
        compiler_params=params(),
        cost_estimate=legendre_cost,
        name="legendre",
    )(modes, head(legendre), in_hbm(legendre))
    spec = exchange(spec, "wave")
    sums = pl.pallas_call(
        sums_kernel,
        grid=(WAVES,),
        in_specs=[pl.BlockSpec((1, 248, 128), lambda i: (i, 0, 0))],
        out_specs=whole(3, 256, 128),
        out_shape=shape(3, 256, 128),
        scratch_shapes=[pltpu.VMEM((256, 768), f32)],
        compiler_params=in_order,
        cost_estimate=cost(2 * 16384 * 256 * 768, 1 << 20),
        name="sums",
    )(spec)

    tile_spec = pl.BlockSpec((2 * BANDS * TILE, 128), lambda i: (i, 0))
    tiles = shape(DEVICES * TILE, 128)
    wave_cost = cost(6 * 384 * 448 * 1024, 4 << 20)
    grid = pl.pallas_call(
        synthesis_kernel,
        out_shape=tiles,
        scratch_shapes=[pltpu.VMEM((768, 2 * MW), bf16)],
        compiler_params=params(),
        cost_estimate=wave_cost,
        name="synthesis",
    )(spec, high, low)
    grid = exchange_tiles(grid)

    field = pl.BlockSpec((7, CH, 128), lambda q: (q, 0, 0))
    scalars = pl.BlockSpec(memory_space=pltpu.SMEM)
    turned = pl.BlockSpec((CH, 8, 128), lambda q: (q, 0, 0))
    flow = pl.pallas_call(
        flow_kernel,
        grid=(4,),
        in_specs=[field],
        out_specs=turned,
        out_shape=shape(4 * CH, 8, 128),
        compiler_params=in_order,
        cost_estimate=cost(6 * 28 * 96 * 128, 3 << 20),
        name="flow",
    )(in_hbm(courant))
    hold, adjoint = pl.pallas_call(
        grid_kernel,
        grid=(4,),
        in_specs=[
            tile_spec,
            turned,
            pl.BlockSpec((3, 64, 128), lambda q: (0, q, 0)),
            scalars,
            scalars,
        ],
        out_specs=(turned, tile_spec),
        out_shape=(shape(4 * CH, 8, 128), tiles),
        compiler_params=in_order,
        cost_estimate=cost(40 * 28 * 96 * 128, 6 << 20),
        name="grid_steps",
    )(grid, flow, in_hbm(sums), lidar_coef, aod_coef)
    state = pl.pallas_call(
        state_kernel,
        grid=(4,),
        in_specs=[turned],
        out_specs=field,
        out_shape=shape(28, CH, 128),
        compiler_params=in_order,
        cost_estimate=cost(6 * 28 * 96 * 128, 3 << 20),
        name="state",
    )(hold)
    adjoint = exchange_tiles(adjoint)

    spec = pl.pallas_call(
        analysis_kernel,
        out_shape=shape(WAVES, GROUPS, 3, 8, 128),
        compiler_params=params(),
        cost_estimate=wave_cost,
        name="analysis",
    )(adjoint, high, low)
    again, spec = lax.optimization_barrier((legendre, spec))
    spec = exchange(spec.reshape(WAVES, 24 * GROUPS, 128), "wave")

    modes = pl.pallas_call(
        legendre_adjoint_kernel,
        in_specs=[whole(WAVES, 168, 128), whole(HEAD, NLAT, NT), hbm],
        out_specs=whole(BANDS, 48, 128),
        out_shape=shape(BANDS, 48, 128),
        scratch_shapes=[pltpu.VMEM((336, NLAT), f32), *table_scratch],
        compiler_params=params(),
        cost_estimate=legendre_cost,
        name="legendre_adjoint",
    )(spec, head(again), in_hbm(legendre))
    modes = exchange(modes, "band").reshape(24, 4, 8, 128)

    gradient = pl.pallas_call(
        unmix_kernel,
        out_shape=shape(28, 16, 192),
        compiler_params=params(),
        cost_estimate=cost(6 * 448 * 192 * 192, 1 << 20),
        name="unmix",
    )(modes, control, scale, vertical_root)
    return jnp.swapaxes(gradient, 0, 1), state


def solution(mesh):
    both = ("wave", "band")
    placed = (
        P("band", "wave", None),
        P("band", "wave", None),
        P(),
        P("wave", None, None),
        P(),
        P("band", None, "wave"),
        P(),
        P(),
        P(both, None),
        P(both, None),
        P(both, None),
        P(both, None),
        P(both, None),
        P(both, None),
    )
    return jax.shard_map(
        body,
        mesh=mesh,
        in_specs=placed,
        out_specs=(P("band", "wave", None), P("band", None, "wave")),
        check_vma=False,
    )
```

```python
import math

import jax
import jax.numpy as jnp
from jax import lax
from jax.experimental import pallas as pl
from jax.experimental.pallas import tpu as pltpu
from jax.sharding import PartitionSpec as P

MW = 224
LEV = 8
BINS = 12
CH = 96
STEPS = 4
WAVES = 8
BANDS = 16
DEVICES = 128
SLOT = 128
GROUPS = 7
NLON = 1024
NLAT = 448
NT = 256
TILE = 21
FACTOR = MW ** (-0.5)
f32 = jnp.float32
bf16 = jnp.bfloat16
highest = lax.Precision.HIGHEST
LIMIT = 24 << 20


def params(**kw):
    return pltpu.CompilerParams(vmem_limit_bytes=LIMIT, **kw)


def split(x):
    hi = x.astype(bf16)
    return hi, (x - hi.astype(f32)).astype(bf16)


def mm(a, b):
    return lax.dot_general(a, b, (((1,), (0,)), ((), ())), preferred_element_type=f32)


def mm_nt(a, b):
    return lax.dot_general(a, b, (((1,), (1,)), ((), ())), preferred_element_type=f32)


def iota(shape, dim):
    return lax.broadcasted_iota(jnp.int32, shape, dim)


def turn(parts, axis, width):
    n = len(parts)
    size = parts[0].shape[axis]
    at = iota(parts[0].shape, axis)
    step = n // 2
    while step:
        keep = (at // (step * width)) % 2 == 0
        new = list(parts)
        for i in range(n):
            if (i // step) % 2 == 0:
                a, b = parts[i], parts[i + step]
                new[i] = jnp.where(keep, a, pltpu.roll(b, step * width, axis))
                new[i + step] = jnp.where(keep, pltpu.roll(a, size - step * width, axis), b)
        parts = new
        step //= 2
    return parts


def doubled_root(root):
    rows = (iota((2 * CH, CH), 0) // 2 == iota((2 * CH, CH), 1)).astype(f32)
    cols = (iota((CH, 2 * CH), 1) // 2 == iota((CH, 2 * CH), 0)).astype(f32)
    wide = jnp.dot(rows, root, precision=highest, preferred_element_type=f32)
    wide = jnp.dot(wide, cols, precision=highest, preferred_element_type=f32)
    same = iota((2 * CH, 2 * CH), 0) % 2 == iota((2 * CH, 2 * CH), 1) % 2
    return jnp.where(same, wide, 0.0)


def mix_kernel(
    control_hbm,
    scale_hbm,
    root_hbm,
    column_hbm,
    level_hbm,
    lidar_hbm,
    aod_hbm,
    weight_hbm,
    count_hbm,
    out_ref,
    control_ref,
    scale_ref,
    root_ref,
    index_ref,
    value_ref,
    count_ref,
    obs_ref,
    sem,
):
    copies = [
        pltpu.make_async_copy(source, target, sem.at[k])
        for k, (source, target) in enumerate(
            (
                (root_hbm, root_ref),
                (control_hbm, control_ref),
                (scale_hbm, scale_ref),
                (column_hbm, index_ref.at[0]),
                (level_hbm, index_ref.at[1]),
                (lidar_hbm, value_ref.at[0]),
                (aod_hbm, value_ref.at[1]),
                (weight_hbm, value_ref.at[2]),
                (count_hbm, count_ref),
            )
        )
    ]
    for copy in copies[3:] + copies[:3]:
        copy.start()
    for copy in copies[3:]:
        copy.wait()
    counts = jnp.broadcast_to(count_ref[...].astype(f32), (DEVICES, DEVICES)).T
    live = iota((DEVICES, SLOT), 1).astype(f32) < counts
    weight = jnp.where(live, value_ref[2], 0.0)
    obs_ref[0] = index_ref[0].astype(f32)
    obs_ref[1] = index_ref[1].astype(f32)
    obs_ref[2] = weight
    obs_ref[3] = weight * value_ref[0]
    obs_ref[4] = weight * value_ref[1]
    for band in range(BANDS):
        for k in range(5):
            rows = obs_ref[k, pl.ds(band, WAVES, stride=BANDS), :]
            out_ref[band, 48 + 8 * k : 56 + 8 * k] = rows

    for copy in copies[:3]:
        copy.wait()
    root = doubled_root(root_ref[...])
    rh, rl = split(root)
    tiles = []
    for m4 in range(4):
        x = jnp.concatenate([control_ref[4 * g + m4] for g in range(GROUPS)], axis=0)
        s = jnp.concatenate([scale_ref[4 * g + m4] for g in range(GROUPS)], axis=0)
        xh, xl = split(x)
        y = (mm(xh, rh) + mm(xl, rh) + mm(xh, rl)) * s
        y = jnp.concatenate([y, jnp.zeros((16, 2 * CH), f32)], axis=0)
        tiles.append(y.T.reshape(24, 8, 128))
    for j, z in enumerate(turn(tiles, 1, 2)):
        for h in range(24):
            c = 4 * h + j
            out_ref[c // 6, 8 * (c % 6) : 8 * (c % 6) + 8] = z[h]


def table_copies(table_hbm, table_ref, sem):
    copies = []
    for g in range(GROUPS):
        at = pl.ds(4 * g, 4)
        copies.append(pltpu.make_async_copy(table_hbm.at[at], table_ref.at[at], sem.at[g]))
    for copy in copies:
        copy.start()
    return copies


def legendre_kernel(modes_ref, table_hbm, out_ref, x_ref, acc_ref, table_ref, sem):
    copies = table_copies(table_hbm, table_ref, sem)
    for half in range(2):
        for c in range(6):
            got = [modes_ref[8 * half + s, 8 * c : 8 * c + 8] for s in range(8)]
            for g, z in enumerate(turn(got, 1, 16)):
                if g < GROUPS:
                    x_ref[g, 8 * c : 8 * c + 8, 128 * half : 128 * half + 128] = z
    for k in range(5):
        for half in range(2):
            got = [modes_ref[8 * half + s, 48 + 8 * k : 56 + 8 * k] for s in range(8)]
            at = 168 + 16 * k + 8 * half
            for w, z in enumerate(turn(got, 0, 1)):
                out_ref[w, at : at + 8] = z

    slot = (iota((48, NT), 0) % 8) // 2
    order = lat_order()
    for g in range(GROUPS):
        copies[g].wait()
        x = x_ref[g]
        acc = None
        for m4 in range(4):
            xh, xl = split(jnp.where(slot == m4, x, 0.0))
            both = jnp.concatenate(split(table_ref[4 * g + m4]), axis=0)
            both = mm_nt(jnp.concatenate([xh, xl], axis=0), both)
            part = both[:48, :NLAT] + (both[48:, :NLAT] + both[:48, NLAT:])
            acc = part if acc is None else acc + part
        acc_ref[g] = acc
        for first, last in ((0, 5), (5, 7)):
            if g + 1 == last:
                rows = 48 * (last - first)
                part = acc_ref[first:last].reshape(rows, NLAT)
                both = mm(jnp.concatenate(split(part), axis=0), order)
                out = both[:rows] + both[rows:]
                for k in range(first, last):
                    for q in range(4):
                        for hc in range(2):
                            at = 48 * (k - first) + 24 * hc
                            tile = out[at : at + 24, 128 * q : 128 * q + 128]
                            out_ref[2 * q + hc, 24 * k : 24 * k + 24] = tile


def lat_order():
    at = iota((NLAT, 512), 1)
    lat = ((at // 8) % 16) * 28 + (at // 128) * 7 + at % 8
    return jnp.where((iota((NLAT, 512), 0) == lat) & (at % 8 < 7), 1.0, 0.0).astype(bf16)


def wave_table_kernel(number_ref, high_ref, low_ref):
    rows = 16
    half = NLON // 2
    row = iota((rows, MW), 0)
    slot = iota((rows, MW), 1)
    part = iota((rows, half), 0) % 2
    lon = iota((rows, half), 1)
    numbers = number_ref[...].astype(f32)
    coefs = [(-1.0) ** k / math.factorial(2 * k + 1) for k in range(6)]

    @pl.loop(0, 2 * MW // rows)
    def _(i):
        first = pl.multiple_of(i * rows, rows)
        mine = (row + first) // 2 == slot
        n = jnp.sum(jnp.where(mine, numbers, 0.0), axis=1, keepdims=True).astype(jnp.int32)
        phase = (n * lon + 256 * part) & (NLON - 1)
        turn_at = (jnp.abs(phase - half) - half // 2).astype(f32)
        y = turn_at * (2.0 * math.pi / NLON)
        y2 = y * y
        value = coefs[5]
        for k in range(4, -1, -1):
            value = value * y2 + coefs[k]
        value = value * y * FACTOR
        vh, vl = split(value)
        high_ref[pl.ds(first, rows), :half] = vh
        low_ref[pl.ds(first, rows), :half] = vl
        sign = (1 - 2 * (n & 1)).astype(f32)
        vh, vl = split(value * sign)
        high_ref[pl.ds(first, rows), half:] = vh
        low_ref[pl.ds(first, rows), half:] = vl


def synthesis_kernel(spec_ref, high_ref, low_ref, out_ref, lhs_ref):
    rows = spec_ref[:, :168].reshape(WAVES, GROUPS, 3, 8, 128)
    for c in range(3):
        high, low = split(rows[:, :, c].reshape(2 * MW, 128).T)
        lhs_ref[128 * c : 128 * c + 128] = high
        lhs_ref[384 + 128 * c : 512 + 128 * c] = low
    for i in range(4):
        lon = pl.ds(256 * i, 256)
        both = mm(lhs_ref[...], high_ref[:, lon])
        out = both[:384] + both[384:] + mm(lhs_ref[:384], low_ref[:, lon])
        for w in range(2):
            for band in range(BANDS):
                for c in range(3):
                    row = 128 * c + 8 * band
                    at = TILE * (BANDS * (2 * i + w) + band) + 7 * c
                    out_ref[at : at + 7] = out[row : row + 7, 128 * w : 128 * w + 128]


def analysis_kernel(grid_ref, high_ref, low_ref, out_ref):
    blank = jnp.zeros((1, 128), f32)
    total = None
    for i in range(4):
        tiles = []
        for c in range(3):
            parts = []
            for w in range(2):
                rows = []
                for band in range(BANDS):
                    at = TILE * (BANDS * (2 * i + w) + band) + 7 * c
                    rows += [grid_ref[at : at + 7], blank]
                parts.append(jnp.concatenate(rows, axis=0))
            tiles.append(jnp.concatenate(parts, axis=1))
        gh, gl = split(jnp.concatenate(tiles, axis=0))
        lon = pl.ds(256 * i, 256)
        both = mm_nt(high_ref[:, lon], jnp.concatenate([gh, gl], axis=0))
        part = both[:, :384] + both[:, 384:] + mm_nt(low_ref[:, lon], gh)
        total = part if total is None else total + part
    for c in range(3):
        rows = total[:, 128 * c : 128 * c + 128]
        out_ref[:, :, c] = rows.reshape(WAVES, GROUPS, 8, 128)


def legendre_adjoint_kernel(spec_ref, table_hbm, out_ref, acc_ref, table_ref, sem):
    copies = table_copies(table_hbm, table_ref, sem)
    order = lat_order()
    for hc in range(2):
        s = jnp.concatenate([spec_ref[2 * q + hc] for q in range(4)], axis=1)
        sh, sl = split(s)
        acc_ref[168 * hc : 168 * hc + 168] = mm_nt(sh, order) + mm_nt(sl, order)
    slot = (iota((48, NLAT), 0) % 8) // 2
    x = []
    for g in range(GROUPS):
        copies[g].wait()
        rows = [acc_ref[168 * hc + 24 * g : 168 * hc + 24 * g + 24] for hc in range(2)]
        mine = jnp.concatenate(rows, axis=0)
        acc = None
        for m4 in range(4):
            xh, xl = split(jnp.where(slot == m4, mine, 0.0))
            th, tl = split(table_ref[4 * g + m4])
            both = mm(jnp.concatenate([xh, xl], axis=0), th)
            part = both[:48] + both[48:] + mm(xh, tl)
            acc = part if acc is None else acc + part
        x.append(acc)
    x.append(jnp.zeros((48, NT), f32))
    for half in range(2):
        for c in range(6):
            got = [v[8 * c : 8 * c + 8, 128 * half : 128 * half + 128] for v in x]
            for s, z in enumerate(turn(got, 1, 16)):
                out_ref[8 * half + s, 8 * c : 8 * c + 8] = z


def unmix_kernel(modes_ref, control_ref, scale_ref, root_ref, out_ref):
    root = doubled_root(root_ref[...])
    rh, rl = split(root)
    tiles = turn([modes_ref[:, j] for j in range(4)], 1, 2)
    for m4 in range(4):
        y = tiles[m4].reshape(2 * CH, 128).T[: 16 * GROUPS]
        s = jnp.concatenate([scale_ref[4 * g + m4] for g in range(GROUPS)], axis=0)
        yh, yl = split(y * s)
        z = mm_nt(yh, rh) + mm_nt(yl, rh) + mm_nt(yh, rl)
        for g in range(GROUPS):
            m = 4 * g + m4
            out_ref[m] = control_ref[m] + z[16 * g : 16 * g + 16]


def sums_kernel(obs_ref, out_ref, acc_ref):
    i = pl.program_id(0)
    part = None
    for half in range(2):

        def line(k):
            at = 168 + 16 * k + 8 * half
            rows = obs_ref[0, at : at + 8]
            return jnp.concatenate([rows[s : s + 1] for s in range(8)], axis=1)

        column = line(0).astype(jnp.int32)
        level = line(1).astype(jnp.int32)
        lat = column // 128
        lon = column % 128
        q = sum((lat >= 7 * k).astype(jnp.int32) for k in range(1, 4))
        row = q * 64 + level * 8 + (lat - 7 * q)
        rows = jnp.where(iota((256, 1024), 0) == row, 1.0, 0.0).astype(bf16)
        cols = jnp.where(iota((128, 1024), 0) == lon, 1.0, 0.0).astype(bf16)
        values = []
        for k in range(2, 5):
            for v in split(line(k)):
                values.append(cols * v)
        new = mm_nt(rows, jnp.concatenate(values, axis=0))
        part = new if part is None else part + new

    @pl.when(i == 0)
    def _():
        acc_ref[...] = part

    @pl.when(i > 0)
    def _():
        acc_ref[...] += part

    @pl.when(i == WAVES - 1)
    def _():
        for k in range(3):
            first = acc_ref[:, 256 * k : 256 * k + 128]
            out_ref[k] = first + acc_ref[:, 256 * k + 128 : 256 * k + 256]


def flow_kernel(courant_ref, out_ref):
    for h in range(12):
        rows = [courant_ref[min(t, 6), 8 * h : 8 * h + 8] for t in range(8)]
        for j, z in enumerate(turn(rows, 0, 1)):
            out_ref[8 * h + j] = z


def grid_kernel(
    grid_ref, flow_ref, sums_ref, lidar_ref, aod_ref, state_ref, adjoint_ref, hold_ref
):
    def tile_rows(l, b2, hc, c):
        return pl.ds(TILE * (BANDS * hc + 2 * l + b2) + 7 * c, 7)

    blank = jnp.zeros((1, 128), f32)
    chains = [(b2, hc, c) for b2 in range(2) for hc in range(2) for c in range(3)]
    lidar_sum = [None] * LEV
    aod_sum = None
    for b2, hc, c in chains:
        bin_at = b2 * 6 + hc * 3 + c
        x = [
            jnp.concatenate([grid_ref[tile_rows(l, b2, hc, c)], blank], axis=0)
            for l in range(LEV)
        ]
        flow = [flow_ref[BINS * l + bin_at] for l in range(LEV)]
        for step in range(STEPS):
            out = [flow[l] * x[l] for l in range(LEV)]
            x = [x[l] - out[l] if l == 0 else x[l] - out[l] + out[l - 1] for l in range(LEV)]
        coef = lidar_ref[bin_at]
        for l in range(LEV):
            hold_ref[BINS * l + bin_at] = x[l]
            lidar_sum[l] = x[l] * coef if lidar_sum[l] is None else lidar_sum[l] + x[l] * coef
            term = x[l] * aod_ref[BINS * l + bin_at]
            aod_sum = term if aod_sum is None else aod_sum + term

    for h in range(12):
        rows = turn([hold_ref[8 * h + j] for j in range(8)], 0, 1)
        for t in range(7):
            state_ref[t, 8 * h : 8 * h + 8] = rows[t]

    weight = [sums_ref[0, 8 * l : 8 * l + 8] for l in range(LEV)]
    lidar = [weight[l] * lidar_sum[l] - sums_ref[1, 8 * l : 8 * l + 8] for l in range(LEV)]
    aod = sum(weight[1:], weight[0]) * aod_sum
    for l in range(LEV):
        aod = aod - sums_ref[2, 8 * l : 8 * l + 8]
    for b2, hc, c in chains:
        bin_at = b2 * 6 + hc * 3 + c
        coef = lidar_ref[bin_at]
        flow = [flow_ref[BINS * l + bin_at] for l in range(LEV)]
        a = [lidar[l] * coef + aod * aod_ref[BINS * l + bin_at] for l in range(LEV)]
        for step in range(STEPS):
            a = [
                a[l] + flow[l] * ((a[l + 1] - a[l]) if l + 1 < LEV else -a[l]) for l in range(LEV)
            ]
        for l in range(LEV):
            adjoint_ref[tile_rows(l, b2, hc, c)] = a[l][:7]


def shape(*lengths, kind=f32):
    return jax.ShapeDtypeStruct(lengths, kind)


def whole(*lengths):
    return pl.BlockSpec(lengths, lambda *_: (0,) * len(lengths))


def in_hbm(x):
    return pltpu.with_memory_space_constraint(x, pltpu.HBM)


def cost(flops, size):
    return pl.CostEstimate(flops=flops, bytes_accessed=size, transcendentals=0)


def exchange(tiles, axis):
    return lax.all_to_all(tiles, axis, split_axis=0, concat_axis=0, tiled=True)


def exchange_tiles(tiles):
    rows = tiles.reshape(DEVICES, 1, TILE * 128)
    return exchange(rows, ("wave", "band")).reshape(DEVICES * TILE, 128)


def body(
    control,
    spectral_scale,
    vertical_root,
    legendre,
    zonal_number,
    courant,
    lidar_coef,
    aod_coef,
    obs_count,
    obs_column,
    obs_level,
    lidar_obs,
    aod_obs,
    obs_weight,
):
    control = jnp.swapaxes(control, 0, 1)
    scale = jnp.swapaxes(spectral_scale, 0, 1)
    hbm = pl.BlockSpec(memory_space=pltpu.HBM)
    modes = pl.pallas_call(
        mix_kernel,
        in_specs=[hbm] * 9,
        out_specs=whole(BANDS, 88, 128),
        out_shape=shape(BANDS, 88, 128),
        scratch_shapes=[
            pltpu.VMEM((28, 16, 192), f32),
            pltpu.VMEM((28, 16, 192), f32),
            pltpu.VMEM((CH, CH), f32),
            pltpu.VMEM((2, DEVICES, SLOT), jnp.int32),
            pltpu.VMEM((3, DEVICES, SLOT), f32),
            pltpu.VMEM((1, DEVICES), jnp.int32),
            pltpu.VMEM((5, DEVICES, SLOT), f32),
            pltpu.SemaphoreType.DMA((9,)),
        ],
        compiler_params=params(),
        cost_estimate=cost(6 * 448 * 192 * 192, 1 << 20),
        name="mix",
    )(
        *(
            in_hbm(x)
            for x in (
                control,
                scale,
                vertical_root,
                obs_column,
                obs_level,
                lidar_obs,
                aod_obs,
                obs_weight,
                obs_count,
            )
        )
    )
    modes = exchange(modes, "band")

    high, low = pl.pallas_call(
        wave_table_kernel,
        out_shape=(shape(2 * MW, NLON, kind=bf16), shape(2 * MW, NLON, kind=bf16)),
        compiler_params=params(),
        cost_estimate=cost(20 * 448 * 1024, 2 << 20),
        name="wave_table",
    )(zonal_number.reshape(1, MW))
    legendre_cost = cost(6 * 28 * 448 * 256 * 48, 14 << 20)
    in_order = params(dimension_semantics=("arbitrary",))
    table_scratch = [pltpu.VMEM((28, NLAT, NT), f32), pltpu.SemaphoreType.DMA((GROUPS,))]
    spec = pl.pallas_call(
        legendre_kernel,
        in_specs=[whole(BANDS, 88, 128), hbm],
        out_specs=whole(WAVES, 248, 128),
        out_shape=shape(WAVES, 248, 128),
        scratch_shapes=[
            pltpu.VMEM((GROUPS, 48, NT), f32),
            pltpu.VMEM((GROUPS, 48, NLAT), f32),
            *table_scratch,
        ],
        compiler_params=params(),
        cost_estimate=legendre_cost,
        name="legendre",
    )(modes, in_hbm(legendre))
    spec = exchange(spec, "wave")
    sums = pl.pallas_call(
        sums_kernel,
        grid=(WAVES,),
        in_specs=[pl.BlockSpec((1, 248, 128), lambda i: (i, 0, 0))],
        out_specs=whole(3, 256, 128),
        out_shape=shape(3, 256, 128),
        scratch_shapes=[pltpu.VMEM((256, 768), f32)],
        compiler_params=in_order,
        cost_estimate=cost(2 * 16384 * 256 * 768, 1 << 20),
        name="sums",
    )(spec)

    tile_spec = pl.BlockSpec((2 * BANDS * TILE, 128), lambda i: (i, 0))
    tiles = shape(DEVICES * TILE, 128)
    wave_cost = cost(6 * 384 * 448 * 1024, 4 << 20)
    grid = pl.pallas_call(
        synthesis_kernel,
        out_shape=tiles,
        scratch_shapes=[pltpu.VMEM((768, 2 * MW), bf16)],
        compiler_params=params(),
        cost_estimate=wave_cost,
        name="synthesis",
    )(spec, high, low)
    grid = exchange_tiles(grid)

    field = pl.BlockSpec((7, CH, 128), lambda q: (q, 0, 0))
    scalars = pl.BlockSpec(memory_space=pltpu.SMEM)
    turned = pl.BlockSpec((CH, 8, 128), lambda q: (q, 0, 0))
    flow = pl.pallas_call(
        flow_kernel,
        grid=(4,),
        in_specs=[field],
        out_specs=turned,
        out_shape=shape(4 * CH, 8, 128),
        compiler_params=in_order,
        cost_estimate=cost(6 * 28 * 96 * 128, 3 << 20),
        name="flow",
    )(in_hbm(courant))
    state, adjoint = pl.pallas_call(
        grid_kernel,
        grid=(4,),
        in_specs=[
            tile_spec,
            turned,
            pl.BlockSpec((3, 64, 128), lambda q: (0, q, 0)),
            scalars,
            scalars,
        ],
        out_specs=(field, tile_spec),
        out_shape=(shape(28, CH, 128), tiles),
        scratch_shapes=[pltpu.VMEM((CH, 8, 128), f32)],
        compiler_params=in_order,
        cost_estimate=cost(40 * 28 * 96 * 128, 6 << 20),
        name="grid_steps",
    )(grid, flow, in_hbm(sums), lidar_coef, aod_coef)
    adjoint = exchange_tiles(adjoint)

    spec = pl.pallas_call(
        analysis_kernel,
        out_shape=shape(WAVES, GROUPS, 3, 8, 128),
        compiler_params=params(),
        cost_estimate=wave_cost,
        name="analysis",
    )(adjoint, high, low)
    spec = exchange(spec.reshape(WAVES, 24 * GROUPS, 128), "wave")

    modes = pl.pallas_call(
        legendre_adjoint_kernel,
        in_specs=[whole(WAVES, 168, 128), hbm],
        out_specs=whole(BANDS, 48, 128),
        out_shape=shape(BANDS, 48, 128),
        scratch_shapes=[pltpu.VMEM((336, NLAT), f32), *table_scratch],
        compiler_params=params(),
        cost_estimate=legendre_cost,
        name="legendre_adjoint",
    )(spec, in_hbm(legendre))
    modes = exchange(modes, "band").reshape(24, 4, 8, 128)

    gradient = pl.pallas_call(
        unmix_kernel,
        out_shape=shape(28, 16, 192),
        compiler_params=params(),
        cost_estimate=cost(6 * 448 * 192 * 192, 1 << 20),
        name="unmix",
    )(modes, control, scale, vertical_root)
    return jnp.swapaxes(gradient, 0, 1), state


def solution(mesh):
    both = ("wave", "band")
    placed = (
        P("band", "wave", None),
        P("band", "wave", None),
        P(),
        P("wave", None, None),
        P(),
        P("band", None, "wave"),
        P(),
        P(),
        P(both, None),
        P(both, None),
        P(both, None),
        P(both, None),
        P(both, None),
        P(both, None),
    )
    return jax.shard_map(
        body,
        mesh=mesh,
        in_specs=placed,
        out_specs=(P("band", "wave", None), P("band", None, "wave")),
        check_vma=False,
    )
```

```python
import math

import jax
import jax.numpy as jnp
from jax import lax
from jax.experimental import pallas as pl
from jax.experimental.pallas import tpu as pltpu
from jax.sharding import PartitionSpec as P

MW = 224
LEV = 8
BINS = 12
CH = 96
STEPS = 4
WAVES = 8
BANDS = 16
DEVICES = 128
SLOT = 128
GROUPS = 7
NLON = 1024
NLAT = 448
NT = 256
TILE = 21
FACTOR = MW ** (-0.5)
f32 = jnp.float32
bf16 = jnp.bfloat16
highest = lax.Precision.HIGHEST
LIMIT = 24 << 20


def params(**kw):
    return pltpu.CompilerParams(vmem_limit_bytes=LIMIT, **kw)


def split(x):
    hi = x.astype(bf16)
    return hi, (x - hi.astype(f32)).astype(bf16)


def mm(a, b):
    return lax.dot_general(a, b, (((1,), (0,)), ((), ())), preferred_element_type=f32)


def mm_nt(a, b):
    return lax.dot_general(a, b, (((1,), (1,)), ((), ())), preferred_element_type=f32)


def iota(shape, dim):
    return lax.broadcasted_iota(jnp.int32, shape, dim)


def turn(parts, axis, width):
    n = len(parts)
    size = parts[0].shape[axis]
    at = iota(parts[0].shape, axis)
    step = n // 2
    while step:
        keep = (at // (step * width)) % 2 == 0
        new = list(parts)
        for i in range(n):
            if (i // step) % 2 == 0:
                a, b = parts[i], parts[i + step]
                new[i] = jnp.where(keep, a, pltpu.roll(b, step * width, axis))
                new[i + step] = jnp.where(keep, pltpu.roll(a, size - step * width, axis), b)
        parts = new
        step //= 2
    return parts


def doubled_root(root):
    rows = (iota((2 * CH, CH), 0) // 2 == iota((2 * CH, CH), 1)).astype(f32)
    cols = (iota((CH, 2 * CH), 1) // 2 == iota((CH, 2 * CH), 0)).astype(f32)
    wide = jnp.dot(rows, root, precision=highest, preferred_element_type=f32)
    wide = jnp.dot(wide, cols, precision=highest, preferred_element_type=f32)
    same = iota((2 * CH, 2 * CH), 0) % 2 == iota((2 * CH, 2 * CH), 1) % 2
    return jnp.where(same, wide, 0.0)


def mix_kernel(control_hbm, scale_hbm, root_hbm, out_ref, control_ref, scale_ref, root_ref, sem):
    copies = [
        pltpu.make_async_copy(source, target, sem.at[k])
        for k, (source, target) in enumerate(
            ((root_hbm, root_ref), (control_hbm, control_ref), (scale_hbm, scale_ref))
        )
    ]
    for copy in copies:
        copy.start()
    copies[0].wait()
    root = doubled_root(root_ref[...])
    rh, rl = split(root)
    copies[1].wait()
    copies[2].wait()
    tiles = []
    for m4 in range(4):
        x = jnp.concatenate([control_ref[4 * g + m4] for g in range(GROUPS)], axis=0)
        s = jnp.concatenate([scale_ref[4 * g + m4] for g in range(GROUPS)], axis=0)
        xh, xl = split(x)
        y = (mm(xh, rh) + mm(xl, rh) + mm(xh, rl)) * s
        y = jnp.concatenate([y, jnp.zeros((16, 2 * CH), f32)], axis=0)
        tiles.append(y.T.reshape(24, 8, 128))
    for j, z in enumerate(turn(tiles, 1, 2)):
        for h in range(24):
            c = 4 * h + j
            out_ref[c // 6, 8 * (c % 6) : 8 * (c % 6) + 8] = z[h]


def pack_kernel(count_ref, column_ref, level_ref, lidar_ref, aod_ref, weight_ref, out_ref):
    me = lax.axis_index("wave")
    counts = jnp.broadcast_to(count_ref[...].astype(f32), (DEVICES, DEVICES)).T
    for wave in range(WAVES):
        at = pl.ds(BANDS * wave, BANDS)
        live = iota((BANDS, SLOT), 1).astype(f32) < counts[BANDS * wave : BANDS * wave + BANDS]
        weight = jnp.where(live, weight_ref[at, :], 0.0)
        tile = (
            column_ref[at, :].astype(f32),
            level_ref[at, :].astype(f32),
            weight,
            weight * lidar_ref[at, :],
            weight * aod_ref[at, :],
        )
        s = (wave - me + WAVES) % WAVES
        for k in range(5):
            out_ref[s, BANDS * k : BANDS * k + BANDS] = tile[k]


def to_y_kernel(*refs):
    out_ref = refs[-1]
    me = lax.axis_index("band") // 4
    for y in range(4):
        s = (y - me + 4) % 4
        for k in range(5):
            rows = [ref[16 * k + 4 * y : 16 * k + 4 * y + 4] for ref in refs[:-1]]
            out_ref[s, 32 * k : 32 * k + 32] = jnp.concatenate(rows, axis=0)


def to_z_kernel(*refs):
    out_ref = refs[-1]
    me = lax.axis_index("band") % 4
    for z in range(4):
        s = (z - me + 4) % 4
        for k in range(5):
            for i, ref in enumerate(refs[:-1]):
                at = 32 * k + 8 * i
                out_ref[s, at : at + 8] = ref[pl.ds(32 * k + z, 8, stride=4), :]


def table_copies(table_hbm, table_ref, sem):
    copies = []
    for g in range(GROUPS):
        at = pl.ds(4 * g, 4)
        copies.append(pltpu.make_async_copy(table_hbm.at[at], table_ref.at[at], sem.at[g]))
    for copy in copies:
        copy.start()
    return copies


def legendre_kernel(modes_ref, table_hbm, out_ref, x_ref, acc_ref, table_ref, sem):
    copies = table_copies(table_hbm, table_ref, sem)
    for half in range(2):
        for c in range(6):
            got = [modes_ref[8 * half + s, 8 * c : 8 * c + 8] for s in range(8)]
            for g, z in enumerate(turn(got, 1, 16)):
                if g < GROUPS:
                    x_ref[g, 8 * c : 8 * c + 8, 128 * half : 128 * half + 128] = z
    slot = (iota((48, NT), 0) % 8) // 2
    order = lat_order()
    for g in range(GROUPS):
        copies[g].wait()
        x = x_ref[g]
        acc = None
        for m4 in range(4):
            xh, xl = split(jnp.where(slot == m4, x, 0.0))
            both = jnp.concatenate(split(table_ref[4 * g + m4]), axis=0)
            both = mm_nt(jnp.concatenate([xh, xl], axis=0), both)
            part = both[:48, :NLAT] + (both[48:, :NLAT] + both[:48, NLAT:])
            acc = part if acc is None else acc + part
        acc_ref[g] = acc
        for first, last in ((0, 5), (5, 7)):
            if g + 1 == last:
                rows = 48 * (last - first)
                part = acc_ref[first:last].reshape(rows, NLAT)
                both = mm(jnp.concatenate(split(part), axis=0), order)
                out = both[:rows] + both[rows:]
                for k in range(first, last):
                    for q in range(4):
                        for hc in range(2):
                            at = 48 * (k - first) + 24 * hc
                            tile = out[at : at + 24, 128 * q : 128 * q + 128]
                            out_ref[2 * q + hc, 24 * k : 24 * k + 24] = tile


def lat_order():
    at = iota((NLAT, 512), 1)
    lat = ((at // 8) % 16) * 28 + (at // 128) * 7 + at % 8
    return jnp.where((iota((NLAT, 512), 0) == lat) & (at % 8 < 7), 1.0, 0.0).astype(bf16)


def wave_table_kernel(number_ref, high_ref, low_ref):
    rows = 16
    half = NLON // 2
    row = iota((rows, MW), 0)
    slot = iota((rows, MW), 1)
    part = iota((rows, half), 0) % 2
    lon = iota((rows, half), 1)
    numbers = number_ref[...].astype(f32)
    coefs = [(-1.0) ** k / math.factorial(2 * k + 1) for k in range(6)]

    @pl.loop(0, 2 * MW // rows)
    def _(i):
        first = pl.multiple_of(i * rows, rows)
        mine = (row + first) // 2 == slot
        n = jnp.sum(jnp.where(mine, numbers, 0.0), axis=1, keepdims=True).astype(jnp.int32)
        phase = (n * lon + 256 * part) & (NLON - 1)
        turn_at = (jnp.abs(phase - half) - half // 2).astype(f32)
        y = turn_at * (2.0 * math.pi / NLON)
        y2 = y * y
        value = coefs[5]
        for k in range(4, -1, -1):
            value = value * y2 + coefs[k]
        value = value * y * FACTOR
        vh, vl = split(value)
        high_ref[pl.ds(first, rows), :half] = vh
        low_ref[pl.ds(first, rows), :half] = vl
        sign = (1 - 2 * (n & 1)).astype(f32)
        vh, vl = split(value * sign)
        high_ref[pl.ds(first, rows), half:] = vh
        low_ref[pl.ds(first, rows), half:] = vl


def synthesis_kernel(spec_ref, high_ref, low_ref, out_ref, lhs_ref):
    rows = spec_ref[...].reshape(WAVES, GROUPS, 3, 8, 128)
    for c in range(3):
        high, low = split(rows[:, :, c].reshape(2 * MW, 128).T)
        lhs_ref[128 * c : 128 * c + 128] = high
        lhs_ref[384 + 128 * c : 512 + 128 * c] = low
    for i in range(4):
        lon = pl.ds(256 * i, 256)
        both = mm(lhs_ref[...], high_ref[:, lon])
        out = both[:384] + both[384:] + mm(lhs_ref[:384], low_ref[:, lon])
        for w in range(2):
            for band in range(BANDS):
                for c in range(3):
                    row = 128 * c + 8 * band
                    at = TILE * (BANDS * (2 * i + w) + band) + 7 * c
                    out_ref[at : at + 7] = out[row : row + 7, 128 * w : 128 * w + 128]


def analysis_kernel(grid_ref, high_ref, low_ref, out_ref):
    blank = jnp.zeros((1, 128), f32)
    total = None
    for i in range(4):
        tiles = []
        for c in range(3):
            parts = []
            for w in range(2):
                rows = []
                for band in range(BANDS):
                    at = TILE * (BANDS * (2 * i + w) + band) + 7 * c
                    rows += [grid_ref[at : at + 7], blank]
                parts.append(jnp.concatenate(rows, axis=0))
            tiles.append(jnp.concatenate(parts, axis=1))
        gh, gl = split(jnp.concatenate(tiles, axis=0))
        lon = pl.ds(256 * i, 256)
        both = mm_nt(high_ref[:, lon], jnp.concatenate([gh, gl], axis=0))
        part = both[:, :384] + both[:, 384:] + mm_nt(low_ref[:, lon], gh)
        total = part if total is None else total + part
    for c in range(3):
        rows = total[:, 128 * c : 128 * c + 128]
        out_ref[:, :, c] = rows.reshape(WAVES, GROUPS, 8, 128)


def legendre_adjoint_kernel(spec_ref, table_hbm, out_ref, acc_ref, table_ref, sem):
    copies = table_copies(table_hbm, table_ref, sem)
    order = lat_order()
    for hc in range(2):
        s = jnp.concatenate([spec_ref[2 * q + hc] for q in range(4)], axis=1)
        sh, sl = split(s)
        acc_ref[168 * hc : 168 * hc + 168] = mm_nt(sh, order) + mm_nt(sl, order)
    slot = (iota((48, NLAT), 0) % 8) // 2
    x = []
    for g in range(GROUPS):
        copies[g].wait()
        rows = [acc_ref[168 * hc + 24 * g : 168 * hc + 24 * g + 24] for hc in range(2)]
        mine = jnp.concatenate(rows, axis=0)
        acc = None
        for m4 in range(4):
            xh, xl = split(jnp.where(slot == m4, mine, 0.0))
            th, tl = split(table_ref[4 * g + m4])
            both = mm(jnp.concatenate([xh, xl], axis=0), th)
            part = both[:48] + both[48:] + mm(xh, tl)
            acc = part if acc is None else acc + part
        x.append(acc)
    x.append(jnp.zeros((48, NT), f32))
    for half in range(2):
        for c in range(6):
            got = [v[8 * c : 8 * c + 8, 128 * half : 128 * half + 128] for v in x]
            for s, z in enumerate(turn(got, 1, 16)):
                out_ref[8 * half + s, 8 * c : 8 * c + 8] = z


def unmix_kernel(modes_ref, control_ref, scale_ref, root_ref, out_ref):
    root = doubled_root(root_ref[...])
    rh, rl = split(root)
    tiles = turn([modes_ref[:, j] for j in range(4)], 1, 2)
    for m4 in range(4):
        y = tiles[m4].reshape(2 * CH, 128).T[: 16 * GROUPS]
        s = jnp.concatenate([scale_ref[4 * g + m4] for g in range(GROUPS)], axis=0)
        yh, yl = split(y * s)
        z = mm_nt(yh, rh) + mm_nt(yl, rh) + mm_nt(yh, rl)
        for g in range(GROUPS):
            m = 4 * g + m4
            out_ref[m] = control_ref[m] + z[16 * g : 16 * g + 16]


def sums_kernel(*refs):
    out_ref, acc_ref = refs[-2:]
    acc_ref[...] = jnp.zeros_like(acc_ref)
    for ref in refs[:-2]:

        @pl.loop(0, 4)
        def _(i):
            def line(k):
                rows = ref[pl.ds(pl.multiple_of(32 * k + 8 * i, 8), 8), :]
                return jnp.concatenate([rows[s : s + 1] for s in range(8)], axis=1)

            column = line(0).astype(jnp.int32)
            level = line(1).astype(jnp.int32)
            lat = column // 128
            lon = column % 128
            q = sum((lat >= 7 * k).astype(jnp.int32) for k in range(1, 4))
            row = q * 64 + level * 8 + (lat - 7 * q)
            rows = jnp.where(iota((256, 1024), 0) == row, 1.0, 0.0).astype(bf16)
            cols = jnp.where(iota((128, 1024), 0) == lon, 1.0, 0.0).astype(bf16)
            values = []
            for k in range(2, 5):
                for v in split(line(k)):
                    values.append(cols * v)
            acc_ref[...] += mm_nt(rows, jnp.concatenate(values, axis=0))

    for k in range(3):
        first = acc_ref[:, 256 * k : 256 * k + 128]
        out_ref[k] = first + acc_ref[:, 256 * k + 128 : 256 * k + 256]


def flow_kernel(courant_ref, out_ref):
    for h in range(12):
        rows = [courant_ref[min(t, 6), 8 * h : 8 * h + 8] for t in range(8)]
        for j, z in enumerate(turn(rows, 0, 1)):
            out_ref[8 * h + j] = z


def grid_kernel(
    grid_ref, flow_ref, sums_ref, lidar_ref, aod_ref, state_ref, adjoint_ref, hold_ref
):
    def tile_rows(l, b2, hc, c):
        return pl.ds(TILE * (BANDS * hc + 2 * l + b2) + 7 * c, 7)

    blank = jnp.zeros((1, 128), f32)
    chains = [(b2, hc, c) for b2 in range(2) for hc in range(2) for c in range(3)]
    lidar_sum = [None] * LEV
    aod_sum = None
    for b2, hc, c in chains:
        bin_at = b2 * 6 + hc * 3 + c
        x = [
            jnp.concatenate([grid_ref[tile_rows(l, b2, hc, c)], blank], axis=0)
            for l in range(LEV)
        ]
        flow = [flow_ref[BINS * l + bin_at] for l in range(LEV)]
        for step in range(STEPS):
            out = [flow[l] * x[l] for l in range(LEV)]
            x = [x[l] - out[l] if l == 0 else x[l] - out[l] + out[l - 1] for l in range(LEV)]
        coef = lidar_ref[bin_at]
        for l in range(LEV):
            hold_ref[BINS * l + bin_at] = x[l]
            lidar_sum[l] = x[l] * coef if lidar_sum[l] is None else lidar_sum[l] + x[l] * coef
            term = x[l] * aod_ref[BINS * l + bin_at]
            aod_sum = term if aod_sum is None else aod_sum + term

    for h in range(12):
        rows = turn([hold_ref[8 * h + j] for j in range(8)], 0, 1)
        for t in range(7):
            state_ref[t, 8 * h : 8 * h + 8] = rows[t]

    weight = [sums_ref[0, 8 * l : 8 * l + 8] for l in range(LEV)]
    lidar = [weight[l] * lidar_sum[l] - sums_ref[1, 8 * l : 8 * l + 8] for l in range(LEV)]
    aod = sum(weight[1:], weight[0]) * aod_sum
    for l in range(LEV):
        aod = aod - sums_ref[2, 8 * l : 8 * l + 8]
    for b2, hc, c in chains:
        bin_at = b2 * 6 + hc * 3 + c
        coef = lidar_ref[bin_at]
        flow = [flow_ref[BINS * l + bin_at] for l in range(LEV)]
        a = [lidar[l] * coef + aod * aod_ref[BINS * l + bin_at] for l in range(LEV)]
        for step in range(STEPS):
            a = [
                a[l] + flow[l] * ((a[l + 1] - a[l]) if l + 1 < LEV else -a[l]) for l in range(LEV)
            ]
        for l in range(LEV):
            adjoint_ref[tile_rows(l, b2, hc, c)] = a[l][:7]


def shape(*lengths, kind=f32):
    return jax.ShapeDtypeStruct(lengths, kind)


def whole(*lengths):
    return pl.BlockSpec(lengths, lambda *_: (0,) * len(lengths))


def in_hbm(x):
    return pltpu.with_memory_space_constraint(x, pltpu.HBM)


def cost(flops, size):
    return pl.CostEstimate(flops=flops, bytes_accessed=size, transcendentals=0)


def exchange(tiles, axis):
    return lax.all_to_all(tiles, axis, split_axis=0, concat_axis=0, tiled=True)


def shifted(tiles, axis, places):
    count = lax.axis_size(axis)
    got = [tiles[0]]
    for s in range(1, tiles.shape[0]):
        got.append(lax.ppermute(tiles[s], axis, [(i, places(i, s)) for i in range(count)]))
    return got


def packed(*arrays):
    return pl.pallas_call(
        pack_kernel,
        out_shape=shape(WAVES, 5 * BANDS, SLOT),
        compiler_params=params(),
        cost_estimate=cost(10 * 16384, 1 << 20),
        name="pack",
    )(*arrays)


def regrouped(kernel, got, name):
    return pl.pallas_call(
        kernel,
        out_shape=shape(4, 160, SLOT),
        compiler_params=params(),
        cost_estimate=cost(0, 1 << 20),
        name=name,
    )(*got)


def summed(got):
    return pl.pallas_call(
        sums_kernel,
        out_shape=shape(3, 256, 128),
        scratch_shapes=[pltpu.VMEM((256, 768), f32)],
        compiler_params=params(),
        cost_estimate=cost(2 * 16384 * 256 * 768, 1 << 20),
        name="sums",
    )(*got)


def exchange_tiles(tiles):
    rows = tiles.reshape(DEVICES, 1, TILE * 128)
    return exchange(rows, ("wave", "band")).reshape(DEVICES * TILE, 128)


def body(
    control,
    spectral_scale,
    vertical_root,
    legendre,
    zonal_number,
    courant,
    lidar_coef,
    aod_coef,
    obs_count,
    obs_column,
    obs_level,
    lidar_obs,
    aod_obs,
    obs_weight,
):
    control = jnp.swapaxes(control, 0, 1)
    scale = jnp.swapaxes(spectral_scale, 0, 1)
    hbm = pl.BlockSpec(memory_space=pltpu.HBM)
    modes = pl.pallas_call(
        mix_kernel,
        in_specs=[hbm] * 3,
        out_specs=whole(BANDS, 48, 128),
        out_shape=shape(BANDS, 48, 128),
        scratch_shapes=[
            pltpu.VMEM((28, 16, 192), f32),
            pltpu.VMEM((28, 16, 192), f32),
            pltpu.VMEM((CH, CH), f32),
            pltpu.SemaphoreType.DMA((3,)),
        ],
        compiler_params=params(),
        cost_estimate=cost(6 * 448 * 192 * 192, 1 << 20),
        name="mix",
    )(in_hbm(control), in_hbm(scale), in_hbm(vertical_root))
    modes, obs_weight = lax.optimization_barrier((modes, obs_weight))
    obs = packed(obs_count, obs_column, obs_level, lidar_obs, aod_obs, obs_weight)
    obs = shifted(obs, "wave", lambda i, s: (i + s) % WAVES)
    modes, obs = lax.optimization_barrier((exchange(modes, "band"), obs))
    obs = regrouped(to_y_kernel, obs, "to_y")
    obs = shifted(obs, "band", lambda i, s: (i + 4 * s) % BANDS)

    high, low = pl.pallas_call(
        wave_table_kernel,
        out_shape=(shape(2 * MW, NLON, kind=bf16), shape(2 * MW, NLON, kind=bf16)),
        compiler_params=params(),
        cost_estimate=cost(20 * 448 * 1024, 2 << 20),
        name="wave_table",
    )(zonal_number.reshape(1, MW))
    legendre_cost = cost(6 * 28 * 448 * 256 * 48, 14 << 20)
    in_order = params(dimension_semantics=("arbitrary",))
    table_scratch = [pltpu.VMEM((28, NLAT, NT), f32), pltpu.SemaphoreType.DMA((GROUPS,))]
    spec = pl.pallas_call(
        legendre_kernel,
        in_specs=[whole(BANDS, 48, 128), hbm],
        out_specs=whole(WAVES, 168, 128),
        out_shape=shape(WAVES, 168, 128),
        scratch_shapes=[
            pltpu.VMEM((GROUPS, 48, NT), f32),
            pltpu.VMEM((GROUPS, 48, NLAT), f32),
            *table_scratch,
        ],
        compiler_params=params(),
        cost_estimate=legendre_cost,
        name="legendre",
    )(modes, in_hbm(legendre))
    spec, obs = lax.optimization_barrier((exchange(spec, "wave"), obs))
    obs = regrouped(to_z_kernel, obs, "to_z")
    obs = shifted(obs, "band", lambda i, s: i // 4 * 4 + (i + s) % 4)
    sums = summed(obs)
    tile_spec = pl.BlockSpec((2 * BANDS * TILE, 128), lambda i: (i, 0))
    tiles = shape(DEVICES * TILE, 128)
    wave_cost = cost(6 * 384 * 448 * 1024, 4 << 20)
    grid = pl.pallas_call(
        synthesis_kernel,
        out_shape=tiles,
        scratch_shapes=[pltpu.VMEM((768, 2 * MW), bf16)],
        compiler_params=params(),
        cost_estimate=wave_cost,
        name="synthesis",
    )(spec, high, low)
    grid = exchange_tiles(grid)

    field = pl.BlockSpec((7, CH, 128), lambda q: (q, 0, 0))
    scalars = pl.BlockSpec(memory_space=pltpu.SMEM)
    turned = pl.BlockSpec((CH, 8, 128), lambda q: (q, 0, 0))
    flow = pl.pallas_call(
        flow_kernel,
        grid=(4,),
        in_specs=[field],
        out_specs=turned,
        out_shape=shape(4 * CH, 8, 128),
        compiler_params=in_order,
        cost_estimate=cost(6 * 28 * 96 * 128, 3 << 20),
        name="flow",
    )(in_hbm(courant))
    state, adjoint = pl.pallas_call(
        grid_kernel,
        grid=(4,),
        in_specs=[
            tile_spec,
            turned,
            pl.BlockSpec((3, 64, 128), lambda q: (0, q, 0)),
            scalars,
            scalars,
        ],
        out_specs=(field, tile_spec),
        out_shape=(shape(28, CH, 128), tiles),
        scratch_shapes=[pltpu.VMEM((CH, 8, 128), f32)],
        compiler_params=in_order,
        cost_estimate=cost(40 * 28 * 96 * 128, 6 << 20),
        name="grid_steps",
    )(grid, flow, in_hbm(sums), lidar_coef, aod_coef)
    adjoint = exchange_tiles(adjoint)

    spec = pl.pallas_call(
        analysis_kernel,
        out_shape=shape(WAVES, GROUPS, 3, 8, 128),
        compiler_params=params(),
        cost_estimate=wave_cost,
        name="analysis",
    )(adjoint, high, low)
    spec = exchange(spec.reshape(WAVES, 24 * GROUPS, 128), "wave")

    modes = pl.pallas_call(
        legendre_adjoint_kernel,
        in_specs=[whole(WAVES, 168, 128), hbm],
        out_specs=whole(BANDS, 48, 128),
        out_shape=shape(BANDS, 48, 128),
        scratch_shapes=[pltpu.VMEM((336, NLAT), f32), *table_scratch],
        compiler_params=params(),
        cost_estimate=legendre_cost,
        name="legendre_adjoint",
    )(spec, in_hbm(legendre))
    modes = exchange(modes, "band").reshape(24, 4, 8, 128)

    gradient = pl.pallas_call(
        unmix_kernel,
        out_shape=shape(28, 16, 192),
        compiler_params=params(),
        cost_estimate=cost(6 * 448 * 192 * 192, 1 << 20),
        name="unmix",
    )(modes, control, scale, vertical_root)
    return jnp.swapaxes(gradient, 0, 1), state


def solution(mesh):
    both = ("wave", "band")
    placed = (
        P("band", "wave", None),
        P("band", "wave", None),
        P(),
        P("wave", None, None),
        P(),
        P("band", None, "wave"),
        P(),
        P(),
        P(both, None),
        P(both, None),
        P(both, None),
        P(both, None),
        P(both, None),
        P(both, None),
    )
    return jax.shard_map(
        body,
        mesh=mesh,
        in_specs=placed,
        out_specs=(P("band", "wave", None), P("band", None, "wave")),
        check_vma=False,
    )
```

```python
import math

import jax
import jax.numpy as jnp
from jax import lax
from jax.experimental import pallas as pl
from jax.experimental.pallas import tpu as pltpu
from jax.sharding import PartitionSpec as P

MW = 224
LEV = 8
BINS = 12
CH = 96
STEPS = 4
WAVES = 8
BANDS = 16
DEVICES = 128
SLOT = 128
GROUPS = 7
NLON = 1024
NLAT = 448
NT = 256
TILE = 21
FACTOR = MW ** (-0.5)
f32 = jnp.float32
bf16 = jnp.bfloat16
highest = lax.Precision.HIGHEST
LIMIT = 24 << 20


def params(**kw):
    return pltpu.CompilerParams(vmem_limit_bytes=LIMIT, **kw)


def split(x):
    hi = x.astype(bf16)
    return hi, (x - hi.astype(f32)).astype(bf16)


def mm(a, b):
    return lax.dot_general(a, b, (((1,), (0,)), ((), ())), preferred_element_type=f32)


def mm_nt(a, b):
    return lax.dot_general(a, b, (((1,), (1,)), ((), ())), preferred_element_type=f32)


def iota(shape, dim):
    return lax.broadcasted_iota(jnp.int32, shape, dim)


def turn(parts, axis, width):
    n = len(parts)
    size = parts[0].shape[axis]
    at = iota(parts[0].shape, axis)
    step = n // 2
    while step:
        keep = (at // (step * width)) % 2 == 0
        new = list(parts)
        for i in range(n):
            if (i // step) % 2 == 0:
                a, b = parts[i], parts[i + step]
                new[i] = jnp.where(keep, a, pltpu.roll(b, step * width, axis))
                new[i + step] = jnp.where(keep, pltpu.roll(a, size - step * width, axis), b)
        parts = new
        step //= 2
    return parts


def doubled_root(root):
    rows = (iota((2 * CH, CH), 0) // 2 == iota((2 * CH, CH), 1)).astype(f32)
    cols = (iota((CH, 2 * CH), 1) // 2 == iota((CH, 2 * CH), 0)).astype(f32)
    wide = jnp.dot(rows, root, precision=highest, preferred_element_type=f32)
    wide = jnp.dot(wide, cols, precision=highest, preferred_element_type=f32)
    same = iota((2 * CH, 2 * CH), 0) % 2 == iota((2 * CH, 2 * CH), 1) % 2
    return jnp.where(same, wide, 0.0)


def mix_kernel(
    control_hbm,
    scale_hbm,
    root_hbm,
    column_hbm,
    level_hbm,
    lidar_hbm,
    aod_hbm,
    weight_hbm,
    count_hbm,
    out_hbm,
    out_ref,
    control_ref,
    scale_ref,
    root_ref,
    index_ref,
    value_ref,
    count_ref,
    obs_ref,
    sem,
):
    copies = [
        pltpu.make_async_copy(source, target, sem.at[k])
        for k, (source, target) in enumerate(
            (
                (root_hbm, root_ref),
                (control_hbm, control_ref),
                (scale_hbm, scale_ref),
                (column_hbm, index_ref.at[0]),
                (level_hbm, index_ref.at[1]),
                (lidar_hbm, value_ref.at[0]),
                (aod_hbm, value_ref.at[1]),
                (weight_hbm, value_ref.at[2]),
                (count_hbm, count_ref),
            )
        )
    ]
    for copy in copies[3:] + copies[:3]:
        copy.start()
    for copy in copies[3:]:
        copy.wait()
    counts = jnp.broadcast_to(count_ref[...].astype(f32), (DEVICES, DEVICES)).T
    live = iota((DEVICES, SLOT), 1).astype(f32) < counts
    weight = jnp.where(live, value_ref[2], 0.0)
    obs_ref[0] = index_ref[0].astype(f32)
    obs_ref[1] = index_ref[1].astype(f32)
    obs_ref[2] = weight
    obs_ref[3] = weight * value_ref[0]
    obs_ref[4] = weight * value_ref[1]
    for band in range(BANDS):
        for k in range(5):
            rows = obs_ref[k, pl.ds(band, WAVES, stride=BANDS), :]
            out_ref[band, 48 + 8 * k : 56 + 8 * k] = rows
    done = []
    for k, at in enumerate((pl.ds(48, 40), pl.ds(0, 48))):
        done.append(pltpu.make_async_copy(out_ref.at[:, at], out_hbm.at[:, at], sem.at[9 + k]))
    done[0].start()

    for copy in copies[:3]:
        copy.wait()
    root = doubled_root(root_ref[...])
    rh, rl = split(root)
    tiles = []
    for m4 in range(4):
        x = jnp.concatenate([control_ref[4 * g + m4] for g in range(GROUPS)], axis=0)
        s = jnp.concatenate([scale_ref[4 * g + m4] for g in range(GROUPS)], axis=0)
        xh, xl = split(x)
        y = (mm(xh, rh) + mm(xl, rh) + mm(xh, rl)) * s
        y = jnp.concatenate([y, jnp.zeros((16, 2 * CH), f32)], axis=0)
        tiles.append(y.T.reshape(24, 8, 128))
    for j, z in enumerate(turn(tiles, 1, 2)):
        for h in range(24):
            c = 4 * h + j
            out_ref[c // 6, 8 * (c % 6) : 8 * (c % 6) + 8] = z[h]
    done[1].start()
    for copy in done:
        copy.wait()


def table_copies(table_hbm, table_ref, sem):
    copies = []
    for g in range(GROUPS):
        at = pl.ds(4 * g, 4)
        copies.append(pltpu.make_async_copy(table_hbm.at[at], table_ref.at[at], sem.at[g]))
    for copy in copies:
        copy.start()
    return copies


def legendre_kernel(modes_ref, table_hbm, out_ref, x_ref, acc_ref, table_ref, sem):
    copies = table_copies(table_hbm, table_ref, sem)
    for half in range(2):
        for c in range(6):
            got = [modes_ref[8 * half + s, 8 * c : 8 * c + 8] for s in range(8)]
            for g, z in enumerate(turn(got, 1, 16)):
                if g < GROUPS:
                    x_ref[g, 8 * c : 8 * c + 8, 128 * half : 128 * half + 128] = z
    for k in range(5):
        for half in range(2):
            got = [modes_ref[8 * half + s, 48 + 8 * k : 56 + 8 * k] for s in range(8)]
            at = 168 + 16 * k + 8 * half
            for w, z in enumerate(turn(got, 0, 1)):
                out_ref[w, at : at + 8] = z

    slot = (iota((48, NT), 0) % 8) // 2
    order = lat_order()
    for g in range(GROUPS):
        copies[g].wait()
        x = x_ref[g]
        acc = None
        for m4 in range(4):
            xh, xl = split(jnp.where(slot == m4, x, 0.0))
            both = jnp.concatenate(split(table_ref[4 * g + m4]), axis=0)
            both = mm_nt(jnp.concatenate([xh, xl], axis=0), both)
            part = both[:48, :NLAT] + (both[48:, :NLAT] + both[:48, NLAT:])
            acc = part if acc is None else acc + part
        acc_ref[g] = acc
        for first, last in ((0, 5), (5, 7)):
            if g + 1 == last:
                rows = 48 * (last - first)
                part = acc_ref[first:last].reshape(rows, NLAT)
                both = mm(jnp.concatenate(split(part), axis=0), order)
                out = both[:rows] + both[rows:]
                for k in range(first, last):
                    for q in range(4):
                        for hc in range(2):
                            at = 48 * (k - first) + 24 * hc
                            tile = out[at : at + 24, 128 * q : 128 * q + 128]
                            out_ref[2 * q + hc, 24 * k : 24 * k + 24] = tile


def lat_order():
    at = iota((NLAT, 512), 1)
    lat = ((at // 8) % 16) * 28 + (at // 128) * 7 + at % 8
    return jnp.where((iota((NLAT, 512), 0) == lat) & (at % 8 < 7), 1.0, 0.0).astype(bf16)


def wave_table_kernel(number_ref, high_ref, low_ref):
    rows = 16
    half = NLON // 2
    row = iota((rows, MW), 0)
    slot = iota((rows, MW), 1)
    part = iota((rows, half), 0) % 2
    lon = iota((rows, half), 1)
    numbers = number_ref[...].astype(f32)
    coefs = [(-1.0) ** k / math.factorial(2 * k + 1) for k in range(6)]

    @pl.loop(0, 2 * MW // rows)
    def _(i):
        first = pl.multiple_of(i * rows, rows)
        mine = (row + first) // 2 == slot
        n = jnp.sum(jnp.where(mine, numbers, 0.0), axis=1, keepdims=True).astype(jnp.int32)
        phase = (n * lon + 256 * part) & (NLON - 1)
        turn_at = (jnp.abs(phase - half) - half // 2).astype(f32)
        y = turn_at * (2.0 * math.pi / NLON)
        y2 = y * y
        value = coefs[5]
        for k in range(4, -1, -1):
            value = value * y2 + coefs[k]
        value = value * y * FACTOR
        vh, vl = split(value)
        high_ref[pl.ds(first, rows), :half] = vh
        low_ref[pl.ds(first, rows), :half] = vl
        sign = (1 - 2 * (n & 1)).astype(f32)
        vh, vl = split(value * sign)
        high_ref[pl.ds(first, rows), half:] = vh
        low_ref[pl.ds(first, rows), half:] = vl


def synthesis_kernel(spec_ref, high_ref, low_ref, out_ref, lhs_ref):
    rows = spec_ref[:, :168].reshape(WAVES, GROUPS, 3, 8, 128)
    for c in range(3):
        high, low = split(rows[:, :, c].reshape(2 * MW, 128).T)
        lhs_ref[128 * c : 128 * c + 128] = high
        lhs_ref[384 + 128 * c : 512 + 128 * c] = low
    for i in range(4):
        lon = pl.ds(256 * i, 256)
        both = mm(lhs_ref[...], high_ref[:, lon])
        out = both[:384] + both[384:] + mm(lhs_ref[:384], low_ref[:, lon])
        for w in range(2):
            for band in range(BANDS):
                for c in range(3):
                    row = 128 * c + 8 * band
                    at = TILE * (BANDS * (2 * i + w) + band) + 7 * c
                    out_ref[at : at + 7] = out[row : row + 7, 128 * w : 128 * w + 128]


def analysis_kernel(grid_ref, high_ref, low_ref, out_ref):
    blank = jnp.zeros((1, 128), f32)
    total = None
    for i in range(4):
        tiles = []
        for c in range(3):
            parts = []
            for w in range(2):
                rows = []
                for band in range(BANDS):
                    at = TILE * (BANDS * (2 * i + w) + band) + 7 * c
                    rows += [grid_ref[at : at + 7], blank]
                parts.append(jnp.concatenate(rows, axis=0))
            tiles.append(jnp.concatenate(parts, axis=1))
        gh, gl = split(jnp.concatenate(tiles, axis=0))
        lon = pl.ds(256 * i, 256)
        both = mm_nt(high_ref[:, lon], jnp.concatenate([gh, gl], axis=0))
        part = both[:, :384] + both[:, 384:] + mm_nt(low_ref[:, lon], gh)
        total = part if total is None else total + part
    for c in range(3):
        rows = total[:, 128 * c : 128 * c + 128]
        out_ref[:, :, c] = rows.reshape(WAVES, GROUPS, 8, 128)


def legendre_adjoint_kernel(spec_ref, table_hbm, out_ref, acc_ref, table_ref, sem):
    copies = table_copies(table_hbm, table_ref, sem)
    order = lat_order()
    for hc in range(2):
        s = jnp.concatenate([spec_ref[2 * q + hc] for q in range(4)], axis=1)
        sh, sl = split(s)
        acc_ref[168 * hc : 168 * hc + 168] = mm_nt(sh, order) + mm_nt(sl, order)
    slot = (iota((48, NLAT), 0) % 8) // 2
    x = []
    for g in range(GROUPS):
        copies[g].wait()
        rows = [acc_ref[168 * hc + 24 * g : 168 * hc + 24 * g + 24] for hc in range(2)]
        mine = jnp.concatenate(rows, axis=0)
        acc = None
        for m4 in range(4):
            xh, xl = split(jnp.where(slot == m4, mine, 0.0))
            th, tl = split(table_ref[4 * g + m4])
            both = mm(jnp.concatenate([xh, xl], axis=0), th)
            part = both[:48] + both[48:] + mm(xh, tl)
            acc = part if acc is None else acc + part
        x.append(acc)
    x.append(jnp.zeros((48, NT), f32))
    for half in range(2):
        for c in range(6):
            got = [v[8 * c : 8 * c + 8, 128 * half : 128 * half + 128] for v in x]
            for s, z in enumerate(turn(got, 1, 16)):
                out_ref[8 * half + s, 8 * c : 8 * c + 8] = z


def unmix_kernel(modes_ref, control_ref, scale_ref, root_ref, out_ref):
    root = doubled_root(root_ref[...])
    rh, rl = split(root)
    tiles = turn([modes_ref[:, j] for j in range(4)], 1, 2)
    for m4 in range(4):
        y = tiles[m4].reshape(2 * CH, 128).T[: 16 * GROUPS]
        s = jnp.concatenate([scale_ref[4 * g + m4] for g in range(GROUPS)], axis=0)
        yh, yl = split(y * s)
        z = mm_nt(yh, rh) + mm_nt(yl, rh) + mm_nt(yh, rl)
        for g in range(GROUPS):
            m = 4 * g + m4
            out_ref[m] = control_ref[m] + z[16 * g : 16 * g + 16]


def sums_kernel(obs_ref, out_ref, acc_ref):
    i = pl.program_id(0)
    part = None
    for half in range(2):

        def line(k):
            at = 168 + 16 * k + 8 * half
            rows = obs_ref[0, at : at + 8]
            return jnp.concatenate([rows[s : s + 1] for s in range(8)], axis=1)

        column = line(0).astype(jnp.int32)
        level = line(1).astype(jnp.int32)
        lat = column // 128
        lon = column % 128
        q = sum((lat >= 7 * k).astype(jnp.int32) for k in range(1, 4))
        row = q * 64 + level * 8 + (lat - 7 * q)
        rows = jnp.where(iota((256, 1024), 0) == row, 1.0, 0.0).astype(bf16)
        cols = jnp.where(iota((128, 1024), 0) == lon, 1.0, 0.0).astype(bf16)
        values = []
        for k in range(2, 5):
            for v in split(line(k)):
                values.append(cols * v)
        new = mm_nt(rows, jnp.concatenate(values, axis=0))
        part = new if part is None else part + new

    @pl.when(i == 0)
    def _():
        acc_ref[...] = part

    @pl.when(i > 0)
    def _():
        acc_ref[...] += part

    @pl.when(i == WAVES - 1)
    def _():
        for k in range(3):
            first = acc_ref[:, 256 * k : 256 * k + 128]
            out_ref[k] = first + acc_ref[:, 256 * k + 128 : 256 * k + 256]


def flow_kernel(courant_ref, out_ref):
    for h in range(12):
        rows = [courant_ref[min(t, 6), 8 * h : 8 * h + 8] for t in range(8)]
        for j, z in enumerate(turn(rows, 0, 1)):
            out_ref[8 * h + j] = z


def grid_kernel(
    grid_ref, flow_ref, sums_ref, lidar_ref, aod_ref, state_ref, adjoint_ref, hold_ref
):
    def tile_rows(l, b2, hc, c):
        return pl.ds(TILE * (BANDS * hc + 2 * l + b2) + 7 * c, 7)

    blank = jnp.zeros((1, 128), f32)
    chains = [(b2, hc, c) for b2 in range(2) for hc in range(2) for c in range(3)]
    lidar_sum = [None] * LEV
    aod_sum = None
    for b2, hc, c in chains:
        bin_at = b2 * 6 + hc * 3 + c
        x = [
            jnp.concatenate([grid_ref[tile_rows(l, b2, hc, c)], blank], axis=0)
            for l in range(LEV)
        ]
        flow = [flow_ref[BINS * l + bin_at] for l in range(LEV)]
        for step in range(STEPS):
            out = [flow[l] * x[l] for l in range(LEV)]
            x = [x[l] - out[l] if l == 0 else x[l] - out[l] + out[l - 1] for l in range(LEV)]
        coef = lidar_ref[bin_at]
        for l in range(LEV):
            hold_ref[BINS * l + bin_at] = x[l]
            lidar_sum[l] = x[l] * coef if lidar_sum[l] is None else lidar_sum[l] + x[l] * coef
            term = x[l] * aod_ref[BINS * l + bin_at]
            aod_sum = term if aod_sum is None else aod_sum + term

    for h in range(12):
        rows = turn([hold_ref[8 * h + j] for j in range(8)], 0, 1)
        for t in range(7):
            state_ref[t, 8 * h : 8 * h + 8] = rows[t]

    weight = [sums_ref[0, 8 * l : 8 * l + 8] for l in range(LEV)]
    lidar = [weight[l] * lidar_sum[l] - sums_ref[1, 8 * l : 8 * l + 8] for l in range(LEV)]
    aod = sum(weight[1:], weight[0]) * aod_sum
    for l in range(LEV):
        aod = aod - sums_ref[2, 8 * l : 8 * l + 8]
    for b2, hc, c in chains:
        bin_at = b2 * 6 + hc * 3 + c
        coef = lidar_ref[bin_at]
        flow = [flow_ref[BINS * l + bin_at] for l in range(LEV)]
        a = [lidar[l] * coef + aod * aod_ref[BINS * l + bin_at] for l in range(LEV)]
        for step in range(STEPS):
            a = [
                a[l] + flow[l] * ((a[l + 1] - a[l]) if l + 1 < LEV else -a[l]) for l in range(LEV)
            ]
        for l in range(LEV):
            adjoint_ref[tile_rows(l, b2, hc, c)] = a[l][:7]


def shape(*lengths, kind=f32):
    return jax.ShapeDtypeStruct(lengths, kind)


def whole(*lengths):
    return pl.BlockSpec(lengths, lambda *_: (0,) * len(lengths))


def in_hbm(x):
    return pltpu.with_memory_space_constraint(x, pltpu.HBM)


def cost(flops, size):
    return pl.CostEstimate(flops=flops, bytes_accessed=size, transcendentals=0)


def exchange(tiles, axis):
    return lax.all_to_all(tiles, axis, split_axis=0, concat_axis=0, tiled=True)


def exchange_tiles(tiles):
    rows = tiles.reshape(DEVICES, 1, TILE * 128)
    return exchange(rows, ("wave", "band")).reshape(DEVICES * TILE, 128)


def body(
    control,
    spectral_scale,
    vertical_root,
    legendre,
    zonal_number,
    courant,
    lidar_coef,
    aod_coef,
    obs_count,
    obs_column,
    obs_level,
    lidar_obs,
    aod_obs,
    obs_weight,
):
    control = jnp.swapaxes(control, 0, 1)
    scale = jnp.swapaxes(spectral_scale, 0, 1)
    hbm = pl.BlockSpec(memory_space=pltpu.HBM)
    modes = pl.pallas_call(
        mix_kernel,
        in_specs=[hbm] * 9,
        out_specs=pl.BlockSpec(memory_space=pl.ANY),
        out_shape=shape(BANDS, 88, 128),
        scratch_shapes=[
            pltpu.VMEM((BANDS, 88, 128), f32),
            pltpu.VMEM((28, 16, 192), f32),
            pltpu.VMEM((28, 16, 192), f32),
            pltpu.VMEM((CH, CH), f32),
            pltpu.VMEM((2, DEVICES, SLOT), jnp.int32),
            pltpu.VMEM((3, DEVICES, SLOT), f32),
            pltpu.VMEM((1, DEVICES), jnp.int32),
            pltpu.VMEM((5, DEVICES, SLOT), f32),
            pltpu.SemaphoreType.DMA((11,)),
        ],
        compiler_params=params(),
        cost_estimate=cost(6 * 448 * 192 * 192, 1 << 20),
        name="mix",
    )(
        *(
            in_hbm(x)
            for x in (
                control,
                scale,
                vertical_root,
                obs_column,
                obs_level,
                lidar_obs,
                aod_obs,
                obs_weight,
                obs_count,
            )
        )
    )
    waves = pl.pallas_call(
        wave_table_kernel,
        out_shape=(shape(2 * MW, NLON, kind=bf16), shape(2 * MW, NLON, kind=bf16)),
        compiler_params=params(),
        cost_estimate=cost(20 * 448 * 1024, 2 << 20),
        name="wave_table",
    )(zonal_number.reshape(1, MW))
    modes, (high, low) = lax.optimization_barrier((exchange(modes, "band"), waves))

    legendre_cost = cost(6 * 28 * 448 * 256 * 48, 14 << 20)
    in_order = params(dimension_semantics=("arbitrary",))
    table_scratch = [pltpu.VMEM((28, NLAT, NT), f32), pltpu.SemaphoreType.DMA((GROUPS,))]
    spec = pl.pallas_call(
        legendre_kernel,
        in_specs=[whole(BANDS, 88, 128), hbm],
        out_specs=whole(WAVES, 248, 128),
        out_shape=shape(WAVES, 248, 128),
        scratch_shapes=[
            pltpu.VMEM((GROUPS, 48, NT), f32),
            pltpu.VMEM((GROUPS, 48, NLAT), f32),
            *table_scratch,
        ],
        compiler_params=params(),
        cost_estimate=legendre_cost,
        name="legendre",
    )(modes, in_hbm(legendre))
    spec = exchange(spec, "wave")
    sums = pl.pallas_call(
        sums_kernel,
        grid=(WAVES,),
        in_specs=[pl.BlockSpec((1, 248, 128), lambda i: (i, 0, 0))],
        out_specs=whole(3, 256, 128),
        out_shape=shape(3, 256, 128),
        scratch_shapes=[pltpu.VMEM((256, 768), f32)],
        compiler_params=in_order,
        cost_estimate=cost(2 * 16384 * 256 * 768, 1 << 20),
        name="sums",
    )(spec)

    tile_spec = pl.BlockSpec((2 * BANDS * TILE, 128), lambda i: (i, 0))
    tiles = shape(DEVICES * TILE, 128)
    wave_cost = cost(6 * 384 * 448 * 1024, 4 << 20)
    grid = pl.pallas_call(
        synthesis_kernel,
        out_shape=tiles,
        scratch_shapes=[pltpu.VMEM((768, 2 * MW), bf16)],
        compiler_params=params(),
        cost_estimate=wave_cost,
        name="synthesis",
    )(spec, high, low)
    grid = exchange_tiles(grid)

    field = pl.BlockSpec((7, CH, 128), lambda q: (q, 0, 0))
    scalars = pl.BlockSpec(memory_space=pltpu.SMEM)
    turned = pl.BlockSpec((CH, 8, 128), lambda q: (q, 0, 0))
    flow = pl.pallas_call(
        flow_kernel,
        grid=(4,),
        in_specs=[field],
        out_specs=turned,
        out_shape=shape(4 * CH, 8, 128),
        compiler_params=in_order,
        cost_estimate=cost(6 * 28 * 96 * 128, 3 << 20),
        name="flow",
    )(in_hbm(courant))
    state, adjoint = pl.pallas_call(
        grid_kernel,
        grid=(4,),
        in_specs=[
            tile_spec,
            turned,
            pl.BlockSpec((3, 64, 128), lambda q: (0, q, 0)),
            scalars,
            scalars,
        ],
        out_specs=(field, tile_spec),
        out_shape=(shape(28, CH, 128), tiles),
        scratch_shapes=[pltpu.VMEM((CH, 8, 128), f32)],
        compiler_params=in_order,
        cost_estimate=cost(40 * 28 * 96 * 128, 6 << 20),
        name="grid_steps",
    )(grid, flow, in_hbm(sums), lidar_coef, aod_coef)
    adjoint = exchange_tiles(adjoint)

    spec = pl.pallas_call(
        analysis_kernel,
        out_shape=shape(WAVES, GROUPS, 3, 8, 128),
        compiler_params=params(),
        cost_estimate=wave_cost,
        name="analysis",
    )(adjoint, high, low)
    spec = exchange(spec.reshape(WAVES, 24 * GROUPS, 128), "wave")

    modes = pl.pallas_call(
        legendre_adjoint_kernel,
        in_specs=[whole(WAVES, 168, 128), hbm],
        out_specs=whole(BANDS, 48, 128),
        out_shape=shape(BANDS, 48, 128),
        scratch_shapes=[pltpu.VMEM((336, NLAT), f32), *table_scratch],
        compiler_params=params(),
        cost_estimate=legendre_cost,
        name="legendre_adjoint",
    )(spec, in_hbm(legendre))
    modes = exchange(modes, "band").reshape(24, 4, 8, 128)

    gradient = pl.pallas_call(
        unmix_kernel,
        out_shape=shape(28, 16, 192),
        compiler_params=params(),
        cost_estimate=cost(6 * 448 * 192 * 192, 1 << 20),
        name="unmix",
    )(modes, control, scale, vertical_root)
    return jnp.swapaxes(gradient, 0, 1), state


def solution(mesh):
    both = ("wave", "band")
    placed = (
        P("band", "wave", None),
        P("band", "wave", None),
        P(),
        P("wave", None, None),
        P(),
        P("band", None, "wave"),
        P(),
        P(),
        P(both, None),
        P(both, None),
        P(both, None),
        P(both, None),
        P(both, None),
        P(both, None),
    )
    return jax.shard_map(
        body,
        mesh=mesh,
        in_specs=placed,
        out_specs=(P("band", "wave", None), P("band", None, "wave")),
        check_vma=False,
    )
```

```python
import math

import jax
import jax.numpy as jnp
from jax import lax
from jax.experimental import pallas as pl
from jax.experimental.pallas import tpu as pltpu
from jax.sharding import PartitionSpec as P

MW = 224
LEV = 8
BINS = 12
CH = 96
STEPS = 4
WAVES = 8
BANDS = 16
DEVICES = 128
SLOT = 128
GROUPS = 7
NLON = 1024
NLAT = 448
NT = 256
TILE = 21
FACTOR = MW ** (-0.5)
f32 = jnp.float32
bf16 = jnp.bfloat16
highest = lax.Precision.HIGHEST
LIMIT = 24 << 20


def params(**kw):
    return pltpu.CompilerParams(vmem_limit_bytes=LIMIT, **kw)


def split(x):
    hi = x.astype(bf16)
    return hi, (x - hi.astype(f32)).astype(bf16)


def mm(a, b):
    return lax.dot_general(a, b, (((1,), (0,)), ((), ())), preferred_element_type=f32)


def mm_nt(a, b):
    return lax.dot_general(a, b, (((1,), (1,)), ((), ())), preferred_element_type=f32)


def iota(shape, dim):
    return lax.broadcasted_iota(jnp.int32, shape, dim)


def turn(parts, axis, width):
    n = len(parts)
    size = parts[0].shape[axis]
    at = iota(parts[0].shape, axis)
    step = n // 2
    while step:
        keep = (at // (step * width)) % 2 == 0
        new = list(parts)
        for i in range(n):
            if (i // step) % 2 == 0:
                a, b = parts[i], parts[i + step]
                new[i] = jnp.where(keep, a, pltpu.roll(b, step * width, axis))
                new[i + step] = jnp.where(keep, pltpu.roll(a, size - step * width, axis), b)
        parts = new
        step //= 2
    return parts


def doubled_root(root):
    rows = (iota((2 * CH, CH), 0) // 2 == iota((2 * CH, CH), 1)).astype(f32).astype(bf16)
    cols = (iota((CH, 2 * CH), 1) // 2 == iota((CH, 2 * CH), 0)).astype(f32).astype(bf16)
    same = iota((2 * CH, 2 * CH), 0) % 2 == iota((2 * CH, 2 * CH), 1) % 2
    parts = []
    for part in split(root):
        wide = mm(mm(rows, part).astype(bf16), cols)
        parts.append(jnp.where(same, wide, 0.0).astype(bf16))
    return parts


def mix_kernel(
    control_hbm,
    scale_hbm,
    root_hbm,
    column_hbm,
    level_hbm,
    lidar_hbm,
    aod_hbm,
    weight_hbm,
    count_hbm,
    out_hbm,
    out_ref,
    control_ref,
    scale_ref,
    root_ref,
    index_ref,
    value_ref,
    count_ref,
    obs_ref,
    sem,
):
    copies = [
        pltpu.make_async_copy(source, target, sem.at[k])
        for k, (source, target) in enumerate(
            (
                (root_hbm, root_ref),
                (control_hbm, control_ref),
                (scale_hbm, scale_ref),
                (column_hbm, index_ref.at[0]),
                (level_hbm, index_ref.at[1]),
                (lidar_hbm, value_ref.at[0]),
                (aod_hbm, value_ref.at[1]),
                (weight_hbm, value_ref.at[2]),
                (count_hbm, count_ref),
            )
        )
    ]
    for copy in copies[3:] + copies[:3]:
        copy.start()
    for copy in copies[3:]:
        copy.wait()
    counts = jnp.broadcast_to(count_ref[...].astype(f32), (DEVICES, DEVICES)).T
    live = iota((DEVICES, SLOT), 1).astype(f32) < counts
    weight = jnp.where(live, value_ref[2], 0.0)
    obs_ref[0] = index_ref[0].astype(f32)
    obs_ref[1] = index_ref[1].astype(f32)
    obs_ref[2] = weight
    obs_ref[3] = weight * value_ref[0]
    obs_ref[4] = weight * value_ref[1]
    for band in range(BANDS):
        for k in range(5):
            rows = obs_ref[k, pl.ds(band, WAVES, stride=BANDS), :]
            out_ref[band, 48 + 8 * k : 56 + 8 * k] = rows
    done = []
    for k, at in enumerate((pl.ds(48, 40), pl.ds(0, 48))):
        done.append(pltpu.make_async_copy(out_ref.at[:, at], out_hbm.at[:, at], sem.at[9 + k]))
    done[0].start()

    for copy in copies[:3]:
        copy.wait()
    rh, rl = doubled_root(root_ref[...])
    tiles = []
    for m4 in range(4):
        x = jnp.concatenate([control_ref[4 * g + m4] for g in range(GROUPS)], axis=0)
        s = jnp.concatenate([scale_ref[4 * g + m4] for g in range(GROUPS)], axis=0)
        xh, xl = split(x)
        y = (mm(xh, rh) + mm(xl, rh) + mm(xh, rl)) * s
        y = jnp.concatenate([y, jnp.zeros((16, 2 * CH), f32)], axis=0)
        tiles.append(y.T.reshape(24, 8, 128))
    for j, z in enumerate(turn(tiles, 1, 2)):
        for h in range(24):
            c = 4 * h + j
            out_ref[c // 6, 8 * (c % 6) : 8 * (c % 6) + 8] = z[h]
    done[1].start()
    for copy in done:
        copy.wait()


def table_copies(table_hbm, table_ref, sem):
    copies = []
    for g in range(GROUPS):
        at = pl.ds(4 * g, 4)
        copies.append(pltpu.make_async_copy(table_hbm.at[at], table_ref.at[at], sem.at[g]))
    for copy in copies:
        copy.start()
    return copies


def legendre_kernel(modes_ref, table_hbm, out_ref, x_ref, acc_ref, table_ref, sem):
    copies = table_copies(table_hbm, table_ref, sem)
    for half in range(2):
        for c in range(6):
            got = [modes_ref[8 * half + s, 8 * c : 8 * c + 8] for s in range(8)]
            for g, z in enumerate(turn(got, 1, 16)):
                if g < GROUPS:
                    x_ref[g, 8 * c : 8 * c + 8, 128 * half : 128 * half + 128] = z
    for k in range(5):
        for half in range(2):
            got = [modes_ref[8 * half + s, 48 + 8 * k : 56 + 8 * k] for s in range(8)]
            at = 168 + 16 * k + 8 * half
            for w, z in enumerate(turn(got, 0, 1)):
                out_ref[w, at : at + 8] = z

    slot = (iota((48, NT), 0) % 8) // 2
    order = lat_order()
    for g in range(GROUPS):
        copies[g].wait()
        x = x_ref[g]
        acc = None
        for m4 in range(4):
            xh, xl = split(jnp.where(slot == m4, x, 0.0))
            both = jnp.concatenate(split(table_ref[4 * g + m4]), axis=0)
            both = mm_nt(jnp.concatenate([xh, xl], axis=0), both)
            part = both[:48, :NLAT] + (both[48:, :NLAT] + both[:48, NLAT:])
            acc = part if acc is None else acc + part
        acc_ref[g] = acc
        for first, last in ((0, 5), (5, 7)):
            if g + 1 == last:
                rows = 48 * (last - first)
                part = acc_ref[first:last].reshape(rows, NLAT)
                both = mm(jnp.concatenate(split(part), axis=0), order)
                out = both[:rows] + both[rows:]
                for k in range(first, last):
                    for q in range(4):
                        for hc in range(2):
                            at = 48 * (k - first) + 24 * hc
                            tile = out[at : at + 24, 128 * q : 128 * q + 128]
                            out_ref[2 * q + hc, 24 * k : 24 * k + 24] = tile


def lat_order():
    at = iota((NLAT, 512), 1)
    lat = ((at // 8) % 16) * 28 + (at // 128) * 7 + at % 8
    return jnp.where((iota((NLAT, 512), 0) == lat) & (at % 8 < 7), 1.0, 0.0).astype(bf16)


def wave_table_kernel(number_ref, high_ref, low_ref):
    rows = 16
    half = NLON // 2
    row = iota((rows, MW), 0)
    slot = iota((rows, MW), 1)
    part = iota((rows, half), 0) % 2
    lon = iota((rows, half), 1)
    numbers = number_ref[...].astype(f32)
    coefs = [(-1.0) ** k / math.factorial(2 * k + 1) for k in range(6)]

    @pl.loop(0, 2 * MW // rows)
    def _(i):
        first = pl.multiple_of(i * rows, rows)
        mine = (row + first) // 2 == slot
        n = jnp.sum(jnp.where(mine, numbers, 0.0), axis=1, keepdims=True).astype(jnp.int32)
        phase = (n * lon + 256 * part) & (NLON - 1)
        turn_at = (jnp.abs(phase - half) - half // 2).astype(f32)
        y = turn_at * (2.0 * math.pi / NLON)
        y2 = y * y
        value = coefs[5]
        for k in range(4, -1, -1):
            value = value * y2 + coefs[k]
        value = value * y * FACTOR
        vh, vl = split(value)
        high_ref[pl.ds(first, rows), :half] = vh
        low_ref[pl.ds(first, rows), :half] = vl
        sign = (1 - 2 * (n & 1)).astype(f32)
        vh, vl = split(value * sign)
        high_ref[pl.ds(first, rows), half:] = vh
        low_ref[pl.ds(first, rows), half:] = vl


def synthesis_kernel(spec_ref, high_ref, low_ref, out_hbm, out_ref, lhs_ref, sem):
    rows = spec_ref[:, :168].reshape(WAVES, GROUPS, 3, 8, 128)
    for c in range(3):
        high, low = split(rows[:, :, c].reshape(2 * MW, 128).T)
        lhs_ref[128 * c : 128 * c + 128] = high
        lhs_ref[384 + 128 * c : 512 + 128 * c] = low
    done = []
    for i in range(4):
        lon = pl.ds(256 * i, 256)
        both = mm(lhs_ref[...], high_ref[:, lon])
        out = both[:384] + both[384:] + mm(lhs_ref[:384], low_ref[:, lon])
        for w in range(2):
            for band in range(BANDS):
                for c in range(3):
                    row = 128 * c + 8 * band
                    at = TILE * (BANDS * (2 * i + w) + band) + 7 * c
                    out_ref[at : at + 7] = out[row : row + 7, 128 * w : 128 * w + 128]
        at = pl.ds(2 * BANDS * TILE * i, 2 * BANDS * TILE)
        done.append(pltpu.make_async_copy(out_ref.at[at], out_hbm.at[at], sem.at[i]))
        done[i].start()
    for copy in done:
        copy.wait()


def analysis_kernel(grid_ref, high_ref, low_ref, out_ref):
    blank = jnp.zeros((1, 128), f32)
    total = None
    for i in range(4):
        tiles = []
        for c in range(3):
            parts = []
            for w in range(2):
                rows = []
                for band in range(BANDS):
                    at = TILE * (BANDS * (2 * i + w) + band) + 7 * c
                    rows += [grid_ref[at : at + 7], blank]
                parts.append(jnp.concatenate(rows, axis=0))
            tiles.append(jnp.concatenate(parts, axis=1))
        gh, gl = split(jnp.concatenate(tiles, axis=0))
        lon = pl.ds(256 * i, 256)
        both = mm_nt(high_ref[:, lon], jnp.concatenate([gh, gl], axis=0))
        part = both[:, :384] + both[:, 384:] + mm_nt(low_ref[:, lon], gh)
        total = part if total is None else total + part
    for c in range(3):
        rows = total[:, 128 * c : 128 * c + 128]
        out_ref[:, :, c] = rows.reshape(WAVES, GROUPS, 8, 128)


def legendre_adjoint_kernel(spec_ref, table_hbm, out_ref, acc_ref, table_ref, sem):
    copies = table_copies(table_hbm, table_ref, sem)
    order = lat_order()
    for hc in range(2):
        s = jnp.concatenate([spec_ref[2 * q + hc] for q in range(4)], axis=1)
        sh, sl = split(s)
        acc_ref[168 * hc : 168 * hc + 168] = mm_nt(sh, order) + mm_nt(sl, order)
    slot = (iota((48, NLAT), 0) % 8) // 2
    x = []
    for g in range(GROUPS):
        copies[g].wait()
        rows = [acc_ref[168 * hc + 24 * g : 168 * hc + 24 * g + 24] for hc in range(2)]
        mine = jnp.concatenate(rows, axis=0)
        acc = None
        for m4 in range(4):
            xh, xl = split(jnp.where(slot == m4, mine, 0.0))
            th, tl = split(table_ref[4 * g + m4])
            both = mm(jnp.concatenate([xh, xl], axis=0), th)
            part = both[:48] + both[48:] + mm(xh, tl)
            acc = part if acc is None else acc + part
        x.append(acc)
    x.append(jnp.zeros((48, NT), f32))
    for half in range(2):
        for c in range(6):
            got = [v[8 * c : 8 * c + 8, 128 * half : 128 * half + 128] for v in x]
            for s, z in enumerate(turn(got, 1, 16)):
                out_ref[8 * half + s, 8 * c : 8 * c + 8] = z


def unmix_kernel(modes_ref, control_ref, scale_ref, root_ref, out_ref):
    rh, rl = doubled_root(root_ref[...])
    tiles = turn([modes_ref[:, j] for j in range(4)], 1, 2)
    for m4 in range(4):
        y = tiles[m4].reshape(2 * CH, 128).T[: 16 * GROUPS]
        s = jnp.concatenate([scale_ref[4 * g + m4] for g in range(GROUPS)], axis=0)
        yh, yl = split(y * s)
        z = mm_nt(yh, rh) + mm_nt(yl, rh) + mm_nt(yh, rl)
        for g in range(GROUPS):
            m = 4 * g + m4
            out_ref[m] = control_ref[m] + z[16 * g : 16 * g + 16]


def sums_kernel(obs_ref, out_ref, acc_ref):
    i = pl.program_id(0)
    part = None
    for half in range(2):

        def line(k):
            at = 168 + 16 * k + 8 * half
            rows = obs_ref[0, at : at + 8]
            return jnp.concatenate([rows[s : s + 1] for s in range(8)], axis=1)

        column = line(0).astype(jnp.int32)
        level = line(1).astype(jnp.int32)
        lat = column // 128
        lon = column % 128
        q = sum((lat >= 7 * k).astype(jnp.int32) for k in range(1, 4))
        row = q * 64 + level * 8 + (lat - 7 * q)
        rows = jnp.where(iota((256, 1024), 0) == row, 1.0, 0.0).astype(bf16)
        cols = jnp.where(iota((128, 1024), 0) == lon, 1.0, 0.0).astype(bf16)
        values = []
        for k in range(2, 5):
            for v in split(line(k)):
                values.append(cols * v)
        new = mm_nt(rows, jnp.concatenate(values, axis=0))
        part = new if part is None else part + new

    @pl.when(i == 0)
    def _():
        acc_ref[...] = part

    @pl.when(i > 0)
    def _():
        acc_ref[...] += part

    @pl.when(i == WAVES - 1)
    def _():
        for k in range(3):
            first = acc_ref[:, 256 * k : 256 * k + 128]
            out_ref[k] = first + acc_ref[:, 256 * k + 128 : 256 * k + 256]


def flow_kernel(courant_ref, out_ref):
    for h in range(12):
        rows = [courant_ref[min(t, 6), 8 * h : 8 * h + 8] for t in range(8)]
        for j, z in enumerate(turn(rows, 0, 1)):
            out_ref[8 * h + j] = z


def grid_kernel(
    grid_ref,
    flow_ref,
    sums_hbm,
    lidar_ref,
    aod_ref,
    state_hbm,
    adjoint_ref,
    hold_ref,
    state_ref,
    sums_ref,
    sem,
):
    fetch = pltpu.make_async_copy(sums_hbm, sums_ref, sem.at[4])
    fetch.start()

    def tile_rows(l, b2, hc, c):
        return pl.ds(TILE * (BANDS * hc + 2 * l + b2) + 7 * c, 7)

    def store(q):
        target = state_hbm.at[pl.ds(7 * q, 7)]
        return pltpu.make_async_copy(state_ref.at[q], target, sem.at[q])

    blank = jnp.zeros((1, 128), f32)
    chains = [(b2, hc, c) for b2 in range(2) for hc in range(2) for c in range(3)]

    @pl.loop(0, 4)
    def _(q):
        lidar_sum = [None] * LEV
        aod_sum = None
        for b2, hc, c in chains:
            bin_at = b2 * 6 + hc * 3 + c
            x = [
                jnp.concatenate([grid_ref[q, tile_rows(l, b2, hc, c)], blank], axis=0)
                for l in range(LEV)
            ]
            flow = [flow_ref[q, BINS * l + bin_at] for l in range(LEV)]
            for step in range(STEPS):
                out = [flow[l] * x[l] for l in range(LEV)]
                x = [x[l] - out[l] if l == 0 else x[l] - out[l] + out[l - 1] for l in range(LEV)]
            coef = lidar_ref[bin_at]
            for l in range(LEV):
                hold_ref[BINS * l + bin_at] = x[l]
                term = x[l] * coef
                lidar_sum[l] = term if lidar_sum[l] is None else lidar_sum[l] + term
                term = x[l] * aod_ref[BINS * l + bin_at]
                aod_sum = term if aod_sum is None else aod_sum + term

        for h in range(12):
            rows = turn([hold_ref[8 * h + j] for j in range(8)], 0, 1)
            for t in range(7):
                state_ref[q, t, 8 * h : 8 * h + 8] = rows[t]
        store(q).start()

        @pl.when(q == 0)
        def _():
            fetch.wait()

        def sums(k, l):
            return sums_ref[k, pl.ds(pl.multiple_of(64 * q + 8 * l, 8), 8), :]

        weight = [sums(0, l) for l in range(LEV)]
        lidar = [weight[l] * lidar_sum[l] - sums(1, l) for l in range(LEV)]
        aod = sum(weight[1:], weight[0]) * aod_sum
        for l in range(LEV):
            aod = aod - sums(2, l)
        for b2, hc, c in chains:
            bin_at = b2 * 6 + hc * 3 + c
            coef = lidar_ref[bin_at]
            flow = [flow_ref[q, BINS * l + bin_at] for l in range(LEV)]
            a = [lidar[l] * coef + aod * aod_ref[BINS * l + bin_at] for l in range(LEV)]
            for step in range(STEPS):
                a = [
                    a[l] + flow[l] * ((a[l + 1] - a[l]) if l + 1 < LEV else -a[l])
                    for l in range(LEV)
                ]
            for l in range(LEV):
                adjoint_ref[q, tile_rows(l, b2, hc, c)] = a[l][:7]

    for q in range(4):
        store(q).wait()


def shape(*lengths, kind=f32):
    return jax.ShapeDtypeStruct(lengths, kind)


def whole(*lengths):
    return pl.BlockSpec(lengths, lambda *_: (0,) * len(lengths))


def in_hbm(x):
    return pltpu.with_memory_space_constraint(x, pltpu.HBM)


def cost(flops, size):
    return pl.CostEstimate(flops=flops, bytes_accessed=size, transcendentals=0)


def exchange(tiles, axis):
    return lax.all_to_all(tiles, axis, split_axis=0, concat_axis=0, tiled=True)


def exchange_tiles(tiles):
    rows = tiles.reshape(DEVICES, 1, TILE * 128)
    return exchange(rows, ("wave", "band")).reshape(DEVICES * TILE, 128)


def body(
    control,
    spectral_scale,
    vertical_root,
    legendre,
    zonal_number,
    courant,
    lidar_coef,
    aod_coef,
    obs_count,
    obs_column,
    obs_level,
    lidar_obs,
    aod_obs,
    obs_weight,
):
    control = jnp.swapaxes(control, 0, 1)
    scale = jnp.swapaxes(spectral_scale, 0, 1)
    hbm = pl.BlockSpec(memory_space=pltpu.HBM)
    modes = pl.pallas_call(
        mix_kernel,
        in_specs=[hbm] * 9,
        out_specs=pl.BlockSpec(memory_space=pl.ANY),
        out_shape=shape(BANDS, 88, 128),
        scratch_shapes=[
            pltpu.VMEM((BANDS, 88, 128), f32),
            pltpu.VMEM((28, 16, 192), f32),
            pltpu.VMEM((28, 16, 192), f32),
            pltpu.VMEM((CH, CH), f32),
            pltpu.VMEM((2, DEVICES, SLOT), jnp.int32),
            pltpu.VMEM((3, DEVICES, SLOT), f32),
            pltpu.VMEM((1, DEVICES), jnp.int32),
            pltpu.VMEM((5, DEVICES, SLOT), f32),
            pltpu.SemaphoreType.DMA((11,)),
        ],
        compiler_params=params(),
        cost_estimate=cost(6 * 448 * 192 * 192, 1 << 20),
        name="mix",
    )(
        *(
            in_hbm(x)
            for x in (
                control,
                scale,
                vertical_root,
                obs_column,
                obs_level,
                lidar_obs,
                aod_obs,
                obs_weight,
                obs_count,
            )
        )
    )
    waves = pl.pallas_call(
        wave_table_kernel,
        out_shape=(shape(2 * MW, NLON, kind=bf16), shape(2 * MW, NLON, kind=bf16)),
        compiler_params=params(),
        cost_estimate=cost(20 * 448 * 1024, 2 << 20),
        name="wave_table",
    )(zonal_number.reshape(1, MW))
    modes, (high, low) = lax.optimization_barrier((exchange(modes, "band"), waves))

    legendre_cost = cost(6 * 28 * 448 * 256 * 48, 14 << 20)
    in_order = params(dimension_semantics=("arbitrary",))
    table_scratch = [pltpu.VMEM((28, NLAT, NT), f32), pltpu.SemaphoreType.DMA((GROUPS,))]
    spec = pl.pallas_call(
        legendre_kernel,
        in_specs=[whole(BANDS, 88, 128), hbm],
        out_specs=whole(WAVES, 248, 128),
        out_shape=shape(WAVES, 248, 128),
        scratch_shapes=[
            pltpu.VMEM((GROUPS, 48, NT), f32),
            pltpu.VMEM((GROUPS, 48, NLAT), f32),
            *table_scratch,
        ],
        compiler_params=params(),
        cost_estimate=legendre_cost,
        name="legendre",
    )(modes, in_hbm(legendre))
    spec = exchange(spec, "wave")
    sums = pl.pallas_call(
        sums_kernel,
        grid=(WAVES,),
        in_specs=[pl.BlockSpec((1, 248, 128), lambda i: (i, 0, 0))],
        out_specs=whole(3, 256, 128),
        out_shape=shape(3, 256, 128),
        scratch_shapes=[pltpu.VMEM((256, 768), f32)],
        compiler_params=in_order,
        cost_estimate=cost(2 * 16384 * 256 * 768, 1 << 20),
        name="sums",
    )(spec)

    tiles = shape(DEVICES * TILE, 128)
    wave_cost = cost(6 * 384 * 448 * 1024, 4 << 20)
    grid = pl.pallas_call(
        synthesis_kernel,
        out_specs=pl.BlockSpec(memory_space=pl.ANY),
        out_shape=tiles,
        scratch_shapes=[
            pltpu.VMEM((DEVICES * TILE, 128), f32),
            pltpu.VMEM((768, 2 * MW), bf16),
            pltpu.SemaphoreType.DMA((4,)),
        ],
        compiler_params=params(),
        cost_estimate=wave_cost,
        name="synthesis",
    )(spec, high, low)
    grid = exchange_tiles(grid)

    field = pl.BlockSpec((7, CH, 128), lambda q: (q, 0, 0))
    scalars = pl.BlockSpec(memory_space=pltpu.SMEM)
    turned = pl.BlockSpec((CH, 8, 128), lambda q: (q, 0, 0))
    flow = pl.pallas_call(
        flow_kernel,
        grid=(4,),
        in_specs=[field],
        out_specs=turned,
        out_shape=shape(4 * CH, 8, 128),
        compiler_params=in_order,
        cost_estimate=cost(6 * 28 * 96 * 128, 3 << 20),
        name="flow",
    )(in_hbm(courant))
    quarters = (4, 2 * BANDS * TILE, 128)
    state, adjoint = pl.pallas_call(
        grid_kernel,
        in_specs=[whole(*quarters), whole(4, CH, 8, 128), hbm, scalars, scalars],
        out_specs=(pl.BlockSpec(memory_space=pl.ANY), whole(*quarters)),
        out_shape=(shape(28, CH, 128), shape(*quarters)),
        scratch_shapes=[
            pltpu.VMEM((CH, 8, 128), f32),
            pltpu.VMEM((4, 7, CH, 128), f32),
            pltpu.VMEM((3, 256, 128), f32),
            pltpu.SemaphoreType.DMA((5,)),
        ],
        compiler_params=params(),
        cost_estimate=cost(40 * 28 * 96 * 128, 6 << 20),
        name="grid_steps",
    )(
        grid.reshape(quarters),
        flow.reshape(4, CH, 8, 128),
        in_hbm(sums),
        lidar_coef,
        aod_coef,
    )
    adjoint = adjoint.reshape(DEVICES * TILE, 128)
    adjoint = exchange_tiles(adjoint)

    spec = pl.pallas_call(
        analysis_kernel,
        out_shape=shape(WAVES, GROUPS, 3, 8, 128),
        compiler_params=params(),
        cost_estimate=wave_cost,
        name="analysis",
    )(adjoint, high, low)
    spec = exchange(spec.reshape(WAVES, 24 * GROUPS, 128), "wave")

    modes = pl.pallas_call(
        legendre_adjoint_kernel,
        in_specs=[whole(WAVES, 168, 128), hbm],
        out_specs=whole(BANDS, 48, 128),
        out_shape=shape(BANDS, 48, 128),
        scratch_shapes=[pltpu.VMEM((336, NLAT), f32), *table_scratch],
        compiler_params=params(),
        cost_estimate=legendre_cost,
        name="legendre_adjoint",
    )(spec, in_hbm(legendre))
    modes = exchange(modes, "band").reshape(24, 4, 8, 128)

    gradient = pl.pallas_call(
        unmix_kernel,
        out_shape=shape(28, 16, 192),
        compiler_params=params(),
        cost_estimate=cost(6 * 448 * 192 * 192, 1 << 20),
        name="unmix",
    )(modes, control, scale, vertical_root)
    return jnp.swapaxes(gradient, 0, 1), state


def solution(mesh):
    both = ("wave", "band")
    placed = (
        P("band", "wave", None),
        P("band", "wave", None),
        P(),
        P("wave", None, None),
        P(),
        P("band", None, "wave"),
        P(),
        P(),
        P(both, None),
        P(both, None),
        P(both, None),
        P(both, None),
        P(both, None),
        P(both, None),
    )
    return jax.shard_map(
        body,
        mesh=mesh,
        in_specs=placed,
        out_specs=(P("band", "wave", None), P("band", None, "wave")),
        check_vma=False,
    )
```

```python
import math

import jax
import jax.numpy as jnp
from jax import lax
from jax.experimental import pallas as pl
from jax.experimental.pallas import tpu as pltpu
from jax.sharding import PartitionSpec as P

MW = 224
LEV = 8
BINS = 12
CH = 96
STEPS = 4
WAVES = 8
BANDS = 16
DEVICES = 128
SLOT = 128
GROUPS = 7
NLON = 1024
NLAT = 448
NT = 256
TILE = 21
FACTOR = MW ** (-0.5)
f32 = jnp.float32
bf16 = jnp.bfloat16
highest = lax.Precision.HIGHEST
LIMIT = 24 << 20


def params(**kw):
    return pltpu.CompilerParams(vmem_limit_bytes=LIMIT, **kw)


def split(x):
    hi = x.astype(bf16)
    return hi, (x - hi.astype(f32)).astype(bf16)


def mm(a, b):
    return lax.dot_general(a, b, (((1,), (0,)), ((), ())), preferred_element_type=f32)


def mm_nt(a, b):
    return lax.dot_general(a, b, (((1,), (1,)), ((), ())), preferred_element_type=f32)


def iota(shape, dim):
    return lax.broadcasted_iota(jnp.int32, shape, dim)


def turn(parts, axis, width):
    n = len(parts)
    size = parts[0].shape[axis]
    at = iota(parts[0].shape, axis)
    step = n // 2
    while step:
        keep = (at // (step * width)) % 2 == 0
        new = list(parts)
        for i in range(n):
            if (i // step) % 2 == 0:
                a, b = parts[i], parts[i + step]
                new[i] = jnp.where(keep, a, pltpu.roll(b, step * width, axis))
                new[i + step] = jnp.where(keep, pltpu.roll(a, size - step * width, axis), b)
        parts = new
        step //= 2
    return parts


def doubled_root(root):
    rows = (iota((2 * CH, CH), 0) // 2 == iota((2 * CH, CH), 1)).astype(f32).astype(bf16)
    cols = (iota((CH, 2 * CH), 1) // 2 == iota((CH, 2 * CH), 0)).astype(f32).astype(bf16)
    same = iota((2 * CH, 2 * CH), 0) % 2 == iota((2 * CH, 2 * CH), 1) % 2
    parts = []
    for part in split(root):
        wide = mm(mm(rows, part).astype(bf16), cols)
        parts.append(jnp.where(same, wide, 0.0).astype(bf16))
    return parts


def mix_kernel(
    control_hbm,
    scale_hbm,
    root_hbm,
    column_hbm,
    level_hbm,
    lidar_hbm,
    aod_hbm,
    weight_hbm,
    count_hbm,
    out_hbm,
    out_ref,
    control_ref,
    scale_ref,
    root_ref,
    index_ref,
    value_ref,
    count_ref,
    obs_ref,
    sem,
):
    copies = [
        pltpu.make_async_copy(source, target, sem.at[k])
        for k, (source, target) in enumerate(
            (
                (root_hbm, root_ref),
                (control_hbm, control_ref),
                (scale_hbm, scale_ref),
                (column_hbm, index_ref.at[0]),
                (level_hbm, index_ref.at[1]),
                (lidar_hbm, value_ref.at[0]),
                (aod_hbm, value_ref.at[1]),
                (weight_hbm, value_ref.at[2]),
                (count_hbm, count_ref),
            )
        )
    ]
    for copy in copies[3:] + copies[:3]:
        copy.start()
    for copy in copies[3:]:
        copy.wait()
    counts = jnp.broadcast_to(count_ref[...].astype(f32), (DEVICES, DEVICES)).T
    live = iota((DEVICES, SLOT), 1).astype(f32) < counts
    weight = jnp.where(live, value_ref[2], 0.0)
    obs_ref[0] = index_ref[0].astype(f32)
    obs_ref[1] = index_ref[1].astype(f32)
    obs_ref[2] = weight
    obs_ref[3] = weight * value_ref[0]
    obs_ref[4] = weight * value_ref[1]
    for band in range(BANDS):
        for k in range(5):
            rows = obs_ref[k, pl.ds(band, WAVES, stride=BANDS), :]
            out_ref[band, 48 + 8 * k : 56 + 8 * k] = rows
    done = []

    def send(first, count, row, rows):
        at = (pl.ds(first, count), pl.ds(row, rows))
        sent = pltpu.make_async_copy(out_ref.at[at], out_hbm.at[at], sem.at[9 + len(done)])
        sent.start()
        done.append(sent)

    send(0, BANDS, 48, 40)

    for copy in copies[:3]:
        copy.wait()
    rh, rl = doubled_root(root_ref[...])
    tiles = []
    for m4 in range(4):
        x = jnp.concatenate([control_ref[4 * g + m4] for g in range(GROUPS)], axis=0)
        s = jnp.concatenate([scale_ref[4 * g + m4] for g in range(GROUPS)], axis=0)
        xh, xl = split(x)
        y = (mm(xh, rh) + mm(xl, rh) + mm(xh, rl)) * s
        y = jnp.concatenate([y, jnp.zeros((16, 2 * CH), f32)], axis=0)
        tiles.append(y.T.reshape(24, 8, 128))
    for part in range(2):
        for j, z in enumerate(turn([t[12 * part : 12 * part + 12] for t in tiles], 1, 2)):
            for h in range(12):
                c = 48 * part + 4 * h + j
                out_ref[c // 6, 8 * (c % 6) : 8 * (c % 6) + 8] = z[h]
        send(8 * part, 8, 0, 48)
    for copy in done:
        copy.wait()


def table_copies(table_hbm, table_ref, sem, counts):
    copies = {}
    first = 0
    for count in counts:
        at = pl.ds(4 * first, 4 * count)
        copies[first] = pltpu.make_async_copy(
            table_hbm.at[at], table_ref.at[at], sem.at[len(copies)]
        )
        copies[first].start()
        first += count
    return copies


def legendre_kernel(modes_ref, table_hbm, out_ref, x_ref, acc_ref, table_ref, sem):
    copies = table_copies(table_hbm, table_ref, sem, (1,) * GROUPS)
    for half in range(2):
        for c in range(6):
            got = [modes_ref[8 * half + s, 8 * c : 8 * c + 8] for s in range(8)]
            for g, z in enumerate(turn(got, 1, 16)):
                if g < GROUPS:
                    x_ref[g, 8 * c : 8 * c + 8, 128 * half : 128 * half + 128] = z
    for k in range(5):
        for half in range(2):
            got = [modes_ref[8 * half + s, 48 + 8 * k : 56 + 8 * k] for s in range(8)]
            at = 168 + 16 * k + 8 * half
            for w, z in enumerate(turn(got, 0, 1)):
                out_ref[w, at : at + 8] = z

    slot = (iota((48, NT), 0) % 8) // 2
    order = lat_order()
    for g in range(GROUPS):
        copies[g].wait()
        x = x_ref[g]
        acc = None
        for m4 in range(4):
            xh, xl = split(jnp.where(slot == m4, x, 0.0))
            both = jnp.concatenate(split(table_ref[4 * g + m4]), axis=0)
            both = mm_nt(jnp.concatenate([xh, xl], axis=0), both)
            part = both[:48, :NLAT] + (both[48:, :NLAT] + both[:48, NLAT:])
            acc = part if acc is None else acc + part
        acc_ref[g] = acc
        for first, last in ((0, 5), (5, 7)):
            if g + 1 == last:
                rows = 48 * (last - first)
                part = acc_ref[first:last].reshape(rows, NLAT)
                both = mm(jnp.concatenate(split(part), axis=0), order)
                out = both[:rows] + both[rows:]
                for k in range(first, last):
                    for q in range(4):
                        for hc in range(2):
                            at = 48 * (k - first) + 24 * hc
                            tile = out[at : at + 24, 128 * q : 128 * q + 128]
                            out_ref[2 * q + hc, 24 * k : 24 * k + 24] = tile


def lat_order():
    at = iota((NLAT, 512), 1)
    lat = ((at // 8) % 16) * 28 + (at // 128) * 7 + at % 8
    return jnp.where((iota((NLAT, 512), 0) == lat) & (at % 8 < 7), 1.0, 0.0).astype(bf16)


def wave_table_kernel(number_ref, high_ref, low_ref):
    rows = 16
    half = NLON // 2
    row = iota((rows, MW), 0)
    slot = iota((rows, MW), 1)
    part = iota((rows, half), 0) % 2
    lon = iota((rows, half), 1)
    numbers = number_ref[...].astype(f32)
    coefs = [(-1.0) ** k / math.factorial(2 * k + 1) for k in range(6)]

    @pl.loop(0, 2 * MW // rows)
    def _(i):
        first = pl.multiple_of(i * rows, rows)
        mine = (row + first) // 2 == slot
        n = jnp.sum(jnp.where(mine, numbers, 0.0), axis=1, keepdims=True).astype(jnp.int32)
        phase = (n * lon + 256 * part) & (NLON - 1)
        turn_at = (jnp.abs(phase - half) - half // 2).astype(f32)
        y = turn_at * (2.0 * math.pi / NLON)
        y2 = y * y
        value = coefs[5]
        for k in range(4, -1, -1):
            value = value * y2 + coefs[k]
        value = value * y * FACTOR
        vh, vl = split(value)
        high_ref[pl.ds(first, rows), :half] = vh
        low_ref[pl.ds(first, rows), :half] = vl
        sign = (1 - 2 * (n & 1)).astype(f32)
        vh, vl = split(value * sign)
        high_ref[pl.ds(first, rows), half:] = vh
        low_ref[pl.ds(first, rows), half:] = vl


def synthesis_kernel(spec_ref, high_ref, low_ref, out_hbm, out_ref, lhs_ref, sem):
    rows = spec_ref[:, :168].reshape(WAVES, GROUPS, 3, 8, 128)
    for c in range(3):
        high, low = split(rows[:, :, c].reshape(2 * MW, 128).T)
        lhs_ref[128 * c : 128 * c + 128] = high
        lhs_ref[384 + 128 * c : 512 + 128 * c] = low
    done = []
    for i in range(4):
        lon = pl.ds(256 * i, 256)
        both = mm(lhs_ref[...], high_ref[:, lon])
        out = both[:384] + both[384:] + mm(lhs_ref[:384], low_ref[:, lon])
        for w in range(2):
            for band in range(BANDS):
                for c in range(3):
                    row = 128 * c + 8 * band
                    at = TILE * (BANDS * (2 * i + w) + band) + 7 * c
                    out_ref[at : at + 7] = out[row : row + 7, 128 * w : 128 * w + 128]
        at = pl.ds(2 * BANDS * TILE * i, 2 * BANDS * TILE)
        done.append(pltpu.make_async_copy(out_ref.at[at], out_hbm.at[at], sem.at[i]))
        done[i].start()
    for copy in done:
        copy.wait()


def analysis_kernel(grid_ref, high_ref, low_ref, out_ref):
    blank = jnp.zeros((1, 128), f32)
    total = None
    for i in range(4):
        tiles = []
        for c in range(3):
            parts = []
            for w in range(2):
                rows = []
                for band in range(BANDS):
                    at = TILE * (BANDS * (2 * i + w) + band) + 7 * c
                    rows += [grid_ref[at : at + 7], blank]
                parts.append(jnp.concatenate(rows, axis=0))
            tiles.append(jnp.concatenate(parts, axis=1))
        gh, gl = split(jnp.concatenate(tiles, axis=0))
        lon = pl.ds(256 * i, 256)
        both = mm_nt(high_ref[:, lon], jnp.concatenate([gh, gl], axis=0))
        part = both[:, :384] + both[:, 384:] + mm_nt(low_ref[:, lon], gh)
        total = part if total is None else total + part
    for c in range(3):
        rows = total[:, 128 * c : 128 * c + 128]
        out_ref[:, :, c] = rows.reshape(WAVES, GROUPS, 8, 128)


def legendre_adjoint_kernel(spec_ref, table_hbm, out_ref, acc_ref, table_ref, sem):
    copies = table_copies(table_hbm, table_ref, sem, (1, 2, 2, 1, 1))
    order = lat_order()
    for hc in range(2):
        s = jnp.concatenate([spec_ref[2 * q + hc] for q in range(4)], axis=1)
        sh, sl = split(s)
        acc_ref[168 * hc : 168 * hc + 168] = mm_nt(sh, order) + mm_nt(sl, order)
    slot = (iota((48, NLAT), 0) % 8) // 2
    x = []
    for g in range(GROUPS):
        if g in copies:
            copies[g].wait()
        rows = [acc_ref[168 * hc + 24 * g : 168 * hc + 24 * g + 24] for hc in range(2)]
        mine = jnp.concatenate(rows, axis=0)
        acc = None
        for m4 in range(4):
            xh, xl = split(jnp.where(slot == m4, mine, 0.0))
            left = jnp.concatenate([xh, xl], axis=0)
            for first, last in ((0, 256), (256, NLAT)):
                th, tl = split(table_ref[4 * g + m4, first:last])
                both = mm(left[:, first:last], th)
                part = both[:48] + both[48:] + mm(xh[:, first:last], tl)
                acc = part if acc is None else acc + part
        x.append(acc)
    x.append(jnp.zeros((48, NT), f32))
    for half in range(2):
        for c in range(6):
            got = [v[8 * c : 8 * c + 8, 128 * half : 128 * half + 128] for v in x]
            for s, z in enumerate(turn(got, 1, 16)):
                out_ref[8 * half + s, 8 * c : 8 * c + 8] = z


def unmix_kernel(modes_ref, control_ref, scale_ref, root_ref, out_ref):
    rh, rl = doubled_root(root_ref[...])
    tiles = turn([modes_ref[:, j] for j in range(4)], 1, 2)
    for m4 in range(4):
        y = tiles[m4].reshape(2 * CH, 128).T[: 16 * GROUPS]
        s = jnp.concatenate([scale_ref[4 * g + m4] for g in range(GROUPS)], axis=0)
        yh, yl = split(y * s)
        z = mm_nt(yh, rh) + mm_nt(yl, rh) + mm_nt(yh, rl)
        for g in range(GROUPS):
            m = 4 * g + m4
            out_ref[m] = control_ref[m] + z[16 * g : 16 * g + 16]


def sums_kernel(obs_ref, out_ref, acc_ref):
    i = pl.program_id(0)
    part = None
    for half in range(2):

        def line(k):
            at = 168 + 16 * k + 8 * half
            rows = obs_ref[0, at : at + 8]
            return jnp.concatenate([rows[s : s + 1] for s in range(8)], axis=1)

        column = line(0).astype(jnp.int32)
        level = line(1).astype(jnp.int32)
        lat = column // 128
        lon = column % 128
        q = sum((lat >= 7 * k).astype(jnp.int32) for k in range(1, 4))
        row = q * 64 + level * 8 + (lat - 7 * q)
        rows = jnp.where(iota((256, 1024), 0) == row, 1.0, 0.0).astype(bf16)
        cols = jnp.where(iota((128, 1024), 0) == lon, 1.0, 0.0).astype(bf16)
        values = []
        for k in range(2, 5):
            for v in split(line(k)):
                values.append(cols * v)
        new = mm_nt(rows, jnp.concatenate(values, axis=0))
        part = new if part is None else part + new

    @pl.when(i == 0)
    def _():
        acc_ref[...] = part

    @pl.when(i > 0)
    def _():
        acc_ref[...] += part

    @pl.when(i == WAVES - 1)
    def _():
        for k in range(3):
            first = acc_ref[:, 256 * k : 256 * k + 128]
            out_ref[k] = first + acc_ref[:, 256 * k + 128 : 256 * k + 256]


def flow_kernel(courant_ref, out_ref):
    for h in range(12):
        rows = [courant_ref[min(t, 6), 8 * h : 8 * h + 8] for t in range(8)]
        for j, z in enumerate(turn(rows, 0, 1)):
            out_ref[8 * h + j] = z


def grid_kernel(
    grid_ref,
    flow_ref,
    sums_hbm,
    lidar_ref,
    aod_ref,
    state_hbm,
    adjoint_ref,
    hold_ref,
    state_ref,
    sums_ref,
    sem,
):
    fetch = pltpu.make_async_copy(sums_hbm, sums_ref, sem.at[4])
    fetch.start()

    def tile_rows(l, b2, hc, c):
        return pl.ds(TILE * (BANDS * hc + 2 * l + b2) + 7 * c, 7)

    def store(q):
        target = state_hbm.at[pl.ds(7 * q, 7)]
        return pltpu.make_async_copy(state_ref.at[q], target, sem.at[q])

    blank = jnp.zeros((1, 128), f32)
    chains = [(b2, hc, c) for b2 in range(2) for hc in range(2) for c in range(3)]

    @pl.loop(0, 4)
    def _(q):
        lidar_sum = [None] * LEV
        aod_sum = None
        for b2, hc, c in chains:
            bin_at = b2 * 6 + hc * 3 + c
            x = [
                jnp.concatenate([grid_ref[q, tile_rows(l, b2, hc, c)], blank], axis=0)
                for l in range(LEV)
            ]
            flow = [flow_ref[q, BINS * l + bin_at] for l in range(LEV)]
            for step in range(STEPS):
                out = [flow[l] * x[l] for l in range(LEV)]
                x = [x[l] - out[l] if l == 0 else x[l] - out[l] + out[l - 1] for l in range(LEV)]
            coef = lidar_ref[bin_at]
            for l in range(LEV):
                hold_ref[BINS * l + bin_at] = x[l]
                term = x[l] * coef
                lidar_sum[l] = term if lidar_sum[l] is None else lidar_sum[l] + term
                term = x[l] * aod_ref[BINS * l + bin_at]
                aod_sum = term if aod_sum is None else aod_sum + term

        for h in range(12):
            rows = turn([hold_ref[8 * h + j] for j in range(8)], 0, 1)
            for t in range(7):
                state_ref[q, t, 8 * h : 8 * h + 8] = rows[t]
        store(q).start()

        @pl.when(q == 0)
        def _():
            fetch.wait()

        def sums(k, l):
            return sums_ref[k, pl.ds(pl.multiple_of(64 * q + 8 * l, 8), 8), :]

        weight = [sums(0, l) for l in range(LEV)]
        lidar = [weight[l] * lidar_sum[l] - sums(1, l) for l in range(LEV)]
        aod = sum(weight[1:], weight[0]) * aod_sum
        for l in range(LEV):
            aod = aod - sums(2, l)
        for b2, hc, c in chains:
            bin_at = b2 * 6 + hc * 3 + c
            coef = lidar_ref[bin_at]
            flow = [flow_ref[q, BINS * l + bin_at] for l in range(LEV)]
            a = [lidar[l] * coef + aod * aod_ref[BINS * l + bin_at] for l in range(LEV)]
            for step in range(STEPS):
                a = [
                    a[l] + flow[l] * ((a[l + 1] - a[l]) if l + 1 < LEV else -a[l])
                    for l in range(LEV)
                ]
            for l in range(LEV):
                adjoint_ref[q, tile_rows(l, b2, hc, c)] = a[l][:7]

    for q in range(4):
        store(q).wait()


def shape(*lengths, kind=f32):
    return jax.ShapeDtypeStruct(lengths, kind)


def whole(*lengths):
    return pl.BlockSpec(lengths, lambda *_: (0,) * len(lengths))


def in_hbm(x):
    return pltpu.with_memory_space_constraint(x, pltpu.HBM)


def cost(flops, size):
    return pl.CostEstimate(flops=flops, bytes_accessed=size, transcendentals=0)


def exchange(tiles, axis):
    return lax.all_to_all(tiles, axis, split_axis=0, concat_axis=0, tiled=True)


def exchange_tiles(tiles):
    rows = tiles.reshape(DEVICES, 1, TILE * 128)
    return exchange(rows, ("wave", "band")).reshape(DEVICES * TILE, 128)


def body(
    control,
    spectral_scale,
    vertical_root,
    legendre,
    zonal_number,
    courant,
    lidar_coef,
    aod_coef,
    obs_count,
    obs_column,
    obs_level,
    lidar_obs,
    aod_obs,
    obs_weight,
):
    control = jnp.swapaxes(control, 0, 1)
    scale = jnp.swapaxes(spectral_scale, 0, 1)
    hbm = pl.BlockSpec(memory_space=pltpu.HBM)
    modes = pl.pallas_call(
        mix_kernel,
        in_specs=[hbm] * 9,
        out_specs=pl.BlockSpec(memory_space=pl.ANY),
        out_shape=shape(BANDS, 88, 128),
        scratch_shapes=[
            pltpu.VMEM((BANDS, 88, 128), f32),
            pltpu.VMEM((28, 16, 192), f32),
            pltpu.VMEM((28, 16, 192), f32),
            pltpu.VMEM((CH, CH), f32),
            pltpu.VMEM((2, DEVICES, SLOT), jnp.int32),
            pltpu.VMEM((3, DEVICES, SLOT), f32),
            pltpu.VMEM((1, DEVICES), jnp.int32),
            pltpu.VMEM((5, DEVICES, SLOT), f32),
            pltpu.SemaphoreType.DMA((12,)),
        ],
        compiler_params=params(),
        cost_estimate=cost(6 * 448 * 192 * 192, 1 << 20),
        name="mix",
    )(
        *(
            in_hbm(x)
            for x in (
                control,
                scale,
                vertical_root,
                obs_column,
                obs_level,
                lidar_obs,
                aod_obs,
                obs_weight,
                obs_count,
            )
        )
    )
    waves = pl.pallas_call(
        wave_table_kernel,
        out_shape=(shape(2 * MW, NLON, kind=bf16), shape(2 * MW, NLON, kind=bf16)),
        compiler_params=params(),
        cost_estimate=cost(20 * 448 * 1024, 2 << 20),
        name="wave_table",
    )(zonal_number.reshape(1, MW))
    modes, (high, low) = lax.optimization_barrier((exchange(modes, "band"), waves))

    legendre_cost = cost(6 * 28 * 448 * 256 * 48, 14 << 20)
    in_order = params(dimension_semantics=("arbitrary",))
    table_scratch = [pltpu.VMEM((28, NLAT, NT), f32), pltpu.SemaphoreType.DMA((GROUPS,))]
    spec = pl.pallas_call(
        legendre_kernel,
        in_specs=[whole(BANDS, 88, 128), hbm],
        out_specs=whole(WAVES, 248, 128),
        out_shape=shape(WAVES, 248, 128),
        scratch_shapes=[
            pltpu.VMEM((GROUPS, 48, NT), f32),
            pltpu.VMEM((GROUPS, 48, NLAT), f32),
            *table_scratch,
        ],
        compiler_params=params(),
        cost_estimate=legendre_cost,
        name="legendre",
    )(modes, in_hbm(legendre))
    spec = exchange(spec, "wave")
    sums = pl.pallas_call(
        sums_kernel,
        grid=(WAVES,),
        in_specs=[pl.BlockSpec((1, 248, 128), lambda i: (i, 0, 0))],
        out_specs=whole(3, 256, 128),
        out_shape=shape(3, 256, 128),
        scratch_shapes=[pltpu.VMEM((256, 768), f32)],
        compiler_params=in_order,
        cost_estimate=cost(2 * 16384 * 256 * 768, 1 << 20),
        name="sums",
    )(spec)

    tiles = shape(DEVICES * TILE, 128)
    wave_cost = cost(6 * 384 * 448 * 1024, 4 << 20)
    grid = pl.pallas_call(
        synthesis_kernel,
        out_specs=pl.BlockSpec(memory_space=pl.ANY),
        out_shape=tiles,
        scratch_shapes=[
            pltpu.VMEM((DEVICES * TILE, 128), f32),
            pltpu.VMEM((768, 2 * MW), bf16),
            pltpu.SemaphoreType.DMA((4,)),
        ],
        compiler_params=params(),
        cost_estimate=wave_cost,
        name="synthesis",
    )(spec, high, low)
    grid = exchange_tiles(grid)

    field = pl.BlockSpec((7, CH, 128), lambda q: (q, 0, 0))
    scalars = pl.BlockSpec(memory_space=pltpu.SMEM)
    turned = pl.BlockSpec((CH, 8, 128), lambda q: (q, 0, 0))
    flow = pl.pallas_call(
        flow_kernel,
        grid=(4,),
        in_specs=[field],
        out_specs=turned,
        out_shape=shape(4 * CH, 8, 128),
        compiler_params=in_order,
        cost_estimate=cost(6 * 28 * 96 * 128, 3 << 20),
        name="flow",
    )(in_hbm(courant))
    quarters = (4, 2 * BANDS * TILE, 128)
    state, adjoint = pl.pallas_call(
        grid_kernel,
        in_specs=[whole(*quarters), whole(4, CH, 8, 128), hbm, scalars, scalars],
        out_specs=(pl.BlockSpec(memory_space=pl.ANY), whole(*quarters)),
        out_shape=(shape(28, CH, 128), shape(*quarters)),
        scratch_shapes=[
            pltpu.VMEM((CH, 8, 128), f32),
            pltpu.VMEM((4, 7, CH, 128), f32),
            pltpu.VMEM((3, 256, 128), f32),
            pltpu.SemaphoreType.DMA((5,)),
        ],
        compiler_params=params(),
        cost_estimate=cost(40 * 28 * 96 * 128, 6 << 20),
        name="grid_steps",
    )(
        grid.reshape(quarters),
        flow.reshape(4, CH, 8, 128),
        in_hbm(sums),
        lidar_coef,
        aod_coef,
    )
    adjoint = adjoint.reshape(DEVICES * TILE, 128)
    adjoint = exchange_tiles(adjoint)

    spec = pl.pallas_call(
        analysis_kernel,
        out_shape=shape(WAVES, GROUPS, 3, 8, 128),
        compiler_params=params(),
        cost_estimate=wave_cost,
        name="analysis",
    )(adjoint, high, low)
    spec = exchange(spec.reshape(WAVES, 24 * GROUPS, 128), "wave")

    modes = pl.pallas_call(
        legendre_adjoint_kernel,
        in_specs=[whole(WAVES, 168, 128), hbm],
        out_specs=whole(BANDS, 48, 128),
        out_shape=shape(BANDS, 48, 128),
        scratch_shapes=[pltpu.VMEM((336, NLAT), f32), *table_scratch],
        compiler_params=params(),
        cost_estimate=legendre_cost,
        name="legendre_adjoint",
    )(spec, in_hbm(legendre))
    modes = exchange(modes, "band").reshape(24, 4, 8, 128)

    gradient = pl.pallas_call(
        unmix_kernel,
        out_shape=shape(28, 16, 192),
        compiler_params=params(),
        cost_estimate=cost(6 * 448 * 192 * 192, 1 << 20),
        name="unmix",
    )(modes, control, scale, vertical_root)
    return jnp.swapaxes(gradient, 0, 1), state


def solution(mesh):
    both = ("wave", "band")
    placed = (
        P("band", "wave", None),
        P("band", "wave", None),
        P(),
        P("wave", None, None),
        P(),
        P("band", None, "wave"),
        P(),
        P(),
        P(both, None),
        P(both, None),
        P(both, None),
        P(both, None),
        P(both, None),
        P(both, None),
    )
    return jax.shard_map(
        body,
        mesh=mesh,
        in_specs=placed,
        out_specs=(P("band", "wave", None), P("band", None, "wave")),
        check_vma=False,
    )
```

```python
import math

import jax
import jax.numpy as jnp
from jax import lax
from jax.experimental import pallas as pl
from jax.experimental.pallas import tpu as pltpu
from jax.sharding import PartitionSpec as P

MW = 224
LEV = 8
BINS = 12
CH = 96
STEPS = 4
WAVES = 8
BANDS = 16
DEVICES = 128
SLOT = 128
GROUPS = 7
NLON = 1024
NLAT = 448
NT = 256
TILE = 21
FACTOR = MW ** (-0.5)
f32 = jnp.float32
bf16 = jnp.bfloat16
highest = lax.Precision.HIGHEST
LIMIT = 24 << 20


def params(**kw):
    return pltpu.CompilerParams(vmem_limit_bytes=LIMIT, **kw)


def split(x):
    hi = x.astype(bf16)
    return hi, (x - hi.astype(f32)).astype(bf16)


def mm(a, b):
    return lax.dot_general(a, b, (((1,), (0,)), ((), ())), preferred_element_type=f32)


def mm_nt(a, b):
    return lax.dot_general(a, b, (((1,), (1,)), ((), ())), preferred_element_type=f32)


def iota(shape, dim):
    return lax.broadcasted_iota(jnp.int32, shape, dim)


def turn(parts, axis, width):
    n = len(parts)
    size = parts[0].shape[axis]
    at = iota(parts[0].shape, axis)
    step = n // 2
    while step:
        keep = (at // (step * width)) % 2 == 0
        new = list(parts)
        for i in range(n):
            if (i // step) % 2 == 0:
                a, b = parts[i], parts[i + step]
                new[i] = jnp.where(keep, a, pltpu.roll(b, step * width, axis))
                new[i + step] = jnp.where(keep, pltpu.roll(a, size - step * width, axis), b)
        parts = new
        step //= 2
    return parts


def doubled_root(root):
    rows = (iota((2 * CH, CH), 0) // 2 == iota((2 * CH, CH), 1)).astype(f32).astype(bf16)
    cols = (iota((CH, 2 * CH), 1) // 2 == iota((CH, 2 * CH), 0)).astype(f32).astype(bf16)
    same = iota((2 * CH, 2 * CH), 0) % 2 == iota((2 * CH, 2 * CH), 1) % 2
    parts = []
    for part in split(root):
        wide = mm(mm(rows, part).astype(bf16), cols)
        parts.append(jnp.where(same, wide, 0.0).astype(bf16))
    return parts


def mix_kernel(
    control_hbm,
    scale_hbm,
    root_hbm,
    column_hbm,
    level_hbm,
    lidar_hbm,
    aod_hbm,
    weight_hbm,
    count_hbm,
    out_hbm,
    out_ref,
    control_ref,
    scale_ref,
    root_ref,
    index_ref,
    value_ref,
    count_ref,
    obs_ref,
    sem,
):
    copies = [
        pltpu.make_async_copy(source, target, sem.at[k])
        for k, (source, target) in enumerate(
            (
                (root_hbm, root_ref),
                (control_hbm, control_ref),
                (scale_hbm, scale_ref),
                (column_hbm, index_ref.at[0]),
                (level_hbm, index_ref.at[1]),
                (lidar_hbm, value_ref.at[0]),
                (aod_hbm, value_ref.at[1]),
                (weight_hbm, value_ref.at[2]),
                (count_hbm, count_ref),
            )
        )
    ]
    for copy in copies[3:] + copies[:3]:
        copy.start()
    for copy in copies[3:]:
        copy.wait()
    counts = jnp.broadcast_to(count_ref[...].astype(f32), (DEVICES, DEVICES)).T
    live = iota((DEVICES, SLOT), 1).astype(f32) < counts
    weight = jnp.where(live, value_ref[2], 0.0)
    obs_ref[0] = index_ref[0].astype(f32)
    obs_ref[1] = index_ref[1].astype(f32)
    obs_ref[2] = weight
    obs_ref[3] = weight * value_ref[0]
    obs_ref[4] = weight * value_ref[1]
    for band in range(BANDS):
        for k in range(5):
            rows = obs_ref[k, pl.ds(band, WAVES, stride=BANDS), :]
            out_ref[band, 48 + 8 * k : 56 + 8 * k] = rows
    done = []

    def send(first, count, row, rows):
        at = (pl.ds(first, count), pl.ds(row, rows))
        sent = pltpu.make_async_copy(out_ref.at[at], out_hbm.at[at], sem.at[9 + len(done)])
        sent.start()
        done.append(sent)

    send(0, BANDS, 48, 40)

    for copy in copies[:3]:
        copy.wait()
    rh, rl = doubled_root(root_ref[...])
    tiles = []
    for m4 in range(4):
        x = jnp.concatenate([control_ref[4 * g + m4] for g in range(GROUPS)], axis=0)
        s = jnp.concatenate([scale_ref[4 * g + m4] for g in range(GROUPS)], axis=0)
        xh, xl = split(x)
        y = (mm(xh, rh) + mm(xl, rh) + mm(xh, rl)) * s
        y = jnp.concatenate([y, jnp.zeros((16, 2 * CH), f32)], axis=0)
        tiles.append(y.T.reshape(24, 8, 128))
    for part in range(2):
        for j, z in enumerate(turn([t[12 * part : 12 * part + 12] for t in tiles], 1, 2)):
            for h in range(12):
                c = 48 * part + 4 * h + j
                out_ref[c // 6, 8 * (c % 6) : 8 * (c % 6) + 8] = z[h]
        send(8 * part, 8, 0, 48)
    for copy in done:
        copy.wait()


def table_copies(table_hbm, table_ref, sem, counts):
    copies = {}
    first = 0
    for count in counts:
        at = pl.ds(4 * first, 4 * count)
        copies[first] = pltpu.make_async_copy(
            table_hbm.at[at], table_ref.at[at], sem.at[len(copies)]
        )
        copies[first].start()
        first += count
    return copies


def legendre_kernel(modes_ref, table_hbm, out_ref, x_ref, acc_ref, table_ref, sem):
    copies = table_copies(table_hbm, table_ref, sem, (1,) * GROUPS)
    for half in range(2):
        for c in range(6):
            got = [modes_ref[8 * half + s, 8 * c : 8 * c + 8] for s in range(8)]
            for g, z in enumerate(turn(got, 1, 16)):
                if g < GROUPS:
                    x_ref[g, 8 * c : 8 * c + 8, 128 * half : 128 * half + 128] = z
    for k in range(5):
        for half in range(2):
            got = [modes_ref[8 * half + s, 48 + 8 * k : 56 + 8 * k] for s in range(8)]
            at = 168 + 16 * k + 8 * half
            for w, z in enumerate(turn(got, 0, 1)):
                out_ref[w, at : at + 8] = z

    slot = (iota((48, NT), 0) % 8) // 2
    order = lat_order()
    for g in range(GROUPS):
        copies[g].wait()
        x = x_ref[g]
        acc = None
        for m4 in range(4):
            xh, xl = split(jnp.where(slot == m4, x, 0.0))
            both = jnp.concatenate(split(table_ref[4 * g + m4]), axis=0)
            both = mm_nt(jnp.concatenate([xh, xl], axis=0), both)
            part = both[:48, :NLAT] + (both[48:, :NLAT] + both[:48, NLAT:])
            acc = part if acc is None else acc + part
        acc_ref[g] = acc
        for first, last in ((0, GROUPS),):
            if g + 1 == last:
                rows = 48 * (last - first)
                part = acc_ref[first:last].reshape(rows, NLAT)
                both = mm(jnp.concatenate(split(part), axis=0), order)
                out = both[:rows] + both[rows:]
                for k in range(first, last):
                    for q in range(4):
                        for hc in range(2):
                            at = 48 * (k - first) + 24 * hc
                            tile = out[at : at + 24, 128 * q : 128 * q + 128]
                            out_ref[2 * q + hc, 24 * k : 24 * k + 24] = tile


def lat_order():
    at = iota((NLAT, 512), 1)
    lat = ((at // 8) % 16) * 28 + (at // 128) * 7 + at % 8
    return jnp.where((iota((NLAT, 512), 0) == lat) & (at % 8 < 7), 1.0, 0.0).astype(bf16)


def wave_table_kernel(number_ref, high_ref, low_ref):
    rows = 16
    half = NLON // 2
    row = iota((rows, MW), 0)
    slot = iota((rows, MW), 1)
    part = iota((rows, half), 0) % 2
    lon = iota((rows, half), 1)
    numbers = number_ref[...].astype(f32)
    coefs = [(-1.0) ** k / math.factorial(2 * k + 1) for k in range(6)]

    @pl.loop(0, 2 * MW // rows)
    def _(i):
        first = pl.multiple_of(i * rows, rows)
        mine = (row + first) // 2 == slot
        n = jnp.sum(jnp.where(mine, numbers, 0.0), axis=1, keepdims=True).astype(jnp.int32)
        phase = (n * lon + 256 * part) & (NLON - 1)
        turn_at = (jnp.abs(phase - half) - half // 2).astype(f32)
        y = turn_at * (2.0 * math.pi / NLON)
        y2 = y * y
        value = coefs[5]
        for k in range(4, -1, -1):
            value = value * y2 + coefs[k]
        value = value * y * FACTOR
        vh, vl = split(value)
        high_ref[pl.ds(first, rows), :half] = vh
        low_ref[pl.ds(first, rows), :half] = vl
        sign = (1 - 2 * (n & 1)).astype(f32)
        vh, vl = split(value * sign)
        high_ref[pl.ds(first, rows), half:] = vh
        low_ref[pl.ds(first, rows), half:] = vl


def synthesis_kernel(spec_ref, high_ref, low_ref, out_hbm, out_ref, lhs_ref, sem):
    rows = spec_ref[:, :168].reshape(WAVES, GROUPS, 3, 8, 128)
    for c in range(3):
        high, low = split(rows[:, :, c].reshape(2 * MW, 128).T)
        lhs_ref[128 * c : 128 * c + 128] = high
        lhs_ref[384 + 128 * c : 512 + 128 * c] = low
    done = []
    for i in range(4):
        lon = pl.ds(256 * i, 256)
        both = mm(lhs_ref[...], high_ref[:, lon])
        out = both[:384] + both[384:] + mm(lhs_ref[:384], low_ref[:, lon])
        for w in range(2):
            for band in range(BANDS):
                for c in range(3):
                    row = 128 * c + 8 * band
                    at = TILE * (BANDS * (2 * i + w) + band) + 7 * c
                    out_ref[at : at + 7] = out[row : row + 7, 128 * w : 128 * w + 128]
        at = pl.ds(2 * BANDS * TILE * i, 2 * BANDS * TILE)
        done.append(pltpu.make_async_copy(out_ref.at[at], out_hbm.at[at], sem.at[i]))
        done[i].start()
    for copy in done:
        copy.wait()


def analysis_kernel(grid_ref, high_ref, low_ref, out_ref):
    blank = jnp.zeros((1, 128), f32)
    total = None
    for i in range(4):
        tiles = []
        for c in range(3):
            parts = []
            for w in range(2):
                rows = []
                for band in range(BANDS):
                    at = TILE * (BANDS * (2 * i + w) + band) + 7 * c
                    rows += [grid_ref[at : at + 7], blank]
                parts.append(jnp.concatenate(rows, axis=0))
            tiles.append(jnp.concatenate(parts, axis=1))
        gh, gl = split(jnp.concatenate(tiles, axis=0))
        lon = pl.ds(256 * i, 256)
        both = mm_nt(high_ref[:, lon], jnp.concatenate([gh, gl], axis=0))
        part = both[:, :384] + both[:, 384:] + mm_nt(low_ref[:, lon], gh)
        total = part if total is None else total + part
    for c in range(3):
        rows = total[:, 128 * c : 128 * c + 128]
        out_ref[:, :, c] = rows.reshape(WAVES, GROUPS, 8, 128)


def legendre_adjoint_kernel(spec_ref, table_hbm, out_ref, acc_ref, table_ref, sem):
    copies = table_copies(table_hbm, table_ref, sem, (1, 2, 2, 1, 1))
    order = lat_order()
    for hc in range(2):
        s = jnp.concatenate([spec_ref[2 * q + hc] for q in range(4)], axis=1)
        sh, sl = split(s)
        acc_ref[168 * hc : 168 * hc + 168] = mm_nt(sh, order) + mm_nt(sl, order)
    slot = (iota((48, NLAT), 0) % 8) // 2
    x = []
    for g in range(GROUPS):
        if g in copies:
            copies[g].wait()
        rows = [acc_ref[168 * hc + 24 * g : 168 * hc + 24 * g + 24] for hc in range(2)]
        mine = jnp.concatenate(rows, axis=0)
        acc = None
        for m4 in range(4):
            xh, xl = split(jnp.where(slot == m4, mine, 0.0))
            left = jnp.concatenate([xh, xl], axis=0)
            for first, last in ((0, 256), (256, NLAT)):
                th, tl = split(table_ref[4 * g + m4, first:last])
                both = mm(left[:, first:last], th)
                part = both[:48] + both[48:] + mm(xh[:, first:last], tl)
                acc = part if acc is None else acc + part
        x.append(acc)
    x.append(jnp.zeros((48, NT), f32))
    for half in range(2):
        for c in range(6):
            got = [v[8 * c : 8 * c + 8, 128 * half : 128 * half + 128] for v in x]
            for s, z in enumerate(turn(got, 1, 16)):
                out_ref[8 * half + s, 8 * c : 8 * c + 8] = z


def unmix_kernel(modes_ref, control_ref, scale_ref, root_ref, out_hbm, out_ref, sem):
    done = []
    rh, rl = doubled_root(root_ref[...])
    tiles = turn([modes_ref[:, j] for j in range(4)], 1, 2)
    for m4 in range(4):
        y = tiles[m4].reshape(2 * CH, 128).T[: 16 * GROUPS]
        s = jnp.concatenate([scale_ref[4 * g + m4] for g in range(GROUPS)], axis=0)
        yh, yl = split(y * s)
        z = mm_nt(yh, rh) + mm_nt(yl, rh) + mm_nt(yh, rl)
        for g in range(GROUPS):
            m = 4 * g + m4
            out_ref[m] = control_ref[m] + z[16 * g : 16 * g + 16]
            done.append(pltpu.make_async_copy(out_ref.at[m], out_hbm.at[m], sem.at[m]))
            done[-1].start()
    for copy in done:
        copy.wait()


def sums_kernel(obs_ref, out_ref, acc_ref):
    i = pl.program_id(0)
    part = None
    for half in range(2):

        def line(k):
            at = 168 + 16 * k + 8 * half
            rows = obs_ref[0, at : at + 8]
            return jnp.concatenate([rows[s : s + 1] for s in range(8)], axis=1)

        column = line(0).astype(jnp.int32)
        level = line(1).astype(jnp.int32)
        lat = column // 128
        lon = column % 128
        q = sum((lat >= 7 * k).astype(jnp.int32) for k in range(1, 4))
        row = q * 64 + level * 8 + (lat - 7 * q)
        rows = jnp.where(iota((256, 1024), 0) == row, 1.0, 0.0).astype(bf16)
        cols = jnp.where(iota((128, 1024), 0) == lon, 1.0, 0.0).astype(bf16)
        values = []
        for k in range(2, 5):
            for v in split(line(k)):
                values.append(cols * v)
        new = mm_nt(rows, jnp.concatenate(values, axis=0))
        part = new if part is None else part + new

    @pl.when(i == 0)
    def _():
        acc_ref[...] = part

    @pl.when(i > 0)
    def _():
        acc_ref[...] += part

    @pl.when(i == WAVES - 1)
    def _():
        for k in range(3):
            first = acc_ref[:, 256 * k : 256 * k + 128]
            out_ref[k] = first + acc_ref[:, 256 * k + 128 : 256 * k + 256]


def flow_kernel(courant_ref, out_ref):
    for h in range(12):
        rows = [courant_ref[min(t, 6), 8 * h : 8 * h + 8] for t in range(8)]
        for j, z in enumerate(turn(rows, 0, 1)):
            out_ref[8 * h + j] = z


def grid_kernel(
    grid_ref,
    flow_ref,
    sums_hbm,
    lidar_ref,
    aod_ref,
    state_hbm,
    adjoint_ref,
    hold_ref,
    state_ref,
    sums_ref,
    sem,
):
    fetch = pltpu.make_async_copy(sums_hbm, sums_ref, sem.at[4])
    fetch.start()

    def tile_rows(l, b2, hc, c):
        return pl.ds(TILE * (BANDS * hc + 2 * l + b2) + 7 * c, 7)

    def store(q):
        target = state_hbm.at[pl.ds(7 * q, 7)]
        return pltpu.make_async_copy(state_ref.at[q], target, sem.at[q])

    blank = jnp.zeros((1, 128), f32)
    chains = [(b2, hc, c) for b2 in range(2) for hc in range(2) for c in range(3)]

    @pl.loop(0, 4)
    def _(q):
        lidar_sum = [None] * LEV
        aod_sum = None
        for b2, hc, c in chains:
            bin_at = b2 * 6 + hc * 3 + c
            x = [
                jnp.concatenate([grid_ref[q, tile_rows(l, b2, hc, c)], blank], axis=0)
                for l in range(LEV)
            ]
            flow = [flow_ref[q, BINS * l + bin_at] for l in range(LEV)]
            for step in range(STEPS):
                out = [flow[l] * x[l] for l in range(LEV)]
                x = [x[l] - out[l] if l == 0 else x[l] - out[l] + out[l - 1] for l in range(LEV)]
            coef = lidar_ref[bin_at]
            for l in range(LEV):
                hold_ref[BINS * l + bin_at] = x[l]
                term = x[l] * coef
                lidar_sum[l] = term if lidar_sum[l] is None else lidar_sum[l] + term
                term = x[l] * aod_ref[BINS * l + bin_at]
                aod_sum = term if aod_sum is None else aod_sum + term

        for h in range(12):
            rows = turn([hold_ref[8 * h + j] for j in range(8)], 0, 1)
            for t in range(7):
                state_ref[q, t, 8 * h : 8 * h + 8] = rows[t]
        store(q).start()

        @pl.when(q == 0)
        def _():
            fetch.wait()

        def sums(k, l):
            return sums_ref[k, pl.ds(pl.multiple_of(64 * q + 8 * l, 8), 8), :]

        weight = [sums(0, l) for l in range(LEV)]
        lidar = [weight[l] * lidar_sum[l] - sums(1, l) for l in range(LEV)]
        aod = sum(weight[1:], weight[0]) * aod_sum
        for l in range(LEV):
            aod = aod - sums(2, l)
        for b2, hc, c in chains:
            bin_at = b2 * 6 + hc * 3 + c
            coef = lidar_ref[bin_at]
            flow = [flow_ref[q, BINS * l + bin_at] for l in range(LEV)]
            a = [lidar[l] * coef + aod * aod_ref[BINS * l + bin_at] for l in range(LEV)]
            for step in range(STEPS):
                a = [
                    a[l] + flow[l] * ((a[l + 1] - a[l]) if l + 1 < LEV else -a[l])
                    for l in range(LEV)
                ]
            for l in range(LEV):
                adjoint_ref[q, tile_rows(l, b2, hc, c)] = a[l][:7]

    for q in range(4):
        store(q).wait()


def shape(*lengths, kind=f32):
    return jax.ShapeDtypeStruct(lengths, kind)


def whole(*lengths):
    return pl.BlockSpec(lengths, lambda *_: (0,) * len(lengths))


def in_hbm(x):
    return pltpu.with_memory_space_constraint(x, pltpu.HBM)


def cost(flops, size):
    return pl.CostEstimate(flops=flops, bytes_accessed=size, transcendentals=0)


def exchange(tiles, axis):
    return lax.all_to_all(tiles, axis, split_axis=0, concat_axis=0, tiled=True)


def exchange_tiles(tiles):
    rows = tiles.reshape(DEVICES, 1, TILE * 128)
    return exchange(rows, ("wave", "band")).reshape(DEVICES * TILE, 128)


def body(
    control,
    spectral_scale,
    vertical_root,
    legendre,
    zonal_number,
    courant,
    lidar_coef,
    aod_coef,
    obs_count,
    obs_column,
    obs_level,
    lidar_obs,
    aod_obs,
    obs_weight,
):
    control = jnp.swapaxes(control, 0, 1)
    scale = jnp.swapaxes(spectral_scale, 0, 1)
    hbm = pl.BlockSpec(memory_space=pltpu.HBM)
    modes = pl.pallas_call(
        mix_kernel,
        in_specs=[hbm] * 9,
        out_specs=pl.BlockSpec(memory_space=pl.ANY),
        out_shape=shape(BANDS, 88, 128),
        scratch_shapes=[
            pltpu.VMEM((BANDS, 88, 128), f32),
            pltpu.VMEM((28, 16, 192), f32),
            pltpu.VMEM((28, 16, 192), f32),
            pltpu.VMEM((CH, CH), f32),
            pltpu.VMEM((2, DEVICES, SLOT), jnp.int32),
            pltpu.VMEM((3, DEVICES, SLOT), f32),
            pltpu.VMEM((1, DEVICES), jnp.int32),
            pltpu.VMEM((5, DEVICES, SLOT), f32),
            pltpu.SemaphoreType.DMA((12,)),
        ],
        compiler_params=params(),
        cost_estimate=cost(6 * 448 * 192 * 192, 1 << 20),
        name="mix",
    )(
        *(
            in_hbm(x)
            for x in (
                control,
                scale,
                vertical_root,
                obs_column,
                obs_level,
                lidar_obs,
                aod_obs,
                obs_weight,
                obs_count,
            )
        )
    )
    waves = pl.pallas_call(
        wave_table_kernel,
        out_shape=(shape(2 * MW, NLON, kind=bf16), shape(2 * MW, NLON, kind=bf16)),
        compiler_params=params(),
        cost_estimate=cost(20 * 448 * 1024, 2 << 20),
        name="wave_table",
    )(zonal_number.reshape(1, MW))
    modes, (high, low) = lax.optimization_barrier((exchange(modes, "band"), waves))

    legendre_cost = cost(6 * 28 * 448 * 256 * 48, 14 << 20)
    in_order = params(dimension_semantics=("arbitrary",))
    table_scratch = [pltpu.VMEM((28, NLAT, NT), f32), pltpu.SemaphoreType.DMA((GROUPS,))]
    spec = pl.pallas_call(
        legendre_kernel,
        in_specs=[whole(BANDS, 88, 128), hbm],
        out_specs=whole(WAVES, 248, 128),
        out_shape=shape(WAVES, 248, 128),
        scratch_shapes=[
            pltpu.VMEM((GROUPS, 48, NT), f32),
            pltpu.VMEM((GROUPS, 48, NLAT), f32),
            *table_scratch,
        ],
        compiler_params=params(),
        cost_estimate=legendre_cost,
        name="legendre",
    )(modes, in_hbm(legendre))
    spec = exchange(spec, "wave")
    sums = pl.pallas_call(
        sums_kernel,
        grid=(WAVES,),
        in_specs=[pl.BlockSpec((1, 248, 128), lambda i: (i, 0, 0))],
        out_specs=whole(3, 256, 128),
        out_shape=shape(3, 256, 128),
        scratch_shapes=[pltpu.VMEM((256, 768), f32)],
        compiler_params=in_order,
        cost_estimate=cost(2 * 16384 * 256 * 768, 1 << 20),
        name="sums",
    )(spec)

    tiles = shape(DEVICES * TILE, 128)
    wave_cost = cost(6 * 384 * 448 * 1024, 4 << 20)
    grid = pl.pallas_call(
        synthesis_kernel,
        out_specs=pl.BlockSpec(memory_space=pl.ANY),
        out_shape=tiles,
        scratch_shapes=[
            pltpu.VMEM((DEVICES * TILE, 128), f32),
            pltpu.VMEM((768, 2 * MW), bf16),
            pltpu.SemaphoreType.DMA((4,)),
        ],
        compiler_params=params(),
        cost_estimate=wave_cost,
        name="synthesis",
    )(spec, high, low)
    grid = exchange_tiles(grid)

    field = pl.BlockSpec((7, CH, 128), lambda q: (q, 0, 0))
    scalars = pl.BlockSpec(memory_space=pltpu.SMEM)
    turned = pl.BlockSpec((CH, 8, 128), lambda q: (q, 0, 0))
    flow = pl.pallas_call(
        flow_kernel,
        grid=(4,),
        in_specs=[field],
        out_specs=turned,
        out_shape=shape(4 * CH, 8, 128),
        compiler_params=in_order,
        cost_estimate=cost(6 * 28 * 96 * 128, 3 << 20),
        name="flow",
    )(in_hbm(courant))
    quarters = (4, 2 * BANDS * TILE, 128)
    state, adjoint = pl.pallas_call(
        grid_kernel,
        in_specs=[whole(*quarters), whole(4, CH, 8, 128), hbm, scalars, scalars],
        out_specs=(pl.BlockSpec(memory_space=pl.ANY), whole(*quarters)),
        out_shape=(shape(28, CH, 128), shape(*quarters)),
        scratch_shapes=[
            pltpu.VMEM((CH, 8, 128), f32),
            pltpu.VMEM((4, 7, CH, 128), f32),
            pltpu.VMEM((3, 256, 128), f32),
            pltpu.SemaphoreType.DMA((5,)),
        ],
        compiler_params=params(),
        cost_estimate=cost(40 * 28 * 96 * 128, 6 << 20),
        name="grid_steps",
    )(
        grid.reshape(quarters),
        flow.reshape(4, CH, 8, 128),
        in_hbm(sums),
        lidar_coef,
        aod_coef,
    )
    adjoint = adjoint.reshape(DEVICES * TILE, 128)
    adjoint = exchange_tiles(adjoint)

    spec = pl.pallas_call(
        analysis_kernel,
        out_shape=shape(WAVES, GROUPS, 3, 8, 128),
        compiler_params=params(),
        cost_estimate=wave_cost,
        name="analysis",
    )(adjoint, high, low)
    spec = exchange(spec.reshape(WAVES, 24 * GROUPS, 128), "wave")

    modes = pl.pallas_call(
        legendre_adjoint_kernel,
        in_specs=[whole(WAVES, 168, 128), hbm],
        out_specs=whole(BANDS, 48, 128),
        out_shape=shape(BANDS, 48, 128),
        scratch_shapes=[pltpu.VMEM((336, NLAT), f32), *table_scratch],
        compiler_params=params(),
        cost_estimate=legendre_cost,
        name="legendre_adjoint",
    )(spec, in_hbm(legendre))
    modes = exchange(modes, "band").reshape(24, 4, 8, 128)

    gradient = pl.pallas_call(
        unmix_kernel,
        out_specs=pl.BlockSpec(memory_space=pl.ANY),
        out_shape=shape(28, 16, 192),
        scratch_shapes=[pltpu.VMEM((28, 16, 192), f32), pltpu.SemaphoreType.DMA((28,))],
        compiler_params=params(),
        cost_estimate=cost(6 * 448 * 192 * 192, 1 << 20),
        name="unmix",
    )(modes, control, scale, vertical_root)
    return jnp.swapaxes(gradient, 0, 1), state


def solution(mesh):
    both = ("wave", "band")
    placed = (
        P("band", "wave", None),
        P("band", "wave", None),
        P(),
        P("wave", None, None),
        P(),
        P("band", None, "wave"),
        P(),
        P(),
        P(both, None),
        P(both, None),
        P(both, None),
        P(both, None),
        P(both, None),
        P(both, None),
    )
    return jax.shard_map(
        body,
        mesh=mesh,
        in_specs=placed,
        out_specs=(P("band", "wave", None), P("band", None, "wave")),
        check_vma=False,
    )
```

```python
import math

import jax
import jax.numpy as jnp
from jax import lax
from jax.experimental import pallas as pl
from jax.experimental.pallas import tpu as pltpu
from jax.sharding import PartitionSpec as P

MW = 224
LEV = 8
BINS = 12
CH = 96
STEPS = 4
WAVES = 8
BANDS = 16
DEVICES = 128
SLOT = 128
GROUPS = 7
NLON = 1024
NLAT = 448
NT = 256
TILE = 21
FACTOR = MW ** (-0.5)
f32 = jnp.float32
bf16 = jnp.bfloat16
highest = lax.Precision.HIGHEST
LIMIT = 24 << 20


def params(**kw):
    return pltpu.CompilerParams(vmem_limit_bytes=LIMIT, **kw)


def split(x):
    hi = x.astype(bf16)
    return hi, (x - hi.astype(f32)).astype(bf16)


def mm(a, b):
    return lax.dot_general(a, b, (((1,), (0,)), ((), ())), preferred_element_type=f32)


def mm_nt(a, b):
    return lax.dot_general(a, b, (((1,), (1,)), ((), ())), preferred_element_type=f32)


def iota(shape, dim):
    return lax.broadcasted_iota(jnp.int32, shape, dim)


def turn(parts, axis, width):
    n = len(parts)
    size = parts[0].shape[axis]
    at = iota(parts[0].shape, axis)
    step = n // 2
    while step:
        keep = (at // (step * width)) % 2 == 0
        new = list(parts)
        for i in range(n):
            if (i // step) % 2 == 0:
                a, b = parts[i], parts[i + step]
                new[i] = jnp.where(keep, a, pltpu.roll(b, step * width, axis))
                new[i + step] = jnp.where(keep, pltpu.roll(a, size - step * width, axis), b)
        parts = new
        step //= 2
    return parts


def doubled_root(root):
    rows = (iota((2 * CH, CH), 0) // 2 == iota((2 * CH, CH), 1)).astype(f32).astype(bf16)
    cols = (iota((CH, 2 * CH), 1) // 2 == iota((CH, 2 * CH), 0)).astype(f32).astype(bf16)
    same = iota((2 * CH, 2 * CH), 0) % 2 == iota((2 * CH, 2 * CH), 1) % 2
    parts = []
    for part in split(root):
        wide = mm(mm(rows, part).astype(bf16), cols)
        parts.append(jnp.where(same, wide, 0.0).astype(bf16))
    return parts


def mix_kernel(
    control_hbm,
    scale_hbm,
    root_hbm,
    column_hbm,
    level_hbm,
    lidar_hbm,
    aod_hbm,
    weight_hbm,
    count_hbm,
    out_hbm,
    out_ref,
    control_ref,
    scale_ref,
    root_ref,
    index_ref,
    value_ref,
    count_ref,
    obs_ref,
    sem,
):
    copies = [
        pltpu.make_async_copy(source, target, sem.at[k])
        for k, (source, target) in enumerate(
            (
                (root_hbm, root_ref),
                (control_hbm, control_ref),
                (scale_hbm, scale_ref),
                (column_hbm, index_ref.at[0]),
                (level_hbm, index_ref.at[1]),
                (lidar_hbm, value_ref.at[0]),
                (aod_hbm, value_ref.at[1]),
                (weight_hbm, value_ref.at[2]),
                (count_hbm, count_ref),
            )
        )
    ]
    for copy in copies:
        copy.start()
    done = []

    def send(first, count, row, rows):
        at = (pl.ds(first, count), pl.ds(row, rows))
        sent = pltpu.make_async_copy(out_ref.at[at], out_hbm.at[at], sem.at[9 + len(done)])
        sent.start()
        done.append(sent)

    for copy in copies[:3]:
        copy.wait()
    rh, rl = doubled_root(root_ref[...])
    tiles = []
    for m4 in range(4):
        x = jnp.concatenate([control_ref[4 * g + m4] for g in range(GROUPS)], axis=0)
        s = jnp.concatenate([scale_ref[4 * g + m4] for g in range(GROUPS)], axis=0)
        xh, xl = split(x)
        y = (mm(xh, rh) + mm(xl, rh) + mm(xh, rl)) * s
        y = jnp.concatenate([y, jnp.zeros((16, 2 * CH), f32)], axis=0)
        tiles.append(y.T.reshape(24, 8, 128))
    for part in range(2):
        for j, z in enumerate(turn([t[12 * part : 12 * part + 12] for t in tiles], 1, 2)):
            for h in range(12):
                c = 48 * part + 4 * h + j
                out_ref[c // 6, 8 * (c % 6) : 8 * (c % 6) + 8] = z[h]
        send(8 * part, 8, 0, 48)

    for copy in copies[3:]:
        copy.wait()
    counts = jnp.broadcast_to(count_ref[...].astype(f32), (DEVICES, DEVICES)).T
    live = iota((DEVICES, SLOT), 1).astype(f32) < counts
    weight = jnp.where(live, value_ref[2], 0.0)
    obs_ref[0] = index_ref[0].astype(f32)
    obs_ref[1] = index_ref[1].astype(f32)
    obs_ref[2] = weight
    obs_ref[3] = weight * value_ref[0]
    obs_ref[4] = weight * value_ref[1]
    for band in range(BANDS):
        for k in range(5):
            rows = obs_ref[k, pl.ds(band, WAVES, stride=BANDS), :]
            out_ref[band, 48 + 8 * k : 56 + 8 * k] = rows
    send(0, BANDS, 48, 40)
    for copy in done:
        copy.wait()


def table_copies(table_hbm, table_ref, sem, counts):
    copies = {}
    first = 0
    for count in counts:
        at = pl.ds(4 * first, 4 * count)
        copies[first] = pltpu.make_async_copy(
            table_hbm.at[at], table_ref.at[at], sem.at[len(copies)]
        )
        copies[first].start()
        first += count
    return copies


def legendre_kernel(modes_ref, table_hbm, out_ref, x_ref, acc_ref, table_ref, sem):
    copies = table_copies(table_hbm, table_ref, sem, (1,) * GROUPS)
    for half in range(2):
        for c in range(6):
            got = [modes_ref[8 * half + s, 8 * c : 8 * c + 8] for s in range(8)]
            for g, z in enumerate(turn(got, 1, 16)):
                if g < GROUPS:
                    x_ref[g, 8 * c : 8 * c + 8, 128 * half : 128 * half + 128] = z
    for k in range(5):
        for half in range(2):
            got = [modes_ref[8 * half + s, 48 + 8 * k : 56 + 8 * k] for s in range(8)]
            at = 168 + 16 * k + 8 * half
            for w, z in enumerate(turn(got, 0, 1)):
                out_ref[w, at : at + 8] = z

    slot = (iota((48, NT), 0) % 8) // 2
    order = lat_order()
    for g in range(GROUPS):
        copies[g].wait()
        x = x_ref[g]
        acc = None
        for m4 in range(4):
            xh, xl = split(jnp.where(slot == m4, x, 0.0))
            both = jnp.concatenate(split(table_ref[4 * g + m4]), axis=0)
            both = mm_nt(jnp.concatenate([xh, xl], axis=0), both)
            part = both[:48, :NLAT] + (both[48:, :NLAT] + both[:48, NLAT:])
            acc = part if acc is None else acc + part
        acc_ref[g] = acc
        for first, last in ((0, GROUPS),):
            if g + 1 == last:
                rows = 48 * (last - first)
                part = acc_ref[first:last].reshape(rows, NLAT)
                both = mm(jnp.concatenate(split(part), axis=0), order)
                out = both[:rows] + both[rows:]
                for k in range(first, last):
                    for q in range(4):
                        for hc in range(2):
                            at = 48 * (k - first) + 24 * hc
                            tile = out[at : at + 24, 128 * q : 128 * q + 128]
                            out_ref[2 * q + hc, 24 * k : 24 * k + 24] = tile


def lat_order():
    at = iota((NLAT, 512), 1)
    lat = ((at // 8) % 16) * 28 + (at // 128) * 7 + at % 8
    return jnp.where((iota((NLAT, 512), 0) == lat) & (at % 8 < 7), 1.0, 0.0).astype(bf16)


def wave_table_kernel(number_ref, high_ref, low_ref):
    rows = 16
    half = NLON // 2
    row = iota((rows, MW), 0)
    slot = iota((rows, MW), 1)
    part = iota((rows, half), 0) % 2
    lon = iota((rows, half), 1)
    numbers = number_ref[...].astype(f32)
    coefs = [(-1.0) ** k / math.factorial(2 * k + 1) for k in range(6)]

    @pl.loop(0, 2 * MW // rows)
    def _(i):
        first = pl.multiple_of(i * rows, rows)
        mine = (row + first) // 2 == slot
        n = jnp.sum(jnp.where(mine, numbers, 0.0), axis=1, keepdims=True).astype(jnp.int32)
        phase = (n * lon + 256 * part) & (NLON - 1)
        turn_at = (jnp.abs(phase - half) - half // 2).astype(f32)
        y = turn_at * (2.0 * math.pi / NLON)
        y2 = y * y
        value = coefs[5]
        for k in range(4, -1, -1):
            value = value * y2 + coefs[k]
        value = value * y * FACTOR
        vh, vl = split(value)
        high_ref[pl.ds(first, rows), :half] = vh
        low_ref[pl.ds(first, rows), :half] = vl
        sign = (1 - 2 * (n & 1)).astype(f32)
        vh, vl = split(value * sign)
        high_ref[pl.ds(first, rows), half:] = vh
        low_ref[pl.ds(first, rows), half:] = vl


def synthesis_kernel(spec_ref, high_ref, low_ref, out_hbm, out_ref, lhs_ref, sem):
    rows = spec_ref[:, :168].reshape(WAVES, GROUPS, 3, 8, 128)
    for c in range(3):
        high, low = split(rows[:, :, c].reshape(2 * MW, 128).T)
        lhs_ref[128 * c : 128 * c + 128] = high
        lhs_ref[384 + 128 * c : 512 + 128 * c] = low
    done = []
    for i in range(4):
        lon = pl.ds(256 * i, 256)
        both = mm(lhs_ref[...], high_ref[:, lon])
        out = both[:384] + both[384:] + mm(lhs_ref[:384], low_ref[:, lon])
        for w in range(2):
            for band in range(BANDS):
                for c in range(3):
                    row = 128 * c + 8 * band
                    at = TILE * (BANDS * (2 * i + w) + band) + 7 * c
                    out_ref[at : at + 7] = out[row : row + 7, 128 * w : 128 * w + 128]
        at = pl.ds(2 * BANDS * TILE * i, 2 * BANDS * TILE)
        done.append(pltpu.make_async_copy(out_ref.at[at], out_hbm.at[at], sem.at[i]))
        done[i].start()
    for copy in done:
        copy.wait()


def analysis_kernel(grid_ref, high_ref, low_ref, out_ref):
    blank = jnp.zeros((1, 128), f32)
    total = None
    for i in range(4):
        tiles = []
        for c in range(3):
            parts = []
            for w in range(2):
                rows = []
                for band in range(BANDS):
                    at = TILE * (BANDS * (2 * i + w) + band) + 7 * c
                    rows += [grid_ref[at : at + 7], blank]
                parts.append(jnp.concatenate(rows, axis=0))
            tiles.append(jnp.concatenate(parts, axis=1))
        gh, gl = split(jnp.concatenate(tiles, axis=0))
        lon = pl.ds(256 * i, 256)
        both = mm_nt(high_ref[:, lon], jnp.concatenate([gh, gl], axis=0))
        part = both[:, :384] + both[:, 384:] + mm_nt(low_ref[:, lon], gh)
        total = part if total is None else total + part
    for c in range(3):
        rows = total[:, 128 * c : 128 * c + 128]
        out_ref[:, :, c] = rows.reshape(WAVES, GROUPS, 8, 128)


def legendre_adjoint_kernel(spec_ref, table_hbm, out_ref, acc_ref, table_ref, sem):
    copies = table_copies(table_hbm, table_ref, sem, (1, 2, 2, 1, 1))
    order = lat_order()
    for hc in range(2):
        s = jnp.concatenate([spec_ref[2 * q + hc] for q in range(4)], axis=1)
        sh, sl = split(s)
        acc_ref[168 * hc : 168 * hc + 168] = mm_nt(sh, order) + mm_nt(sl, order)
    slot = (iota((48, NLAT), 0) % 8) // 2
    x = []
    for g in range(GROUPS):
        if g in copies:
            copies[g].wait()
        rows = [acc_ref[168 * hc + 24 * g : 168 * hc + 24 * g + 24] for hc in range(2)]
        mine = jnp.concatenate(rows, axis=0)
        acc = None
        for m4 in range(4):
            xh, xl = split(jnp.where(slot == m4, mine, 0.0))
            left = jnp.concatenate([xh, xl], axis=0)
            for first, last in ((0, 256), (256, NLAT)):
                th, tl = split(table_ref[4 * g + m4, first:last])
                both = mm(left[:, first:last], th)
                part = both[:48] + both[48:] + mm(xh[:, first:last], tl)
                acc = part if acc is None else acc + part
        x.append(acc)
    x.append(jnp.zeros((48, NT), f32))
    for half in range(2):
        for c in range(6):
            got = [v[8 * c : 8 * c + 8, 128 * half : 128 * half + 128] for v in x]
            for s, z in enumerate(turn(got, 1, 16)):
                out_ref[8 * half + s, 8 * c : 8 * c + 8] = z


def unmix_kernel(modes_ref, control_ref, scale_ref, root_ref, out_ref):
    rh, rl = doubled_root(root_ref[...])
    tiles = turn([modes_ref[:, j] for j in range(4)], 1, 2)
    for m4 in range(4):
        y = tiles[m4].reshape(2 * CH, 128).T[: 16 * GROUPS]
        s = jnp.concatenate([scale_ref[4 * g + m4] for g in range(GROUPS)], axis=0)
        yh, yl = split(y * s)
        z = mm_nt(yh, rh) + mm_nt(yl, rh) + mm_nt(yh, rl)
        for g in range(GROUPS):
            m = 4 * g + m4
            out_ref[m] = control_ref[m] + z[16 * g : 16 * g + 16]


def sums_kernel(obs_ref, out_ref, acc_ref):
    i = pl.program_id(0)
    part = None
    for half in range(2):

        def line(k):
            at = 168 + 16 * k + 8 * half
            rows = obs_ref[0, at : at + 8]
            return jnp.concatenate([rows[s : s + 1] for s in range(8)], axis=1)

        column = line(0).astype(jnp.int32)
        level = line(1).astype(jnp.int32)
        lat = column // 128
        lon = column % 128
        q = sum((lat >= 7 * k).astype(jnp.int32) for k in range(1, 4))
        row = q * 64 + level * 8 + (lat - 7 * q)
        rows = jnp.where(iota((256, 1024), 0) == row, 1.0, 0.0).astype(bf16)
        cols = jnp.where(iota((128, 1024), 0) == lon, 1.0, 0.0).astype(bf16)
        values = []
        for k in range(2, 5):
            for v in split(line(k)):
                values.append(cols * v)
        new = mm_nt(rows, jnp.concatenate(values, axis=0))
        part = new if part is None else part + new

    @pl.when(i == 0)
    def _():
        acc_ref[...] = part

    @pl.when(i > 0)
    def _():
        acc_ref[...] += part

    @pl.when(i == WAVES - 1)
    def _():
        for k in range(3):
            first = acc_ref[:, 256 * k : 256 * k + 128]
            out_ref[k] = first + acc_ref[:, 256 * k + 128 : 256 * k + 256]


def flow_kernel(courant_ref, out_ref):
    for h in range(12):
        rows = [courant_ref[min(t, 6), 8 * h : 8 * h + 8] for t in range(8)]
        for j, z in enumerate(turn(rows, 0, 1)):
            out_ref[8 * h + j] = z


def grid_kernel(
    grid_ref,
    flow_ref,
    sums_hbm,
    lidar_ref,
    aod_ref,
    state_hbm,
    adjoint_ref,
    hold_ref,
    state_ref,
    sums_ref,
    sem,
):
    fetch = pltpu.make_async_copy(sums_hbm, sums_ref, sem.at[4])
    fetch.start()

    def tile_rows(l, b2, hc, c):
        return pl.ds(TILE * (BANDS * hc + 2 * l + b2) + 7 * c, 7)

    def store(q):
        target = state_hbm.at[pl.ds(7 * q, 7)]
        return pltpu.make_async_copy(state_ref.at[q], target, sem.at[q])

    blank = jnp.zeros((1, 128), f32)
    chains = [(b2, hc, c) for b2 in range(2) for hc in range(2) for c in range(3)]

    @pl.loop(0, 4)
    def _(q):
        lidar_sum = [None] * LEV
        aod_sum = None
        for b2, hc, c in chains:
            bin_at = b2 * 6 + hc * 3 + c
            x = [
                jnp.concatenate([grid_ref[q, tile_rows(l, b2, hc, c)], blank], axis=0)
                for l in range(LEV)
            ]
            flow = [flow_ref[q, BINS * l + bin_at] for l in range(LEV)]
            for step in range(STEPS):
                out = [flow[l] * x[l] for l in range(LEV)]
                x = [x[l] - out[l] if l == 0 else x[l] - out[l] + out[l - 1] for l in range(LEV)]
            coef = lidar_ref[bin_at]
            for l in range(LEV):
                hold_ref[BINS * l + bin_at] = x[l]
                term = x[l] * coef
                lidar_sum[l] = term if lidar_sum[l] is None else lidar_sum[l] + term
                term = x[l] * aod_ref[BINS * l + bin_at]
                aod_sum = term if aod_sum is None else aod_sum + term

        for h in range(12):
            rows = turn([hold_ref[8 * h + j] for j in range(8)], 0, 1)
            for t in range(7):
                state_ref[q, t, 8 * h : 8 * h + 8] = rows[t]
        store(q).start()

        @pl.when(q == 0)
        def _():
            fetch.wait()

        def sums(k, l):
            return sums_ref[k, pl.ds(pl.multiple_of(64 * q + 8 * l, 8), 8), :]

        weight = [sums(0, l) for l in range(LEV)]
        lidar = [weight[l] * lidar_sum[l] - sums(1, l) for l in range(LEV)]
        aod = sum(weight[1:], weight[0]) * aod_sum
        for l in range(LEV):
            aod = aod - sums(2, l)
        for b2, hc, c in chains:
            bin_at = b2 * 6 + hc * 3 + c
            coef = lidar_ref[bin_at]
            flow = [flow_ref[q, BINS * l + bin_at] for l in range(LEV)]
            a = [lidar[l] * coef + aod * aod_ref[BINS * l + bin_at] for l in range(LEV)]
            for step in range(STEPS):
                a = [
                    a[l] + flow[l] * ((a[l + 1] - a[l]) if l + 1 < LEV else -a[l])
                    for l in range(LEV)
                ]
            for l in range(LEV):
                adjoint_ref[q, tile_rows(l, b2, hc, c)] = a[l][:7]

    for q in range(4):
        store(q).wait()


def shape(*lengths, kind=f32):
    return jax.ShapeDtypeStruct(lengths, kind)


def whole(*lengths):
    return pl.BlockSpec(lengths, lambda *_: (0,) * len(lengths))


def in_hbm(x):
    return pltpu.with_memory_space_constraint(x, pltpu.HBM)


def cost(flops, size):
    return pl.CostEstimate(flops=flops, bytes_accessed=size, transcendentals=0)


def exchange(tiles, axis):
    return lax.all_to_all(tiles, axis, split_axis=0, concat_axis=0, tiled=True)


def exchange_tiles(tiles):
    rows = tiles.reshape(DEVICES, 1, TILE * 128)
    return exchange(rows, ("wave", "band")).reshape(DEVICES * TILE, 128)


def body(
    control,
    spectral_scale,
    vertical_root,
    legendre,
    zonal_number,
    courant,
    lidar_coef,
    aod_coef,
    obs_count,
    obs_column,
    obs_level,
    lidar_obs,
    aod_obs,
    obs_weight,
):
    control = jnp.swapaxes(control, 0, 1)
    scale = jnp.swapaxes(spectral_scale, 0, 1)
    hbm = pl.BlockSpec(memory_space=pltpu.HBM)
    modes = pl.pallas_call(
        mix_kernel,
        in_specs=[hbm] * 9,
        out_specs=pl.BlockSpec(memory_space=pl.ANY),
        out_shape=shape(BANDS, 88, 128),
        scratch_shapes=[
            pltpu.VMEM((BANDS, 88, 128), f32),
            pltpu.VMEM((28, 16, 192), f32),
            pltpu.VMEM((28, 16, 192), f32),
            pltpu.VMEM((CH, CH), f32),
            pltpu.VMEM((2, DEVICES, SLOT), jnp.int32),
            pltpu.VMEM((3, DEVICES, SLOT), f32),
            pltpu.VMEM((1, DEVICES), jnp.int32),
            pltpu.VMEM((5, DEVICES, SLOT), f32),
            pltpu.SemaphoreType.DMA((12,)),
        ],
        compiler_params=params(),
        cost_estimate=cost(6 * 448 * 192 * 192, 1 << 20),
        name="mix",
    )(
        *(
            in_hbm(x)
            for x in (
                control,
                scale,
                vertical_root,
                obs_column,
                obs_level,
                lidar_obs,
                aod_obs,
                obs_weight,
                obs_count,
            )
        )
    )
    waves = pl.pallas_call(
        wave_table_kernel,
        out_shape=(shape(2 * MW, NLON, kind=bf16), shape(2 * MW, NLON, kind=bf16)),
        compiler_params=params(),
        cost_estimate=cost(20 * 448 * 1024, 2 << 20),
        name="wave_table",
    )(zonal_number.reshape(1, MW))
    modes, (high, low) = lax.optimization_barrier((exchange(modes, "band"), waves))

    legendre_cost = cost(6 * 28 * 448 * 256 * 48, 14 << 20)
    in_order = params(dimension_semantics=("arbitrary",))
    table_scratch = [pltpu.VMEM((28, NLAT, NT), f32), pltpu.SemaphoreType.DMA((GROUPS,))]
    spec = pl.pallas_call(
        legendre_kernel,
        in_specs=[whole(BANDS, 88, 128), hbm],
        out_specs=whole(WAVES, 248, 128),
        out_shape=shape(WAVES, 248, 128),
        scratch_shapes=[
            pltpu.VMEM((GROUPS, 48, NT), f32),
            pltpu.VMEM((GROUPS, 48, NLAT), f32),
            *table_scratch,
        ],
        compiler_params=params(),
        cost_estimate=legendre_cost,
        name="legendre",
    )(modes, in_hbm(legendre))
    spec = exchange(spec, "wave")
    sums = pl.pallas_call(
        sums_kernel,
        grid=(WAVES,),
        in_specs=[pl.BlockSpec((1, 248, 128), lambda i: (i, 0, 0))],
        out_specs=whole(3, 256, 128),
        out_shape=shape(3, 256, 128),
        scratch_shapes=[pltpu.VMEM((256, 768), f32)],
        compiler_params=in_order,
        cost_estimate=cost(2 * 16384 * 256 * 768, 1 << 20),
        name="sums",
    )(spec)

    tiles = shape(DEVICES * TILE, 128)
    wave_cost = cost(6 * 384 * 448 * 1024, 4 << 20)
    grid = pl.pallas_call(
        synthesis_kernel,
        out_specs=pl.BlockSpec(memory_space=pl.ANY),
        out_shape=tiles,
        scratch_shapes=[
            pltpu.VMEM((DEVICES * TILE, 128), f32),
            pltpu.VMEM((768, 2 * MW), bf16),
            pltpu.SemaphoreType.DMA((4,)),
        ],
        compiler_params=params(),
        cost_estimate=wave_cost,
        name="synthesis",
    )(spec, high, low)
    grid = exchange_tiles(grid)

    field = pl.BlockSpec((7, CH, 128), lambda q: (q, 0, 0))
    scalars = pl.BlockSpec(memory_space=pltpu.SMEM)
    turned = pl.BlockSpec((CH, 8, 128), lambda q: (q, 0, 0))
    flow = pl.pallas_call(
        flow_kernel,
        grid=(4,),
        in_specs=[field],
        out_specs=turned,
        out_shape=shape(4 * CH, 8, 128),
        compiler_params=in_order,
        cost_estimate=cost(6 * 28 * 96 * 128, 3 << 20),
        name="flow",
    )(in_hbm(courant))
    quarters = (4, 2 * BANDS * TILE, 128)
    state, adjoint = pl.pallas_call(
        grid_kernel,
        in_specs=[whole(*quarters), whole(4, CH, 8, 128), hbm, scalars, scalars],
        out_specs=(pl.BlockSpec(memory_space=pl.ANY), whole(*quarters)),
        out_shape=(shape(28, CH, 128), shape(*quarters)),
        scratch_shapes=[
            pltpu.VMEM((CH, 8, 128), f32),
            pltpu.VMEM((4, 7, CH, 128), f32),
            pltpu.VMEM((3, 256, 128), f32),
            pltpu.SemaphoreType.DMA((5,)),
        ],
        compiler_params=params(),
        cost_estimate=cost(40 * 28 * 96 * 128, 6 << 20),
        name="grid_steps",
    )(
        grid.reshape(quarters),
        flow.reshape(4, CH, 8, 128),
        in_hbm(sums),
        lidar_coef,
        aod_coef,
    )
    adjoint = adjoint.reshape(DEVICES * TILE, 128)
    adjoint = exchange_tiles(adjoint)

    spec = pl.pallas_call(
        analysis_kernel,
        out_shape=shape(WAVES, GROUPS, 3, 8, 128),
        compiler_params=params(),
        cost_estimate=wave_cost,
        name="analysis",
    )(adjoint, high, low)
    spec = exchange(spec.reshape(WAVES, 24 * GROUPS, 128), "wave")

    modes = pl.pallas_call(
        legendre_adjoint_kernel,
        in_specs=[whole(WAVES, 168, 128), hbm],
        out_specs=whole(BANDS, 48, 128),
        out_shape=shape(BANDS, 48, 128),
        scratch_shapes=[pltpu.VMEM((336, NLAT), f32), *table_scratch],
        compiler_params=params(),
        cost_estimate=legendre_cost,
        name="legendre_adjoint",
    )(spec, in_hbm(legendre))
    modes = exchange(modes, "band").reshape(24, 4, 8, 128)

    gradient = pl.pallas_call(
        unmix_kernel,
        out_shape=shape(28, 16, 192),
        compiler_params=params(),
        cost_estimate=cost(6 * 448 * 192 * 192, 1 << 20),
        name="unmix",
    )(modes, control, scale, vertical_root)
    return jnp.swapaxes(gradient, 0, 1), state


def solution(mesh):
    both = ("wave", "band")
    placed = (
        P("band", "wave", None),
        P("band", "wave", None),
        P(),
        P("wave", None, None),
        P(),
        P("band", None, "wave"),
        P(),
        P(),
        P(both, None),
        P(both, None),
        P(both, None),
        P(both, None),
        P(both, None),
        P(both, None),
    )
    return jax.shard_map(
        body,
        mesh=mesh,
        in_specs=placed,
        out_specs=(P("band", "wave", None), P("band", None, "wave")),
        check_vma=False,
    )
```
